32 devices in a mesh: dp: 4 (over z), row: 2 (over x), col: 4 (over y, core).
Axes of the slice: x: 2, y: 2, z: 4, core: 2. Of those that a mesh axis runs over, the one named last changes fastest.
Arguments:
- block_input: bfloat16 [4096, 768], P(('dp', 'col'), 'row'), may hold values from -6 to 6
- span_end: int32 [4096], P('dp'), may hold values from 0 to 1023, as said below
- encoder_attention_gain: float32 [768], P('row'), may hold values from 0.25 to 1.75
- encoder_attention_bias: float32 [768], P('row'), may hold values from -1.75 to 1.75
- encoder_query_key_value: bfloat16 [768, 3, 768], P('row', None, 'col'), may hold values from -0.21875 to 0.21875
- encoder_output_weight: bfloat16 [768, 768], P('col', 'row'), may hold values from -3.5 to 3.5
- encoder_feedforward_gain: float32 [768], P('row'), may hold values from 0.25 to 1.75
- encoder_feedforward_bias: float32 [768], P('row'), may hold values from -1.75 to 1.75
- encoder_up_weight: bfloat16 [768, 3072], P('row', 'col'), may hold values from -0.21875 to 0.21875
- encoder_down_weight: bfloat16 [3072, 768], P('col', 'row'), may hold values from -0.109375 to 0.109375
- projection: bfloat16 [768, 512], P('row', 'col'), may hold values from -0.21875 to 0.21875
- decoder_attention_gain: float32 [512], P('col'), may hold values from 0.25 to 1.75
- decoder_attention_bias: float32 [512], P('col'), may hold values from -1.75 to 1.75
- decoder_query_key_value: bfloat16 [512, 3, 512], P('col', None, 'row'), may hold values from -0.25 to 0.25
- decoder_output_weight: bfloat16 [512, 512], P('row', 'col'), may hold values from -4 to 4
- decoder_feedforward_gain: float32 [512], P('col'), may hold values from 0.25 to 1.75
- decoder_feedforward_bias: float32 [512], P('col'), may hold values from -1.75 to 1.75
- decoder_up_weight: bfloat16 [512, 2048], P('col', 'row'), may hold values from -0.25 to 0.25
- decoder_down_weight: bfloat16 [2048, 512], P('row', 'col'), may hold values from -0.125 to 0.125
- output_cotangent: bfloat16 [4096, 512], P(('dp', 'row'), 'col'), may hold values from -6 to 6
Outputs:
- encoder_output: float32 [4096, 768], P(('dp', 'col'), 'row')
- decoder_output: float32 [4096, 512], P(('dp', 'row'), 'col')
- input_gradient: float32 [4096, 768], P(('dp', 'col'), 'row')
- grad_encoder_attention_gain: float32 [768], P('row')
- grad_encoder_attention_bias: float32 [768], P('row')
- grad_encoder_query_key_value: float32 [768, 3, 768], P('row', None, 'col')
- grad_encoder_output_weight: float32 [768, 768], P('col', 'row')
- grad_encoder_feedforward_gain: float32 [768], P('row')
- grad_encoder_feedforward_bias: float32 [768], P('row')
- grad_encoder_up_weight: float32 [768, 3072], P('row', 'col')
- grad_encoder_down_weight: float32 [3072, 768], P('col', 'row')
- grad_projection: float32 [768, 512], P('row', 'col')
- grad_decoder_attention_gain: float32 [512], P('col')
- grad_decoder_attention_bias: float32 [512], P('col')
- grad_decoder_query_key_value: float32 [512, 3, 512], P('col', None, 'row')
- grad_decoder_output_weight: float32 [512, 512], P('row', 'col')
- grad_decoder_feedforward_gain: float32 [512], P('col')
- grad_decoder_feedforward_bias: float32 [512], P('col')
- grad_decoder_up_weight: float32 [512, 2048], P('col', 'row')
- grad_decoder_down_weight: float32 [2048, 512], P('row', 'col')
The draws below stay inside these ranges and needn't reach their ends.
Inputs may be any that keep to these rules, and one draw needn't show every extreme that they name: `span_end`: each aligned block of 512 positions of a sequence holds one image piece of 256 consecutive patches that starts at a place between 0 and 256 of the block; a patch's value is its piece's last position, every other token's value is its own position in its sequence.
All inputs are finite; a program needn't handle non-finite values.
Results may differ from the reference program's by a relative error of at most 0.039.
Values may be sent and summed in bfloat16 or wider, within the bound.
No kernel may reach another device: no remote copies, remote signals or barrier semaphores. Data moves between devices by JAX's collectives and lax.ppermute only.
A program may use at most 128 MiB of HBM per device.

```python
import jax
import jax.numpy as jnp
from jax import lax

D1 = 768
H1 = 12
F1 = 3072
D2 = 512
H2 = 16
F2 = 2048
SEQ = 1024
IMG = 256
TOKENS = 4096


def draw_span_end(key, part):
    blocks = TOKENS // (2 * IMG)
    offsets = jax.random.randint(key, (blocks, 1), 0, IMG + 1, dtype=jnp.int32)
    places = lax.broadcasted_iota(jnp.int32, (blocks, 2 * IMG), 1)
    block_start = lax.broadcasted_iota(jnp.int32, (blocks, 2 * IMG), 0) * (2 * IMG) % SEQ
    inside = (places >= offsets) & (places < offsets + IMG)
    ending = jnp.where(inside, block_start + offsets + IMG - 1, block_start + places)
    return ending.reshape(TOKENS).astype(jnp.int32)


def block_levels(rng, dims, shards, smallest, high):
    level, own = 1.0, jax.random.fold_in(rng, 6)
    for dim, parts in shards:
        steps = jnp.exp(jax.random.uniform(jax.random.fold_in(own, dim), (parts,), jnp.float32, smallest / len(shards), high / len(shards)))
        level = level * jnp.repeat(steps, dims[dim] // parts).reshape([-1 if axis == dim else 1 for axis in range(len(dims))])
    return level


def centred(rng, extent, deviation, reach, split=(), kind=jnp.bfloat16):
    level = block_levels(rng, extent, split, -0.22, 0.18) if split else 1.0
    result = jax.random.normal(rng, extent, jnp.float32) * deviation * level
    return jnp.minimum(jnp.maximum(result, -reach), reach).astype(kind)


def setup_inputs(seed: int = 0) -> dict:
    keys = jax.random.split(jax.random.key(seed), 21)
    block_input = centred(keys[0], (TOKENS, D1), 1.0, 6.0, ((0, 16), (1, 2)))
    span_end = draw_span_end(jax.random.fold_in(keys[20], 71), 0)
    encoder_attention_gain = jnp.clip(1.0 + 0.15 * jax.random.normal(keys[2], (D1,), jnp.float32), 0.25, 1.75)
    encoder_attention_bias = centred(keys[3], (D1,), 0.3, 1.75, ((0, 2),), jnp.float32)
    encoder_query_key_value = centred(keys[4], (D1, 3, D1), D1 ** -0.5, 0.21875, ((0, 2), (2, 4)))
    encoder_output_weight = centred(keys[5], (D1, D1), (max(4 * D1 // SEQ, 1)) ** -0.5, 3.5, ((0, 4), (1, 2)))
    encoder_feedforward_gain = jnp.clip(1.0 + 0.15 * jax.random.normal(keys[6], (D1,), jnp.float32), 0.25, 1.75)
    encoder_feedforward_bias = centred(keys[7], (D1,), 0.3, 1.75, ((0, 2),), jnp.float32)
    encoder_up_weight = centred(keys[8], (D1, F1), D1 ** -0.5, 0.21875, ((0, 2), (1, 4)))
    encoder_down_weight = centred(keys[9], (F1, D1), F1 ** -0.5, 0.109375, ((0, 4), (1, 2)))
    projection = centred(keys[10], (D1, D2), D1 ** -0.5, 0.21875, ((0, 2), (1, 4)))
    decoder_attention_gain = jnp.clip(1.0 + 0.15 * jax.random.normal(keys[11], (D2,), jnp.float32), 0.25, 1.75)
    decoder_attention_bias = centred(keys[12], (D2,), 0.3, 1.75, ((0, 4),), jnp.float32)
    decoder_query_key_value = centred(keys[13], (D2, 3, D2), D2 ** -0.5, 0.25, ((0, 4), (2, 2)))
    decoder_output_weight = centred(keys[14], (D2, D2), (max(4 * D2 // SEQ, 1)) ** -0.5, 4.0, ((0, 2), (1, 4)))
    decoder_feedforward_gain = jnp.clip(1.0 + 0.15 * jax.random.normal(keys[15], (D2,), jnp.float32), 0.25, 1.75)
    decoder_feedforward_bias = centred(keys[16], (D2,), 0.3, 1.75, ((0, 4),), jnp.float32)
    decoder_up_weight = centred(keys[17], (D2, F2), D2 ** -0.5, 0.25, ((0, 4), (1, 2)))
    decoder_down_weight = centred(keys[18], (F2, D2), F2 ** -0.5, 0.125, ((0, 2), (1, 4)))
    output_cotangent = centred(keys[19], (TOKENS, D2), 1.0, 6.0, ((0, 8), (1, 4)))
    return {"block_input": block_input, "span_end": span_end, "encoder_attention_gain": encoder_attention_gain, "encoder_attention_bias": encoder_attention_bias, "encoder_query_key_value": encoder_query_key_value, "encoder_output_weight": encoder_output_weight, "encoder_feedforward_gain": encoder_feedforward_gain, "encoder_feedforward_bias": encoder_feedforward_bias, "encoder_up_weight": encoder_up_weight, "encoder_down_weight": encoder_down_weight, "projection": projection, "decoder_attention_gain": decoder_attention_gain, "decoder_attention_bias": decoder_attention_bias, "decoder_query_key_value": decoder_query_key_value, "decoder_output_weight": decoder_output_weight, "decoder_feedforward_gain": decoder_feedforward_gain, "decoder_feedforward_bias": decoder_feedforward_bias, "decoder_up_weight": decoder_up_weight, "decoder_down_weight": decoder_down_weight, "output_cotangent": output_cotangent}


HIGHEST = lax.Precision.HIGHEST
EPSILON = 1e-06

@jax.custom_vjp
def low(v):
    return lax.optimization_barrier(v.astype(jnp.bfloat16)).astype(jnp.float32)

@jax.custom_vjp
def low_back(v):
    return v

def low_keep(v):
    return (low(v), None)

def low_pass(kept, grad):
    return (grad,)

def back_keep(v):
    return (v, None)

def back_low(kept, grad):
    return (low(grad),)
low.defvjp(low_keep, low_pass)
low_back.defvjp(back_keep, back_low)

def matmul(left, right):
    return jnp.dot(left, right, precision=HIGHEST, preferred_element_type=jnp.float32)

def layer_norm(values, gain, bias):
    average = lax.optimization_barrier(jnp.mean(values, axis=1, keepdims=True))
    variance = lax.optimization_barrier(jnp.mean(values * values, axis=1, keepdims=True)) - average * average
    return (values - average) * lax.rsqrt(variance + EPSILON) * gain + bias

def attention(mixed_rows, span_ends, head_count):
    columns = mixed_rows.shape[1] // 3
    head_size = columns // head_count
    scaling = head_size ** (-0.5)
    block_rows = min(512, SEQ)
    places = jnp.arange(SEQ, dtype=jnp.int32)

    def one_block(query_rows, limits, key_rows, value_rows):
        scores = low_back(jnp.einsum('qhd,khd->hqk', query_rows, key_rows, precision=HIGHEST) * scaling)
        visible = places[None, None, :] <= limits[None, :, None]
        weights = jnp.where(visible, jnp.exp(scores), 0.0)
        denominator = lax.optimization_barrier(jnp.sum(weights, axis=2))
        numerator = low_back(jnp.einsum('hqk,khd->qhd', low(weights), value_rows, precision=HIGHEST))
        return low(numerator / jnp.transpose(denominator)[:, :, None])
    checked = jax.checkpoint(one_block)

    def one_sequence(sequence_pair):
        sequence, limits = sequence_pair
        queries = sequence[:, 0].reshape(SEQ // block_rows, block_rows, head_count, head_size)
        blocked_limits = limits.reshape(SEQ // block_rows, block_rows)

        def run_block(block_pair):
            return checked(block_pair[0], block_pair[1], sequence[:, 1], sequence[:, 2])
        return lax.map(run_block, (queries, blocked_limits)).reshape(SEQ, columns)
    pieces = mixed_rows.reshape(TOKENS // SEQ, SEQ, 3, head_count, head_size)
    limits_all = span_ends.reshape(TOKENS // SEQ, SEQ)
    return lax.map(one_sequence, (pieces, limits_all)).reshape(TOKENS, columns)

def residual_block(stream, params, head_count, span_ends):
    first_gain, first_bias, mixing, output, second_gain, second_bias, upward, downward = params
    normed = low(layer_norm(stream, first_gain, first_bias))
    mixed_rows = low(low_back(matmul(normed, mixing.reshape(mixing.shape[0], -1))))
    attended = attention(mixed_rows, span_ends, head_count)
    middle = stream + low_back(matmul(attended, output))
    normed_second = low(layer_norm(middle, second_gain, second_bias))
    hidden = low_back(matmul(normed_second, upward))
    active = low(jax.nn.gelu(hidden, approximate=False))
    return middle + low_back(matmul(active, downward))

def reference(block_input, span_end, encoder_attention_gain, encoder_attention_bias, encoder_query_key_value, encoder_output_weight, encoder_feedforward_gain, encoder_feedforward_bias, encoder_up_weight, encoder_down_weight, projection, decoder_attention_gain, decoder_attention_bias, decoder_query_key_value, decoder_output_weight, decoder_feedforward_gain, decoder_feedforward_bias, decoder_up_weight, decoder_down_weight, output_cotangent):
    given_params = (encoder_attention_gain, encoder_attention_bias, encoder_query_key_value, encoder_output_weight, encoder_feedforward_gain, encoder_feedforward_bias, encoder_up_weight, encoder_down_weight, projection, decoder_attention_gain, decoder_attention_bias, decoder_query_key_value, decoder_output_weight, decoder_feedforward_gain, decoder_feedforward_bias, decoder_up_weight, decoder_down_weight)
    weights = tuple((element.astype(jnp.float32) for element in given_params))

    def forward(stream, params):
        encoded = residual_block(stream, params[0:8], H1, span_end)
        decoder_in = low_back(matmul(low(encoded), params[8]))
        decoded = residual_block(decoder_in, params[9:17], H2, span_end)
        return (encoded, decoded)
    outputs, backward = jax.vjp(forward, block_input.astype(jnp.float32), weights)
    grad_input, gradients = backward((jnp.zeros_like(outputs[0]), output_cotangent.astype(jnp.float32)))
    return (outputs[0], outputs[1], grad_input, gradients[0], gradients[1], gradients[2], gradients[3], gradients[4], gradients[5], gradients[6], gradients[7], gradients[8], gradients[9], gradients[10], gradients[11], gradients[12], gradients[13], gradients[14], gradients[15], gradients[16])
```

```python
import functools

import jax
import jax.numpy as jnp
from jax import lax
from jax.experimental import pallas as pl
from jax.experimental.pallas import tpu as pltpu
from jax.sharding import Mesh, PartitionSpec as P

D1 = 768
D2 = 512
HD1 = 64
HD2 = 32
EPSILON = 1e-06
BLOCK = 512
LANES = 128
LOG2E = 1.4426950408889634
SWAP = [(0, 1), (1, 0)]
BF16 = jnp.bfloat16
F32 = jnp.float32


def mm(left, right):
    return jnp.dot(left, right, preferred_element_type=F32)


def mm_nt(left, right):
    return lax.dot_general(left, right, (((1,), (1,)), ((), ())), preferred_element_type=F32)


def mm_tn(left, right):
    return lax.dot_general(left, right, (((0,), (0,)), ((), ())), preferred_element_type=F32)


def swap(value, axis):
    return lax.ppermute(value, axis, SWAP)


def gather_four(block):
    half = block.shape[0] // 2
    by_x = swap(block, "row")
    by_y = swap(block, "y")
    first = swap(by_x[:half], "y")
    second = swap(by_y[half:], "row")
    return (block, by_x, by_y, jnp.concatenate([first, second], 0))


def head_lanes(head, head_size, rows):
    lane = lax.broadcasted_iota(jnp.int32, (rows, LANES), 1)
    return (lane >= head * head_size) & (lane < (head + 1) * head_size)


def attention_forward_kernel(head_size, q_ref, k_ref, v_ref, limit_ref, out_ref, inv_ref, aug_ref):
    tile = pl.program_id(1)
    rows = q_ref.shape[0]
    heads = LANES // head_size
    per_block = BLOCK // rows
    scale = head_size ** (-0.5) * LOG2E

    @pl.when(tile == 0)
    def _():
        aug_ref[:, :LANES] = v_ref[...]
        aug_ref[:, LANES:] = jnp.ones_like(v_ref)

    def run(block):
        queries = q_ref[...]
        limits = limit_ref[...]
        places = block * BLOCK + lax.broadcasted_iota(jnp.int32, (rows, BLOCK), 1)
        visible = places <= limits
        result = jnp.zeros((rows, LANES), F32)
        inverses = jnp.zeros((rows, LANES), F32)
        for head in range(heads):
            own = head_lanes(head, head_size, rows)
            masked = jnp.where(own, queries, jnp.zeros_like(queries))
            total = jnp.zeros((rows, 2 * LANES), F32)
            for part in range(block + 1):
                span = slice(part * BLOCK, (part + 1) * BLOCK)
                weights = jnp.exp2(mm_nt(masked, k_ref[span, :]) * scale)
                if part == block:
                    weights = jnp.where(visible, weights, 0.0)
                total = total + mm(weights.astype(BF16), aug_ref[span, :])
            inverse = 1.0 / total[:, LANES:]
            result = jnp.where(own, total[:, :LANES] * inverse, result)
            inverses = jnp.where(own, inverse, inverses)
        out_ref[...] = result.astype(BF16)
        inv_ref[...] = inverses

    for block in range(k_ref.shape[0] // BLOCK):
        pl.when(tile // per_block == block)(functools.partial(run, block))


def attention_forward(mixed, limits, head_size):
    length, width = mixed.shape[0], mixed.shape[1] // 3
    groups = width // LANES
    rows = 256
    return pl.pallas_call(
        functools.partial(attention_forward_kernel, head_size),
        out_shape=(
            jax.ShapeDtypeStruct((length, width), BF16),
            jax.ShapeDtypeStruct((length, width), F32),
        ),
        grid=(groups, length // rows),
        in_specs=[
            pl.BlockSpec((rows, LANES), lambda g, t: (t, g)),
            pl.BlockSpec((length, LANES), lambda g, t: (0, groups + g)),
            pl.BlockSpec((length, LANES), lambda g, t: (0, 2 * groups + g)),
            pl.BlockSpec((rows, 1), lambda g, t: (t, 0)),
        ],
        out_specs=[
            pl.BlockSpec((rows, LANES), lambda g, t: (t, g)),
            pl.BlockSpec((rows, LANES), lambda g, t: (t, g)),
        ],
        scratch_shapes=[pltpu.VMEM((length, 2 * LANES), BF16)],
        compiler_params=pltpu.CompilerParams(vmem_limit_bytes=40 << 20),
        name="attention_forward",
    )(mixed, mixed, mixed, limits)


def attention_backward_kernel(
    head_size,
    pairs,
    q_ref,
    k_ref,
    v_ref,
    att_ref,
    inv_ref,
    grad_ref,
    limit_ref,
    dq_ref,
    dk_ref,
    dv_ref,
    vaug_ref,
    naug_ref,
    dq_acc,
    dk_acc,
    dv_acc,
):
    step = pl.program_id(1)
    length = q_ref.shape[0]
    heads = LANES // head_size
    scaling = head_size ** (-0.5)

    @pl.when(step == 0)
    def _():
        lane = lax.broadcasted_iota(jnp.int32, (length, LANES), 1)
        vaug_ref[:, :LANES] = v_ref[...]
        vaug_ref[:, LANES:] = jnp.where(lane < 2, 1.0, 0.0).astype(BF16)
        scaled = grad_ref[...] * inv_ref[...]
        terms = scaled * att_ref[...].astype(F32)
        low = scaled.astype(BF16)
        for head in range(heads):
            own = head_lanes(head, head_size, length)
            total = -jnp.sum(jnp.where(own, terms, 0.0), 1, keepdims=True)
            high = total.astype(BF16).astype(F32)
            rest = total - high
            naug_ref[head, :, :LANES] = jnp.where(own, low, jnp.zeros_like(low))
            naug_ref[head, :, LANES:] = jnp.where(
                lane == 0, high, jnp.where(lane == 1, rest, 0.0)
            ).astype(BF16)
        dq_acc[...] = jnp.zeros_like(dq_acc)
        dk_acc[...] = jnp.zeros_like(dk_acc)
        dv_acc[...] = jnp.zeros_like(dv_acc)

    def run(key_block, query_block):
        keys = slice(key_block * BLOCK, (key_block + 1) * BLOCK)
        queries = slice(query_block * BLOCK, (query_block + 1) * BLOCK)
        key_rows = k_ref[keys, :]
        query_rows = q_ref[queries, :]
        key_flipped = key_rows.astype(F32).T.astype(BF16)
        if key_block == query_block:
            places = key_block * BLOCK + lax.broadcasted_iota(jnp.int32, (BLOCK, BLOCK), 0)
            visible = places <= limit_ref[:, queries]
        dq = jnp.zeros((LANES, BLOCK), F32)
        dk = jnp.zeros((BLOCK, LANES), F32)
        dv = jnp.zeros((BLOCK, LANES), F32)
        for head in range(heads):
            own = head_lanes(head, head_size, BLOCK)
            masked = jnp.where(own, query_rows, jnp.zeros_like(query_rows))
            weights = jnp.exp2(mm_nt(key_rows, masked) * (scaling * LOG2E))
            if key_block == query_block:
                weights = jnp.where(visible, weights, 0.0)
            naug = naug_ref[head, queries, :]
            slopes = mm_nt(vaug_ref[keys, :], naug)
            scores = (weights * slopes).astype(BF16)
            dv += mm(weights.astype(BF16), naug[:, :LANES])
            dk += mm(scores, masked)
            row = lax.broadcasted_iota(jnp.int32, (LANES, BLOCK), 0)
            mine = (row >= head * head_size) & (row < (head + 1) * head_size)
            dq += mm(jnp.where(mine, key_flipped, jnp.zeros_like(key_flipped)), scores)
        dq_acc[:, queries] += dq
        dk_acc[keys, :] += dk
        dv_acc[keys, :] += dv

    for number, (key_block, query_block) in enumerate(pairs):
        pl.when(step == number)(functools.partial(run, key_block, query_block))

    @pl.when(step == len(pairs) - 1)
    def _():
        dq_ref[...] = (dq_acc[...].T * scaling).astype(BF16)
        dk_ref[...] = (dk_acc[...] * scaling).astype(BF16)
        dv_ref[...] = dv_acc[...].astype(BF16)


def attention_backward(mixed, attended, inverse, grad, limits_row, head_size):
    length, width = attended.shape
    groups = width // LANES
    blocks = length // BLOCK
    pairs = [(k, q) for q in range(blocks) for k in range(q + 1)]
    whole = lambda offset: pl.BlockSpec((length, LANES), lambda g, s: (0, offset + g))
    return pl.pallas_call(
        functools.partial(attention_backward_kernel, head_size, pairs),
        out_shape=(jax.ShapeDtypeStruct((length, width), BF16),) * 3,
        grid=(groups, len(pairs)),
        in_specs=[
            whole(0),
            whole(groups),
            whole(2 * groups),
            whole(0),
            whole(0),
            whole(0),
            pl.BlockSpec((1, length), lambda g, s: (0, 0)),
        ],
        out_specs=[whole(0), whole(0), whole(0)],
        scratch_shapes=[
            pltpu.VMEM((length, 2 * LANES), BF16),
            pltpu.VMEM((LANES // head_size, length, 2 * LANES), BF16),
            pltpu.VMEM((LANES, length), F32),
            pltpu.VMEM((length, LANES), F32),
            pltpu.VMEM((length, LANES), F32),
        ],
        compiler_params=pltpu.CompilerParams(vmem_limit_bytes=40 << 20),
        name="attention_backward",
    )(mixed, mixed, mixed, attended, inverse, grad, limits_row)


def norm_stats(values):
    width = values.shape[1]
    average = jnp.sum(values, 1, keepdims=True) / width
    variance = jnp.sum(values * values, 1, keepdims=True) / width - average * average
    inverse = lax.rsqrt(variance + EPSILON)
    return ((values - average) * inverse, inverse)


def norm_backward(incoming, centred, inverse, gain):
    width = incoming.shape[1]
    scaled = incoming * gain
    first = jnp.sum(scaled, 1, keepdims=True) / width
    second = jnp.sum(scaled * centred, 1, keepdims=True) / width
    return inverse * (scaled - first - centred * second)


def gelu_pair(values):
    area = 0.5 * (1.0 + lax.erf(values * (0.5**0.5)))
    slope = area + values * jnp.exp(-0.5 * values * values) * (0.5 / jnp.pi) ** 0.5
    return (values * area, slope)


def core_sum(partial):
    low = partial.astype(BF16)
    return low.astype(F32) + swap(low, "core").astype(F32)


def dp_sum(value, size):
    if size & (size - 1):
        return lax.psum(value, "dp")
    distance = 1
    while distance < size:
        pairs = [(i, i ^ distance) for i in range(size)]
        value = value + lax.ppermute(value, "dp", pairs)
        distance *= 2
    return value


def block_forward(stream, params, limits, head_size):
    first_gain, first_bias, mixing, output, second_gain, second_bias, upward = params
    centred_first, inverse_first = norm_stats(stream)
    normed_first = (centred_first * first_gain + first_bias).astype(BF16)
    mixed = mm(normed_first, mixing).astype(BF16)
    attended, inverse = attention_forward(mixed, limits, head_size)
    middle = stream + core_sum(mm(attended, output))
    centred_second, inverse_second = norm_stats(middle)
    normed_second = (centred_second * second_gain + second_bias).astype(BF16)
    hidden = mm(normed_second, upward)
    active, slope = gelu_pair(hidden)
    kept = (
        centred_first,
        inverse_first,
        normed_first,
        mixed,
        attended,
        inverse,
        centred_second,
        inverse_second,
        normed_second,
        slope.astype(BF16),
    )
    return (middle, active.astype(BF16), kept)


def block_backward(out_grad, params, downward, kept, limits_row, head_size):
    first_gain, first_bias, mixing, output, second_gain, second_bias, upward = params
    (
        centred_first,
        inverse_first,
        normed_first,
        mixed,
        attended,
        inverse,
        centred_second,
        inverse_second,
        normed_second,
        slope,
    ) = kept
    down_low = out_grad.astype(BF16)
    hidden_low = (mm_nt(down_low, downward) * slope.astype(F32)).astype(BF16)
    second_grad = core_sum(mm_nt(hidden_low, upward))
    middle_grad = out_grad + norm_backward(second_grad, centred_second, inverse_second, second_gain)
    middle_low = middle_grad.astype(BF16)
    attended_grad = mm_nt(middle_low, output)
    mixed_low = jnp.concatenate(
        attention_backward(mixed, attended, inverse, attended_grad, limits_row, head_size), 1
    )
    return (down_low, hidden_low, second_grad, middle_grad, middle_low, mixed_low)


def per_device(
    data_size,
    block_input,
    span_end,
    encoder_attention_gain,
    encoder_attention_bias,
    encoder_query_key_value,
    encoder_output_weight,
    encoder_feedforward_gain,
    encoder_feedforward_bias,
    encoder_up_weight,
    encoder_down_weight,
    projection,
    decoder_attention_gain,
    decoder_attention_bias,
    decoder_query_key_value,
    decoder_output_weight,
    decoder_feedforward_gain,
    decoder_feedforward_bias,
    decoder_up_weight,
    decoder_down_weight,
    output_cotangent,
):
    row = lax.axis_index("row")
    y = lax.axis_index("y")
    core = lax.axis_index("core")
    length = span_end.shape[0]
    own_rows = block_input.shape[0]
    limits = span_end.reshape(length, 1)
    limits_row = span_end.reshape(1, length)

    parts = gather_four(block_input)
    near = jnp.concatenate([parts[0], parts[1]], 1)
    far = jnp.concatenate([parts[2], parts[3]], 1)
    sides = lax.all_gather(
        jnp.stack([near, far]), "core", axis=1, tiled=False
    )
    ordered = jnp.where(y == 0, sides, sides[::-1])
    encoder_in = ordered.reshape(length, -1)

    vectors = jnp.stack(
        [
            encoder_attention_gain,
            encoder_attention_bias,
            encoder_feedforward_gain,
            encoder_feedforward_bias,
        ]
    )
    encoder_vectors = jnp.concatenate([vectors, swap(vectors, "row")], 1)
    vectors = jnp.stack(
        [
            decoder_attention_gain,
            decoder_attention_bias,
            decoder_feedforward_gain,
            decoder_feedforward_bias,
        ]
    )
    vectors = lax.all_gather(vectors, "core", axis=1, tiled=True)
    decoder_vectors = jnp.concatenate([vectors, swap(vectors, "y")], 1)

    def square(parts, row_dim):
        own, by_x, by_y, by_both = parts
        if row_dim == 0:
            return jnp.concatenate(
                [jnp.concatenate([own, by_y], 1), jnp.concatenate([by_x, by_both], 1)], 0
            )
        return jnp.concatenate(
            [jnp.concatenate([own, by_x], 1), jnp.concatenate([by_y, by_both], 1)], 0
        )

    def mixing_square(parts, row_dim):
        width = parts[0].shape[1] // 3
        return jnp.concatenate(
            [square([p[:, i * width : (i + 1) * width] for p in parts], row_dim) for i in range(3)],
            1,
        )

    mixing = encoder_query_key_value.reshape(encoder_query_key_value.shape[0], -1)
    encoder_mixing = mixing_square(gather_four(mixing), 0)
    encoder_output = square(gather_four(encoder_output_weight), 1)
    encoder_up = square(gather_four(encoder_up_weight), 0)
    encoder_down = square(gather_four(encoder_down_weight), 1)
    pieces = square(gather_four(projection), 0)
    both = lax.all_gather(pieces, "core", axis=0, tiled=False)
    width = projection.shape[1]
    projection_all = jnp.concatenate(
        [both[0, :, :width], both[1, :, :width], both[0, :, width:], both[1, :, width:]], 1
    )

    def core_rows(value):
        return lax.all_to_all(value, "core", value.ndim - 1, 0, tiled=True)

    def core_columns(value):
        return lax.all_to_all(value, "core", 0, value.ndim - 1, tiled=True)

    mixing = core_rows(decoder_query_key_value)
    mixing = mixing.reshape(mixing.shape[0], -1)
    decoder_mixing = mixing_square(gather_four(mixing), 1)
    decoder_output = square(gather_four(core_columns(decoder_output_weight)), 0)
    decoder_up = square(gather_four(core_rows(decoder_up_weight)), 1)
    decoder_down = square(gather_four(core_columns(decoder_down_weight)), 0)

    cotangent = lax.all_gather(output_cotangent, "core", axis=1, tiled=True)
    cotangent = jnp.concatenate([cotangent, swap(cotangent, "y")], 1)
    other = swap(cotangent, "row")
    cotangent = jnp.where(
        row == 0,
        jnp.concatenate([cotangent, other], 0),
        jnp.concatenate([other, cotangent], 0),
    )

    encoder_params = (
        encoder_vectors[0],
        encoder_vectors[1],
        encoder_mixing,
        encoder_output,
        encoder_vectors[2],
        encoder_vectors[3],
        encoder_up,
    )
    decoder_params = (
        decoder_vectors[0],
        decoder_vectors[1],
        decoder_mixing,
        decoder_output,
        decoder_vectors[2],
        decoder_vectors[3],
        decoder_up,
    )

    stream = encoder_in.astype(F32)
    middle, encoder_active, encoder_kept = block_forward(stream, encoder_params, limits, HD1)
    encoder_out = middle + core_sum(mm(encoder_active, encoder_down))
    encoder_low = encoder_out.astype(BF16)
    decoder_in = mm(encoder_low, projection_all)
    decoder_middle, decoder_active, decoder_kept = block_forward(
        decoder_in, decoder_params, limits, HD2
    )
    own_tokens = (2 * y + core) * own_rows
    own_encoder_out = lax.dynamic_slice(
        encoder_out, (own_tokens, 0), (own_rows, block_input.shape[1])
    )
    out_rows, out_columns = output_cotangent.shape
    active_rows = lax.dynamic_slice_in_dim(decoder_active, row * out_rows, out_rows, 0)
    last = mm(active_rows, decoder_down[:, : 2 * out_columns])
    mine = lax.dynamic_slice_in_dim(last, core * out_columns, out_columns, 1)
    others = lax.dynamic_slice_in_dim(last, (1 - core) * out_columns, out_columns, 1)
    own_decoder_out = (
        lax.dynamic_slice(
            decoder_middle, (row * out_rows, core * out_columns), (out_rows, out_columns)
        )
        + mine
        + swap(others.astype(BF16), "core").astype(F32)
    )

    down_low, hidden_low, second_grad, middle_grad, middle_low, mixed_low = block_backward(
        cotangent.astype(F32), decoder_params, decoder_down, decoder_kept, limits_row, HD2
    )
    first_grad = core_sum(mm_nt(mixed_low, decoder_mixing))
    decoder_grad = middle_grad + norm_backward(
        first_grad, decoder_kept[0], decoder_kept[1], decoder_vectors[0]
    )

    def own_sums(first_grad, second_grad, kept):
        def part(value):
            return lax.dynamic_slice_in_dim(value, own_tokens, own_rows, 0)

        first, second = part(first_grad), part(second_grad)
        return jnp.stack(
            [
                jnp.sum(first * part(kept[0]), 0),
                jnp.sum(first, 0),
                jnp.sum(second * part(kept[6]), 0),
                jnp.sum(second, 0),
            ]
        )

    decoder_sums = own_sums(first_grad, second_grad, decoder_kept)
    heads_own = decoder_query_key_value.shape[2] // 2
    features = 2 * decoder_output_weight.shape[1]
    columns = mixed_low.shape[1] // 3
    mixed_own = jnp.concatenate(
        [mixed_low[:, i * columns : i * columns + heads_own] for i in range(3)], 1
    )
    units = decoder_up_weight.shape[1] // 2
    decoder_weight_grads = [
        mm_tn(decoder_kept[2][:, :features], mixed_own).astype(BF16),
        mm_tn(decoder_kept[4][:, :heads_own], middle_low[:, :features]).astype(BF16),
        mm_tn(decoder_kept[8][:, :features], hidden_low[:, :units]).astype(BF16),
        mm_tn(decoder_active[:, :units], down_low[:, :features]).astype(BF16),
    ]

    projection_low = decoder_grad.astype(BF16)
    projection_own = lax.dynamic_slice_in_dim(
        projection_low, core * projection.shape[1], projection.shape[1], 1
    )
    projection_grad = mm_tn(encoder_low[:, : projection.shape[0]], projection_own).astype(BF16)
    encoder_grad = mm_nt(projection_low, projection_all)

    down_low, hidden_low, second_grad, middle_grad, middle_low, mixed_low = block_backward(
        encoder_grad, encoder_params, encoder_down, encoder_kept, limits_row, HD1
    )
    first_grad = core_sum(mm_nt(mixed_low, encoder_mixing))
    input_grad = middle_grad + norm_backward(
        first_grad, encoder_kept[0], encoder_kept[1], encoder_vectors[0]
    )
    own_input_grad = lax.dynamic_slice(
        input_grad, (own_tokens, 0), (own_rows, block_input.shape[1])
    )
    encoder_sums = own_sums(first_grad, second_grad, encoder_kept)
    features = encoder_up_weight.shape[0]
    heads_own = encoder_output_weight.shape[0]
    columns = mixed_low.shape[1] // 3
    mixed_own = jnp.concatenate(
        [mixed_low[:, i * columns : i * columns + heads_own] for i in range(3)], 1
    )
    units = encoder_up_weight.shape[1]
    encoder_weight_grads = [
        mm_tn(encoder_kept[2][:, :features], mixed_own).astype(BF16),
        mm_tn(encoder_kept[4][:, :heads_own], middle_low[:, :features]).astype(BF16),
        mm_tn(encoder_kept[8][:, :features], hidden_low[:, :units]).astype(BF16),
        mm_tn(encoder_active[:, :units], down_low[:, :features]).astype(BF16),
    ]

    decoder_weight_grads = [dp_sum(g, data_size).astype(F32) for g in decoder_weight_grads]
    projection_grad = dp_sum(projection_grad, data_size).astype(F32)
    encoder_weight_grads = [dp_sum(g, data_size).astype(F32) for g in encoder_weight_grads]
    encoder_sums = lax.psum(encoder_sums[:, :features], ("dp", "y", "core"))
    decoder_sums = jnp.where(
        y == 0,
        decoder_sums,
        jnp.concatenate(
            [decoder_sums[:, decoder_sums.shape[1] // 2 :], decoder_sums[:, : decoder_sums.shape[1] // 2]], 1
        ),
    )
    decoder_sums = lax.psum(decoder_sums, ("dp", "y", "core"))
    share = decoder_attention_gain.shape[0]
    decoder_sums = lax.dynamic_slice_in_dim(decoder_sums, (2 * y + core) * share, share, 1)

    decoder_weight_grads = [
        core_columns(
            decoder_weight_grads[0].reshape(decoder_weight_grads[0].shape[0], 3, -1)
        ),
        core_rows(decoder_weight_grads[1]),
        core_columns(decoder_weight_grads[2]),
        core_rows(decoder_weight_grads[3]),
    ]
    return (
        own_encoder_out,
        own_decoder_out,
        own_input_grad,
        encoder_sums[0],
        encoder_sums[1],
        encoder_weight_grads[0].reshape(encoder_query_key_value.shape),
        encoder_weight_grads[1],
        encoder_sums[2],
        encoder_sums[3],
        encoder_weight_grads[2],
        encoder_weight_grads[3],
        projection_grad,
        decoder_sums[0],
        decoder_sums[1],
        decoder_weight_grads[0],
        decoder_weight_grads[1],
        decoder_sums[2],
        decoder_sums[3],
        decoder_weight_grads[2],
        decoder_weight_grads[3],
    )


def solution(mesh):
    data, row, col = (mesh.shape[name] for name in ("dp", "row", "col"))
    split = Mesh(mesh.devices.reshape(data, row, col // 2, 2), ("dp", "row", "y", "core"))
    c = ("y", "core")
    in_specs = (
        P(("dp", *c), "row"),
        P("dp"),
        P("row"),
        P("row"),
        P("row", None, c),
        P(c, "row"),
        P("row"),
        P("row"),
        P("row", c),
        P(c, "row"),
        P("row", c),
        P(c),
        P(c),
        P(c, None, "row"),
        P("row", c),
        P(c),
        P(c),
        P(c, "row"),
        P("row", c),
        P(("dp", "row"), c),
    )
    out_specs = (
        P(("dp", *c), "row"),
        P(("dp", "row"), c),
        P(("dp", *c), "row"),
        P("row"),
        P("row"),
        P("row", None, c),
        P(c, "row"),
        P("row"),
        P("row"),
        P("row", c),
        P(c, "row"),
        P("row", c),
        P(c),
        P(c),
        P(c, None, "row"),
        P("row", c),
        P(c),
        P(c),
        P(c, "row"),
        P("row", c),
    )
    return jax.shard_map(
        functools.partial(per_device, data),
        mesh=split,
        in_specs=in_specs,
        out_specs=out_specs,
        check_vma=False,
    )
```

```python
import functools
import math

import jax
import jax.numpy as jnp
from jax import lax
from jax.experimental import pallas as pl
from jax.experimental.pallas import tpu as pltpu
from jax.sharding import Mesh, PartitionSpec as P

D1 = 768
D2 = 512
HD1 = 64
HD2 = 32
EPSILON = 1e-06
BLOCK = 512
LANES = 128
LOG2E = 1.4426950408889634
SWAP = [(0, 1), (1, 0)]
BF16 = jnp.bfloat16
F32 = jnp.float32


def mm(left, right):
    return jnp.dot(left, right, preferred_element_type=F32)


def mm_nt(left, right):
    return lax.dot_general(left, right, (((1,), (1,)), ((), ())), preferred_element_type=F32)


def mm_tn(left, right):
    return lax.dot_general(left, right, (((0,), (0,)), ((), ())), preferred_element_type=F32)


def head_lanes(head, head_size, rows):
    lane = lax.broadcasted_iota(jnp.int32, (rows, LANES), 1)
    return (lane >= head * head_size) & (lane < (head + 1) * head_size)


def attention_forward_kernel(head_size, q_ref, k_ref, v_ref, limit_ref, out_ref, inv_ref, aug_ref):
    tile = pl.program_id(1)
    rows = q_ref.shape[0]
    heads = LANES // head_size
    per_block = BLOCK // rows
    scale = head_size ** (-0.5) * LOG2E

    @pl.when(tile == 0)
    def _():
        aug_ref[:, :LANES] = v_ref[...]
        aug_ref[:, LANES:] = jnp.ones_like(v_ref)

    def run(block):
        queries = q_ref[...]
        limits = limit_ref[...]
        places = block * BLOCK + lax.broadcasted_iota(jnp.int32, (rows, BLOCK), 1)
        visible = places <= limits
        result = jnp.zeros((rows, LANES), F32)
        inverses = jnp.zeros((rows, LANES), F32)
        for head in range(heads):
            own = head_lanes(head, head_size, rows)
            masked = jnp.where(own, queries, jnp.zeros_like(queries))
            total = jnp.zeros((rows, 2 * LANES), F32)
            for part in range(block + 1):
                span = slice(part * BLOCK, (part + 1) * BLOCK)
                weights = jnp.exp2(mm_nt(masked, k_ref[span, :]) * scale)
                if part == block:
                    weights = jnp.where(visible, weights, 0.0)
                total = total + mm(weights.astype(BF16), aug_ref[span, :])
            inverse = 1.0 / total[:, LANES:]
            result = jnp.where(own, total[:, :LANES] * inverse, result)
            inverses = jnp.where(own, inverse, inverses)
        out_ref[...] = result.astype(BF16)
        inv_ref[...] = inverses

    for block in range(k_ref.shape[0] // BLOCK):
        pl.when(tile // per_block == block)(functools.partial(run, block))


def attention_forward(mixed, limits, head_size):
    length, width = mixed.shape[0], mixed.shape[1] // 3
    groups = width // LANES
    rows = 256
    return pl.pallas_call(
        functools.partial(attention_forward_kernel, head_size),
        out_shape=(
            jax.ShapeDtypeStruct((length, width), BF16),
            jax.ShapeDtypeStruct((length, width), F32),
        ),
        grid=(groups, length // rows),
        in_specs=[
            pl.BlockSpec((rows, LANES), lambda g, t: (t, g)),
            pl.BlockSpec((length, LANES), lambda g, t: (0, groups + g)),
            pl.BlockSpec((length, LANES), lambda g, t: (0, 2 * groups + g)),
            pl.BlockSpec((rows, 1), lambda g, t: (t, 0)),
        ],
        out_specs=[
            pl.BlockSpec((rows, LANES), lambda g, t: (t, g)),
            pl.BlockSpec((rows, LANES), lambda g, t: (t, g)),
        ],
        scratch_shapes=[pltpu.VMEM((length, 2 * LANES), BF16)],
        compiler_params=pltpu.CompilerParams(vmem_limit_bytes=24 << 20),
        cost_estimate=pl.CostEstimate(flops=int(10.5 * COST), bytes_accessed=1, transcendentals=0),
        name="attention_forward",
    )(mixed, mixed, mixed, limits)


def attention_backward_kernel(
    head_size,
    pairs,
    q_ref,
    k_ref,
    v_ref,
    att_ref,
    inv_ref,
    grad_ref,
    limit_ref,
    dq_ref,
    dk_ref,
    dv_ref,
    vaug_ref,
    naug_ref,
    dq_acc,
    dk_acc,
    dv_acc,
):
    step = pl.program_id(1)
    length = q_ref.shape[0]
    heads = LANES // head_size
    scaling = head_size ** (-0.5)

    @pl.when(step == 0)
    def _():
        lane = lax.broadcasted_iota(jnp.int32, (length, LANES), 1)
        vaug_ref[:, :LANES] = v_ref[...]
        vaug_ref[:, LANES:] = jnp.where(lane < 2, 1.0, 0.0).astype(BF16)
        scaled = grad_ref[...] * inv_ref[...]
        terms = scaled * att_ref[...].astype(F32)
        low = scaled.astype(BF16)
        for head in range(heads):
            own = head_lanes(head, head_size, length)
            total = -jnp.sum(jnp.where(own, terms, 0.0), 1, keepdims=True)
            high = total.astype(BF16).astype(F32)
            rest = total - high
            naug_ref[head, :, :LANES] = jnp.where(own, low, jnp.zeros_like(low))
            naug_ref[head, :, LANES:] = jnp.where(
                lane == 0, high, jnp.where(lane == 1, rest, 0.0)
            ).astype(BF16)
        dq_acc[...] = jnp.zeros_like(dq_acc)
        dk_acc[...] = jnp.zeros_like(dk_acc)
        dv_acc[...] = jnp.zeros_like(dv_acc)

    def run(key_block, query_block):
        keys = slice(key_block * BLOCK, (key_block + 1) * BLOCK)
        queries = slice(query_block * BLOCK, (query_block + 1) * BLOCK)
        key_rows = k_ref[keys, :]
        query_rows = q_ref[queries, :]
        key_flipped = key_rows.astype(F32).T.astype(BF16)
        if key_block == query_block:
            places = key_block * BLOCK + lax.broadcasted_iota(jnp.int32, (BLOCK, BLOCK), 0)
            visible = places <= limit_ref[:, queries]
        dq = jnp.zeros((LANES, BLOCK), F32)
        dk = jnp.zeros((BLOCK, LANES), F32)
        dv = jnp.zeros((BLOCK, LANES), F32)
        for head in range(heads):
            own = head_lanes(head, head_size, BLOCK)
            masked = jnp.where(own, query_rows, jnp.zeros_like(query_rows))
            weights = jnp.exp2(mm_nt(key_rows, masked) * (scaling * LOG2E))
            if key_block == query_block:
                weights = jnp.where(visible, weights, 0.0)
            naug = naug_ref[head, queries, :]
            slopes = mm_nt(vaug_ref[keys, :], naug)
            scores = (weights * slopes).astype(BF16)
            dv += mm(weights.astype(BF16), naug[:, :LANES])
            dk += mm(scores, masked)
            row = lax.broadcasted_iota(jnp.int32, (LANES, BLOCK), 0)
            mine = (row >= head * head_size) & (row < (head + 1) * head_size)
            dq += mm(jnp.where(mine, key_flipped, jnp.zeros_like(key_flipped)), scores)
        dq_acc[:, queries] += dq
        dk_acc[keys, :] += dk
        dv_acc[keys, :] += dv

    for number, (key_block, query_block) in enumerate(pairs):
        pl.when(step == number)(functools.partial(run, key_block, query_block))

    @pl.when(step == len(pairs) - 1)
    def _():
        dq_ref[...] = (dq_acc[...].T * scaling).astype(BF16)
        dk_ref[...] = (dk_acc[...] * scaling).astype(BF16)
        dv_ref[...] = dv_acc[...].astype(BF16)


def attention_backward(
    mixed, attended, inverse, grad, limits_row, head_size, start=0, count=None
):
    length, width = attended.shape
    groups = width // LANES
    count = groups if count is None else count
    blocks = length // BLOCK
    pairs = [(k, q) for q in range(blocks) for k in range(q + 1)]
    whole = lambda offset: pl.BlockSpec((length, LANES), lambda g, s: (0, offset + g))
    results = pl.pallas_call(
        functools.partial(attention_backward_kernel, head_size, pairs),
        out_shape=(jax.ShapeDtypeStruct((length, count * LANES), BF16),) * 3,
        grid=(count, len(pairs)),
        in_specs=[
            whole(start),
            whole(groups + start),
            whole(2 * groups + start),
            whole(start),
            whole(start),
            whole(start),
            pl.BlockSpec((1, length), lambda g, s: (0, 0)),
        ],
        out_specs=[whole(0), whole(0), whole(0)],
        scratch_shapes=[
            pltpu.VMEM((length, 2 * LANES), BF16),
            pltpu.VMEM((LANES // head_size, length, 2 * LANES), BF16),
            pltpu.VMEM((LANES, length), F32),
            pltpu.VMEM((length, LANES), F32),
            pltpu.VMEM((length, LANES), F32),
        ],
        compiler_params=pltpu.CompilerParams(vmem_limit_bytes=32 << 20),
        cost_estimate=pl.CostEstimate(
            flops=int(count * (5.2 if head_size == HD1 else 9.6) * COST), bytes_accessed=1, transcendentals=0
        ),
        name="attention_backward",
    )(mixed, mixed, mixed, attended, inverse, grad, limits_row)
    if count == 1:
        return tuple(results)
    return tuple(r[:, g * LANES : (g + 1) * LANES] for g in range(count) for r in results)


def swap(value, axis):
    return lax.ppermute(value, axis, SWAP)


def after(value, *others):
    return lax.optimization_barrier((value, *others))[0]


def cross_once(pack):
    return (swap(pack, "row"), swap(pack, "y"))


def cross_twice(near, *others):
    by_row, by_y = near
    half = by_row.shape[0] // 2
    first, second = after((by_row[:half], by_y[half:]), *others)
    return (swap(first, "y"), swap(second, "row"))


class Parts:
    def __init__(self, refs):
        own, by_row, by_y, first, second, both = refs
        half = first.shape[0]
        both[:half, :] = first[...]
        both[half:, :] = second[...]
        self.refs = ((own, by_y), (by_row, both))

    def rows(self, by_row, by_y, base, count, offset=0):
        return self.refs[by_row][by_y][pl.ds(base + offset, count), :]


def both_scratch(parts):
    return pltpu.VMEM(parts[0].shape, parts[0].dtype)


COST = 1e7
VMEM = pl.BlockSpec(memory_space=pltpu.VMEM)
SMEM = pl.BlockSpec(memory_space=pltpu.SMEM)


def call(kernel, name, outs, args, scratch=(), scalars=0, limit=48, cost=1):
    return pl.pallas_call(
        kernel,
        out_shape=outs,
        in_specs=[SMEM] * scalars + [VMEM] * (len(args) - scalars),
        out_specs=jax.tree.map(lambda _: VMEM, outs),
        scratch_shapes=scratch,
        compiler_params=pltpu.CompilerParams(vmem_limit_bytes=limit << 20),
        cost_estimate=pl.CostEstimate(
            flops=int(cost * COST), bytes_accessed=1, transcendentals=0
        ),
        name=name,
    )(*args)


def shaped(rows, columns, kind):
    return jax.ShapeDtypeStruct((rows, columns), kind)


def split_three(values):
    high = values.astype(BF16)
    rest = values - high.astype(F32)
    middle = rest.astype(BF16)
    low = (rest - middle.astype(F32)).astype(BF16)
    return jnp.concatenate([high, middle, low, jnp.zeros_like(high)], 0)


def join_three(rows):
    wide = rows.astype(F32)
    return wide[0:4] + wide[4:8] + wide[8:12]


TILE = 256


def lane_roll(values):
    return pltpu.roll(values.astype(F32), LANES // 2, 1)


HALF = LANES // 2
E_ROWS = 3 * LANES
M_V = 2 * E_ROWS
M_LAST = M_V + E_ROWS
M_REST = M_LAST + E_ROWS
M_OUT = M_REST + E_ROWS // 2
M_END = M_OUT + 3 * (E_ROWS // 2)
U_PROJ = 6 * E_ROWS
U_END = U_PROJ + E_ROWS
DM_OUT = 6 * LANES
DM_VEC = 8 * LANES
DM_END = DM_VEC + 32
DF_DOWN = 8 * LANES
DF_COT = 16 * LANES
DF_END = 20 * LANES


def pack_mixing_kernel(w_ref, out_ref, pack_ref):
    rows = w_ref.shape[1]
    for kind in range(3):
        pack_ref[kind * rows : (kind + 1) * rows, :] = w_ref[kind, :, :LANES]
    pack_ref[M_LAST:M_REST, :HALF] = w_ref[0, :, LANES:]
    pack_ref[M_LAST:M_REST, HALF:] = w_ref[1, :, LANES:]
    pack_ref[M_REST:M_OUT, :HALF] = w_ref[2, : rows // 2, LANES:]
    pack_ref[M_REST:M_OUT, HALF:] = w_ref[2, rows // 2 :, LANES:]
    heads = out_ref.shape[0]
    for tile in range(3):
        pack_ref[M_OUT + tile * heads : M_OUT + (tile + 1) * heads, :] = out_ref[
            :, tile * LANES : (tile + 1) * LANES
        ]


def pack_up_kernel(up_ref, proj_ref, pack_ref):
    for tile in range(6):
        pack_ref[tile * E_ROWS : (tile + 1) * E_ROWS, :] = up_ref[
            :, tile * LANES : (tile + 1) * LANES
        ]
    pack_ref[U_PROJ:U_END, :] = proj_ref[...]


def pack_down_kernel(down_ref, pack_ref):
    rows = down_ref.shape[0]
    for tile in range(3):
        pack_ref[tile * rows : (tile + 1) * rows, :] = down_ref[
            :, tile * LANES : (tile + 1) * LANES
        ]


def pack_decoder_kernel(core_ref, mix_ref, out_ref, up_ref, down_ref, vec_ref, keep_ref, send_ref):
    core = core_ref[0]
    rows = mix_ref.shape[1]
    units = up_ref.shape[1] // 2
    for target, half in ((keep_ref, core), (send_ref, 1 - core)):
        base = 0
        for i in range(3):
            target[base : base + rows, :] = mix_ref[i, :, pl.ds(half * LANES, LANES)]
            base += rows
        target[base : base + LANES, :] = out_ref[pl.ds(half * LANES, LANES), :]
        base += LANES
        target[base : base + 16, :] = vec_ref[...]
        base += 16
        for i in range(units // LANES):
            target[base : base + rows, :] = up_ref[:, pl.ds(half * units + i * LANES, LANES)]
            base += rows
        target[base : base + units, :] = down_ref[pl.ds(half * units, units), :]


def join_decoder_kernel(core_ref, keep_ref, got_ref, cot_ref, mix_ref, feed_ref):
    core = core_ref[0]
    rows = LANES
    for source, place in ((keep_ref, core), (got_ref, 1 - core)):
        base = 0
        for i in range(4):
            mix_ref[pl.ds(2 * i * rows + place * rows, rows), :] = source[base : base + rows, :]
            base += rows
        mix_ref[pl.ds(DM_VEC + place * 16, 16), :] = source[base : base + 16, :]
        base += 16
        for i in range(4):
            feed_ref[pl.ds(2 * i * rows + place * rows, rows), :] = source[base : base + rows, :]
            base += rows
        feed_ref[pl.ds(DF_DOWN + place * 4 * rows, 4 * rows), :] = source[base : base + 4 * rows, :]
    feed_ref[DF_COT:DF_END, :] = cot_ref[...]


def join_input_kernel(y_ref, own, near_x, near_y, first, second, out_ref):
    y = y_ref[0]
    rows = out_ref.shape[0] // 2
    width = own.shape[1]
    half = first.shape[0]
    out_ref[pl.ds(y * rows, rows), :width] = own[:rows, :]
    out_ref[pl.ds(y * rows, rows), width:] = near_x[:rows, :]
    other = (1 - y) * rows
    out_ref[pl.ds(other, rows), :width] = near_y[:rows, :]
    out_ref[pl.ds(other, half), width:] = first[...]
    out_ref[pl.ds(other + half, rows - half), width:] = second[: rows - half, :]


def norm_rows(values):
    width = values.shape[1]
    average = jnp.sum(values, 1, keepdims=True) / width
    variance = jnp.sum(values * values, 1, keepdims=True) / width - average * average
    inverse = lax.rsqrt(variance + EPSILON)
    return ((values - average) * inverse, inverse)


def first_norm_kernel(core_ref, own, other, vec_own, vec_other, x_ref, normed_ref, vec_ref):
    core = core_ref[0]
    width = vec_own.shape[1]
    vec_ref[:, :width] = join_three(vec_own[...])
    vec_ref[:, width:] = join_three(vec_other[...])
    rows = own.shape[0] // 2
    gain, bias = vec_ref[0:1, :], vec_ref[1:2, :]
    for source, place in ((own, core), (other, 1 - core)):
        for y in range(2):
            values = source[y * rows : (y + 1) * rows, :]
            target = pl.ds((2 * y + place) * rows, rows)
            x_ref[target, :] = values
            centred, _ = norm_rows(values.astype(F32))
            normed_ref[target, :] = (centred * gain + bias).astype(BF16)


def encoder_mixing_kernel(normed_ref, *refs):
    parts = Parts((*refs[:5], refs[7]))
    mixed_ref, weight_ref = refs[5:7]
    rows = E_ROWS
    low = lax.broadcasted_iota(jnp.int32, (rows, LANES), 1) < HALF
    for half in range(2):
        at = slice(half * rows, (half + 1) * rows)
        for kind in range(3):
            for group, side in ((0, 0), (2, 1)):
                tile = (3 * kind + group) * LANES
                weight_ref[at, tile : tile + LANES] = parts.rows(half, side, kind * rows, rows)
        mine = parts.rows(half, 0, M_LAST, rows).astype(F32)
        theirs = parts.rows(half, 1, M_LAST, rows).astype(F32)
        weight_ref[at, LANES : 2 * LANES] = jnp.where(low, mine, lane_roll(theirs)).astype(BF16)
        weight_ref[at, 4 * LANES : 5 * LANES] = jnp.where(low, lane_roll(mine), theirs).astype(BF16)
        mine = parts.rows(half, 0, M_REST, rows // 2).astype(F32)
        theirs = parts.rows(half, 1, M_REST, rows // 2).astype(F32)
        mine = jnp.concatenate([mine, lane_roll(mine)], 0)
        theirs = jnp.concatenate([lane_roll(theirs), theirs], 0)
        weight_ref[at, 7 * LANES : 8 * LANES] = jnp.where(low, mine, theirs).astype(BF16)

    @pl.loop(0, normed_ref.shape[0] // TILE)
    def _(tile):
        at = pl.ds(tile * TILE, TILE)
        mixed_ref[at, :] = mm(normed_ref[at, :], weight_ref[...]).astype(BF16)


def encoder_out_rows(parts):
    heads = 3 * LANES // 2
    sides = [
        jnp.concatenate(
            [parts.rows(i, j, M_OUT + t * heads, heads) for i in range(2) for t in range(3)], 1
        )
        for j in range(2)
    ]
    return jnp.concatenate([sides[0], sides[1][LANES:], sides[1][:LANES]], 0)


def decoder_out_rows(parts):
    return jnp.concatenate(
        [
            jnp.concatenate(
                [parts.rows(i, j, DM_OUT + t * LANES, LANES) for j in range(2) for t in range(2)], 1
            )
            for i in range(2)
        ],
        0,
    )


def out_product_kernel(chooser, attended_ref, *refs):
    partial_ref, weight_ref = refs[5], refs[6]
    weight_ref[...] = chooser(Parts((*refs[:5], refs[7])))

    @pl.loop(0, attended_ref.shape[0] // TILE)
    def _(tile):
        at = pl.ds(tile * TILE, TILE)
        partial_ref[at, :] = mm(attended_ref[at, :], weight_ref[...]).astype(BF16)


def gelu_pair(values):
    area = 0.5 * (1.0 + lax.erf(values * (0.5**0.5)))
    slope = area + values * jnp.exp2(values * values * (-0.5 * LOG2E)) * (0.5 / math.pi) ** 0.5
    return (values * area, slope)


class Feed:
    def __init__(self, up_parts, down_parts, decoder):
        self.up_parts = up_parts
        self.down_parts = down_parts
        self.decoder = decoder
        self.features = 2 * LANES if decoder else 3 * LANES
        self.units = 4 * LANES if decoder else 6 * LANES
        self.down = DF_DOWN if decoder else 0
        self.chunks = self.units // (2 * LANES)

    def rows(self, parts, feature, unit, base, count, offset):
        if self.decoder:
            return parts.rows(unit, feature, base, count, offset)
        return parts.rows(feature, unit, base, count, offset)

    def up_chunk(self, unit, chunk):
        f = self.features
        return jnp.concatenate(
            [
                jnp.concatenate(
                    [
                        self.rows(
                            self.up_parts, i, unit, 0, f, pl.multiple_of((2 * chunk + t) * f, f)
                        )
                        for t in range(2)
                    ],
                    1,
                )
                for i in range(2)
            ],
            0,
        )

    def down_chunk(self, unit, chunk):
        return jnp.concatenate(
            [
                self.rows(
                    self.down_parts,
                    i,
                    unit,
                    self.down + t * self.units,
                    2 * LANES,
                    pl.multiple_of(chunk * 2 * LANES, 2 * LANES),
                )
                for i in range(2)
                for t in range(self.features // LANES)
            ],
            1,
        )


def feed_forward_kernel(stream_ref, mine_ref, got_ref, vec_ref, *refs):
    middle_ref, normed_ref, active_ref, slope_ref, partial_ref, total_ref = refs[10:16]
    feed = Feed(Parts((*refs[:5], refs[16])), Parts((*refs[5:10], refs[17])), False)
    gain, bias = vec_ref[2:3, :], vec_ref[3:4, :]

    @pl.loop(0, stream_ref.shape[0] // TILE)
    def _(tile):
        at = pl.ds(tile * TILE, TILE)
        middle = stream_ref[at, :].astype(F32) + (
            mine_ref[at, :].astype(F32) + got_ref[at, :].astype(F32)
        )
        middle_ref[at, :] = middle
        centred, _ = norm_rows(middle)
        normed_ref[at, :] = (centred * gain + bias).astype(BF16)
        total_ref[...] = jnp.zeros_like(total_ref)

        @pl.loop(0, feed.chunks)
        def _(chunk):
            for unit in range(2):
                hidden = mm(normed_ref[at, :], feed.up_chunk(unit, chunk))
                active, slope = gelu_pair(hidden)
                lanes = pl.ds(unit * feed.units + chunk * 2 * LANES, 2 * LANES)
                low = active.astype(BF16)
                active_ref[at, lanes] = low
                slope_ref[at, lanes] = slope.astype(BF16)
                total_ref[...] += mm(low, feed.down_chunk(unit, chunk))

        partial_ref[at, :] = total_ref[...].astype(BF16)


def decoder_feed_kernel(
    stream_ref, mine_ref, got_ref, vec_ref, cot_ref, own, near_x, near_y, first, second,
    middle_ref, normed_ref, active_ref, hidden_ref, partial_ref, total_ref, both_ref,
):
    parts = Parts((own, near_x, near_y, first, second, both_ref))
    feed = Feed(parts, parts, True)
    gain, bias = vec_ref[2:3, :], vec_ref[3:4, :]

    @pl.loop(0, stream_ref.shape[0] // TILE)
    def _(tile):
        at = pl.ds(tile * TILE, TILE)
        middle = stream_ref[at, :] + (mine_ref[at, :].astype(F32) + got_ref[at, :].astype(F32))
        middle_ref[at, :] = middle
        centred, _ = norm_rows(middle)
        normed_ref[at, :] = (centred * gain + bias).astype(BF16)
        total_ref[...] = jnp.zeros_like(total_ref)

        @pl.loop(0, feed.chunks)
        def _(chunk):
            for unit in range(2):
                upward = feed.up_chunk(unit, chunk)
                hidden = mm(normed_ref[at, :], upward)
                active, slope = gelu_pair(hidden)
                lanes = pl.ds(unit * feed.units + chunk * 2 * LANES, 2 * LANES)
                active_ref[at, lanes] = active.astype(BF16)
                grad = mm_nt(cot_ref[at, :], feed.down_chunk(unit, chunk))
                low = (grad * slope).astype(BF16)
                hidden_ref[at, lanes] = low
                total_ref[...] += mm_nt(low, upward)

        partial_ref[at, :] = total_ref[...].astype(BF16)


def bridge_kernel(
    place_ref, middle_ref, mine_ref, got_ref, proj_ref, other_ref, own, near_x, near_y, first, second,
    out_ref, low_ref, stream_ref, normed_ref, mixed_ref, weight_ref, vec_ref, mixing_ref, both_ref,
):
    core, block = place_ref[0], place_ref[1]
    parts = Parts((own, near_x, near_y, first, second, both_ref))
    rows = E_ROWS
    for i in range(2):
        for j in range(2):
            at = slice((2 * i + j) * rows, (2 * i + j + 1) * rows)
            for source, side in ((proj_ref, core), (other_ref, 1 - core)):
                weight_ref[i * rows : (i + 1) * rows, pl.ds((2 * j + side) * LANES, LANES)] = source[
                    at, :
                ]
    for j in range(2):
        for c in range(2):
            tile = (2 * j + c) * LANES
            vec_ref[:, tile : tile + LANES] = join_three(parts.rows(0, j, DM_VEC + 16 * c, 16))
    for kind in range(3):
        for i in range(2):
            tile = (2 * kind + i) * LANES
            for j in range(2):
                mixing_ref[2 * j * LANES : 2 * (j + 1) * LANES, tile : tile + LANES] = parts.rows(
                    i, j, 2 * kind * LANES, 2 * LANES
                )
    gain, bias = vec_ref[0:1, :], vec_ref[1:2, :]
    width = low_ref.shape[1]

    @pl.loop(0, middle_ref.shape[0] // TILE)
    def _(tile):
        at = pl.ds(tile * TILE, TILE)
        total = middle_ref[at, :] + (mine_ref[at, :].astype(F32) + got_ref[at, :].astype(F32))
        low = total.astype(BF16)

        @pl.when(tile == block)
        def _():
            out_ref[...] = total[:, :width]

        low_ref[at, :] = low[:, :width]
        stream = mm(low, weight_ref[...])
        stream_ref[at, :] = stream
        centred, _ = norm_rows(stream)
        normed = (centred * gain + bias).astype(BF16)
        normed_ref[at, :] = normed
        mixed_ref[at, :] = mm(normed, mixing_ref[...]).astype(BF16)


def cotangent_kernel(place_ref, mine_ref, got_ref, cot_ref):
    core, row = place_ref[0], place_ref[2]
    rows = 4 * LANES
    for i in range(2):
        at = pl.ds((row if i == 0 else 1 - row) * rows, rows)
        for j in range(2):
            part = slice((2 * i + j) * rows, (2 * i + j + 1) * rows)
            for source, side in ((mine_ref, core), (got_ref, 1 - core)):
                cot_ref[at, pl.ds((2 * j + side) * LANES, LANES)] = source[part, :]


def norm_back(incoming, centred, inverse, gain):
    width = incoming.shape[1]
    scaled = incoming * gain
    first = jnp.sum(scaled, 1, keepdims=True) / width
    second = jnp.sum(scaled * centred, 1, keepdims=True) / width
    return inverse * (scaled - first - centred * second)


def store_sums(sums_ref, incoming, centred):
    sums_ref[0:1, :] = jnp.sum(incoming * centred, 0, keepdims=True)
    sums_ref[1:2, :] = jnp.sum(incoming, 0, keepdims=True)


def own_sums(place_ref, tile, sums_ref, incoming, centred):
    half = TILE // 2

    @pl.when((tile == place_ref[1]) & (place_ref[2] == 0))
    def _():
        store_sums(sums_ref, incoming[:half], centred[:half])

    @pl.when((tile == place_ref[1]) & (place_ref[2] == 1))
    def _():
        store_sums(sums_ref, incoming[half:], centred[half:])


def middle_back_kernel(
    chooser, place_ref, mine_ref, got_ref, middle_ref, grad_ref, vec_ref,
    own, near_x, near_y, first, second,
    total_ref, low_ref, attended_ref, sums_ref, weight_ref, both_ref,
):
    weight_ref[...] = chooser(Parts((own, near_x, near_y, first, second, both_ref)))
    gain = vec_ref[2:3, :]
    width = low_ref.shape[1]

    @pl.loop(0, middle_ref.shape[0] // TILE)
    def _(tile):
        at = pl.ds(tile * TILE, TILE)
        incoming = mine_ref[at, :].astype(F32) + got_ref[at, :].astype(F32)
        centred, inverse = norm_rows(middle_ref[at, :])
        total = grad_ref[at, :].astype(F32) + norm_back(incoming, centred, inverse, gain)
        total_ref[at, :] = total
        low = total.astype(BF16)
        low_ref[at, :] = low[:, :width]
        attended_ref[at, :] = mm_nt(low, weight_ref[...])
        own_sums(place_ref, tile, sums_ref, incoming, centred)


def mixed_low(refs, at):
    kinds = len(refs) // 3
    return jnp.concatenate([refs[3 * g + i][at, :] for i in range(3) for g in range(kinds)], 1)


def mixed_back_kernel(*refs):
    lows, weight_ref, partial_ref = refs[:-2], refs[-2], refs[-1]

    @pl.loop(0, partial_ref.shape[0] // TILE)
    def _(tile):
        at = pl.ds(tile * TILE, TILE)
        partial_ref[at, :] = mm_nt(mixed_low(lows, at), weight_ref[...]).astype(BF16)


def mixed_last_kernel(place_ref, *refs):
    core, y = place_ref[0], place_ref[3]
    lows, weight_ref, keep_ref, send_ref = refs[:-3], refs[-3], refs[-2], refs[-1]
    for target, side in ((keep_ref, core), (send_ref, 1 - core)):
        at = pl.ds((2 * y + side) * TILE, TILE)
        target[...] = mm_nt(mixed_low(lows, at), weight_ref[...]).astype(BF16)


def bridge_back_kernel(
    place_ref, mine_ref, got_ref, stream_ref, grad_ref, vec_ref, proj_ref,
    low_ref, encoder_ref, down_ref, sums_ref,
):
    gain = vec_ref[0:1, :]

    @pl.loop(0, stream_ref.shape[0] // TILE)
    def _(tile):
        at = pl.ds(tile * TILE, TILE)
        incoming = mine_ref[at, :].astype(F32) + got_ref[at, :].astype(F32)
        centred, inverse = norm_rows(stream_ref[at, :])
        grad = grad_ref[at, :] + norm_back(incoming, centred, inverse, gain)
        own_sums(place_ref, tile, sums_ref, incoming, centred)
        low = grad.astype(BF16)
        low_ref[at, :] = low
        encoder = mm_nt(low, proj_ref[...])
        encoder_ref[at, :] = encoder
        down_ref[at, :] = encoder.astype(BF16)


def feed_back_kernel(down_ref, slope_ref, *refs):
    hidden_ref, partial_ref, total_ref = refs[10:13]
    feed = Feed(Parts((*refs[:5], refs[13])), Parts((*refs[5:10], refs[14])), False)

    @pl.loop(0, down_ref.shape[0] // TILE)
    def _(tile):
        at = pl.ds(tile * TILE, TILE)
        total_ref[...] = jnp.zeros_like(total_ref)

        @pl.loop(0, feed.chunks)
        def _(chunk):
            for unit in range(2):
                lanes = pl.ds(unit * feed.units + chunk * 2 * LANES, 2 * LANES)
                back = mm_nt(down_ref[at, :], feed.down_chunk(unit, chunk))
                hidden = (back * slope_ref[at, lanes].astype(F32)).astype(BF16)
                hidden_ref[at, lanes] = hidden
                total_ref[...] += mm_nt(hidden, feed.up_chunk(unit, chunk))

        partial_ref[at, :] = total_ref[...].astype(BF16)


def input_back_kernel(place_ref, mine_ref, got_ref, x_ref, grad_ref, vec_ref, out_ref, sums_ref):
    at = pl.ds(place_ref[1] * TILE, TILE)
    incoming = mine_ref[...].astype(F32) + got_ref[...].astype(F32)
    centred, inverse = norm_rows(x_ref[at, :].astype(F32))
    total = grad_ref[at, :] + norm_back(incoming, centred, inverse, vec_ref[0:1, :])
    out_ref[...] = total[:, : out_ref.shape[1]]
    own_sums(place_ref, place_ref[1], sums_ref, incoming, centred)


def store_tiles(ref, base, value):
    rows = value.shape[0]
    for tile in range(value.shape[1] // LANES):
        ref[base + tile * rows : base + (tile + 1) * rows, :] = value[
            :, tile * LANES : (tile + 1) * LANES
        ].astype(BF16)


GA_UP = 8 * LANES
GA_END = 16 * LANES
GB_OUT = 6 * LANES
GB_PROJ = 8 * LANES
GB_END = 11 * LANES


def feed_grads_kernel(active_ref, cot_ref, normed_ref, hidden_ref, pack_ref):
    units, features = 4 * LANES, 2 * LANES
    store_tiles(pack_ref, 0, mm_tn(active_ref[:, :units], cot_ref[:, :features]))
    store_tiles(pack_ref, GA_UP, mm_tn(normed_ref[:, :features], hidden_ref[:, :units]))


def mixing_grads_kernel(
    place_ref, normed_ref, q_ref, k_ref, v_ref, attended_ref, middle_ref, encoder_ref, proj_ref, pack_ref
):
    lows = jnp.concatenate([q_ref[:, :LANES], k_ref[:, :LANES], v_ref[:, :LANES]], 1)
    store_tiles(pack_ref, 0, mm_tn(normed_ref[:, : 2 * LANES], lows))
    store_tiles(pack_ref, GB_OUT, mm_tn(attended_ref[:, :LANES], middle_ref[...]))
    own = proj_ref[:, pl.ds(place_ref[0] * LANES, LANES)]
    store_tiles(pack_ref, GB_PROJ, mm_tn(encoder_ref[...], own))


def product_kernel(left_ref, right_ref, out_ref):
    rows, columns = out_ref.shape
    out_ref[...] = mm_tn(left_ref[:, :rows], right_ref[:, :columns]).astype(BF16)


def encoder_grads_kernel(
    normed_ref, q_ref, k_ref, v_ref, q2_ref, k2_ref, v2_ref, attended_ref, middle_ref, pack_ref
):
    low = lax.broadcasted_iota(jnp.int32, q2_ref.shape, 1) < HALF
    last = jnp.where(low, q2_ref[...].astype(F32), lane_roll(k2_ref[...])).astype(BF16)
    lows = jnp.concatenate([q_ref[...], k_ref[...], v_ref[...], last, v2_ref[...]], 1)
    grads = mm_tn(normed_ref[:, :E_ROWS], lows)
    store_tiles(pack_ref, 0, grads[:, : 4 * LANES])
    rest = grads[:, 4 * LANES :]
    half = E_ROWS // 2
    low = lax.broadcasted_iota(jnp.int32, (half, LANES), 1) < HALF
    pack_ref[M_REST:M_OUT, :] = jnp.where(low, rest[:half], lane_roll(rest[half:])).astype(BF16)
    grads = mm_tn(attended_ref[:, : 2 * LANES], middle_ref[...])
    store_tiles(pack_ref, M_OUT, grads[:half])


def encoder_unpack_kernel(pack_ref, mixing_ref, out_ref):
    rows, half = E_ROWS, E_ROWS // 2
    for kind in range(3):
        mixing_ref[kind, :, :LANES] = pack_ref[kind * rows : (kind + 1) * rows, :].astype(F32)
    last = pack_ref[M_LAST:M_REST, :].astype(F32)
    mixing_ref[0, :, LANES:] = last[:, :HALF]
    mixing_ref[1, :, LANES:] = last[:, HALF:]
    rest = pack_ref[M_REST:M_OUT, :].astype(F32)
    mixing_ref[2, :half, LANES:] = rest[:, :HALF]
    mixing_ref[2, half:, LANES:] = rest[:, HALF:]
    for tile in range(3):
        at = slice(M_OUT + tile * half, M_OUT + (tile + 1) * half)
        out_ref[:, tile * LANES : (tile + 1) * LANES] = pack_ref[at, :].astype(F32)


def decoder_send_kernel(place_ref, feed_ref, mix_ref, send_ref):
    other = 1 - place_ref[0]
    rows = LANES
    send_ref[: 4 * rows, :] = feed_ref[pl.ds(other * 4 * rows, 4 * rows), :]
    for tile in range(4):
        send_ref[(4 + tile) * rows : (5 + tile) * rows, :] = feed_ref[
            pl.ds(GA_UP + 2 * tile * rows + other * rows, rows), :
        ]
    for tile in range(3):
        send_ref[(8 + tile) * rows : (9 + tile) * rows, :] = mix_ref[
            pl.ds(2 * tile * rows + other * rows, rows), :
        ]
    send_ref[11 * rows : 12 * rows, :] = mix_ref[pl.ds(GB_OUT + other * rows, rows), :]


def decoder_unpack_kernel(
    place_ref, feed_ref, mix_ref, got_ref, mixing_ref, out_ref, up_ref, down_ref, proj_ref
):
    core = place_ref[0]
    rows = LANES
    units = 4 * rows
    down_ref[pl.ds(core * units, units), :] = feed_ref[pl.ds(core * units, units), :].astype(F32)
    down_ref[pl.ds((1 - core) * units, units), :] = got_ref[:units, :].astype(F32)
    for tile in range(4):
        up_ref[:, pl.ds(core * units + tile * rows, rows)] = feed_ref[
            pl.ds(GA_UP + 2 * tile * rows + core * rows, rows), :
        ].astype(F32)
        up_ref[:, pl.ds((1 - core) * units + tile * rows, rows)] = got_ref[
            (4 + tile) * rows : (5 + tile) * rows, :
        ].astype(F32)
    for tile in range(3):
        mixing_ref[tile, :, pl.ds(core * rows, rows)] = mix_ref[
            pl.ds(2 * tile * rows + core * rows, rows), :
        ].astype(F32)
        mixing_ref[tile, :, pl.ds((1 - core) * rows, rows)] = got_ref[
            (8 + tile) * rows : (9 + tile) * rows, :
        ].astype(F32)
    out_ref[pl.ds(core * rows, rows), :] = mix_ref[pl.ds(GB_OUT + core * rows, rows), :].astype(F32)
    out_ref[pl.ds((1 - core) * rows, rows), :] = got_ref[11 * rows : 12 * rows, :].astype(F32)
    proj_ref[...] = mix_ref[GB_PROJ:GB_END, :].astype(F32)


def line_first(value, size):
    if size == 4:
        return (value, lax.ppermute(value, "dp", [(0, 1), (3, 2)]))
    if size & (size - 1):
        return lax.psum(value, "dp")
    distance = 1
    while distance < size:
        got = lax.ppermute(value, "dp", [(i, i ^ distance) for i in range(size)])
        value = (value.astype(F32) + got.astype(F32)).astype(BF16)
        distance *= 2
    return value


def line_next(state, size, pairs, *others):
    if size != 4:
        return state
    mine, got = after(state, *others)
    total = (mine.astype(F32) + got.astype(F32)).astype(BF16)
    return (total, lax.ppermute(total, "dp", pairs))


def line_across(state, size, *others):
    return line_next(state, size, [(1, 2), (2, 1)], *others)


def line_back(state, size, *others):
    return line_next(state, size, [(1, 0), (2, 3)], *others)


def line_last(state, size, *others):
    if size != 4:
        return state
    mine, got = after(state, *others)
    place = lax.axis_index("dp")
    return jnp.where((place == 0) | (place == 3), got, mine)


def per_device(
    data_size,
    block_input,
    span_end,
    encoder_attention_gain,
    encoder_attention_bias,
    encoder_query_key_value,
    encoder_output_weight,
    encoder_feedforward_gain,
    encoder_feedforward_bias,
    encoder_up_weight,
    encoder_down_weight,
    projection,
    decoder_attention_gain,
    decoder_attention_bias,
    decoder_query_key_value,
    decoder_output_weight,
    decoder_feedforward_gain,
    decoder_feedforward_bias,
    decoder_up_weight,
    decoder_down_weight,
    output_cotangent,
):
    row = lax.axis_index("row").astype(jnp.int32)
    y = lax.axis_index("y").astype(jnp.int32)
    core = lax.axis_index("core").astype(jnp.int32)
    length = span_end.shape[0]
    own_rows, width = block_input.shape
    block = 2 * y + core
    place = jnp.stack([core, block, row, y])
    limits = span_end.reshape(length, 1)
    limits_row = span_end.reshape(1, length)
    full = 2 * width
    low_full = 4 * LANES
    units = 2 * encoder_up_weight.shape[1]
    d_units = decoder_up_weight.shape[1]
    features = 2 * LANES

    vectors = split_three(
        jnp.stack(
            [
                encoder_attention_gain,
                encoder_attention_bias,
                encoder_feedforward_gain,
                encoder_feedforward_bias,
            ]
        )
    )
    x_pack = jnp.concatenate([block_input, vectors], 0)
    x_near = cross_once(x_pack)
    m_pack = call(
        pack_mixing_kernel,
        "pack_mixing",
        shaped(M_END, LANES, BF16),
        (after(jnp.transpose(encoder_query_key_value, (1, 0, 2)), x_pack), encoder_output_weight),
        limit=8,
    )
    m_near = cross_once(m_pack)
    vectors = split_three(
        jnp.stack(
            [
                decoder_attention_gain,
                decoder_attention_bias,
                decoder_feedforward_gain,
                decoder_feedforward_bias,
            ]
        )
    )
    keep, send = call(
        pack_decoder_kernel,
        "pack_decoder",
        (shaped(12 * LANES + 16, LANES, BF16),) * 2,
        (
            place,
            after(jnp.transpose(decoder_query_key_value, (1, 0, 2)), m_pack),
            decoder_output_weight,
            decoder_up_weight,
            decoder_down_weight,
            vectors,
        ),
        scalars=1,
        limit=8,
    )
    d_got = swap(send, "core")
    x_far = cross_twice((x_near[0][:own_rows], x_near[1][:own_rows]))
    sides = call(
        join_input_kernel,
        "join_input",
        shaped(2 * own_rows, full, BF16),
        (y.reshape(1), after(x_pack, keep), *x_near, *x_far),
        scalars=1,
        limit=8,
    )
    m_far = cross_twice(m_near)
    u_pack = call(
        pack_up_kernel,
        "pack_up",
        shaped(U_END, LANES, BF16),
        (after(encoder_up_weight, x_near), projection),
        limit=8,
    )
    stream, normed_first, e_vec = call(
        first_norm_kernel,
        "first_norm",
        (shaped(length, full, BF16), shaped(length, full, BF16), shaped(4, full, F32)),
        (place, after(sides, m_far), swap(sides, "core"), x_pack[own_rows:], x_near[0][own_rows:]),
        scalars=1,
        limit=8,
        cost=2.4,
    )
    m_parts = (m_pack, *m_near, *m_far)
    u_near = cross_once(u_pack)
    down_pack = call(
        pack_down_kernel,
        "pack_down",
        shaped(encoder_down_weight.shape[0] * 3, LANES, BF16),
        (after(encoder_down_weight, u_pack, m_near),),
        limit=8,
    )
    down_near = cross_once(down_pack)
    mixed, e_mixing = call(
        encoder_mixing_kernel,
        "encoder_mixing",
        (shaped(length, 9 * LANES, BF16), shaped(full, 9 * LANES, BF16)),
        (after(normed_first, down_pack), *m_parts),
        (both_scratch(m_parts),),
        limit=12,
        cost=3,
    )
    attended, inverse = attention_forward(mixed, limits, HD1)
    u_parts = (u_pack, *u_near, *cross_twice(u_near))
    partial = call(
        functools.partial(out_product_kernel, encoder_out_rows),
        "encoder_out",
        shaped(length, full, BF16),
        (after(attended, u_near, down_near), *m_parts),
        (pltpu.VMEM((E_ROWS, full), BF16), both_scratch(m_parts)),
        limit=12,
        cost=1.5,
    )
    got = swap(partial, "core")
    down_parts = (down_pack, *down_near, *cross_twice(down_near))
    dm_pack, df_pack = call(
        join_decoder_kernel,
        "join_decoder",
        (shaped(DM_END, LANES, BF16), shaped(DF_END, LANES, BF16)),
        (place, after(keep, partial), d_got, output_cotangent),
        scalars=1,
        limit=8,
    )
    dm_near = cross_once(dm_pack)
    own, near_x, near_y, first, second = u_parts
    half = second.shape[0]
    proj_rows = jnp.concatenate(
        [own[U_PROJ:], near_y[U_PROJ:], near_x[U_PROJ:], second[U_PROJ - half :]], 0
    )
    proj_got = swap(proj_rows, "core")

    middle, normed_second, active, slope, partial = call(
        feed_forward_kernel,
        "feed_forward",
        (
            shaped(length, full, F32),
            shaped(length, full, BF16),
            shaped(length, units, BF16),
            shaped(length, units, BF16),
            shaped(length, full, BF16),
        ),
        (after(stream, dm_pack), partial, got, e_vec, *u_parts, *down_parts),
        (pltpu.VMEM((TILE, full), F32), both_scratch(u_parts), both_scratch(down_parts)),
        limit=16,
        cost=12,
    )
    dm_parts = (dm_pack, *dm_near, *cross_twice(dm_near, middle))
    df_near = cross_once(after(df_pack, dm_near, middle))
    (
        own_encoder_out, encoder_low, d_stream, d_normed_first, d_mixed, proj_weight, d_vec, d_mixing,
    ) = call(
        bridge_kernel,
        "bridge",
        (
            shaped(own_rows, width, F32),
            shaped(length, width, BF16),
            shaped(length, low_full, F32),
            shaped(length, low_full, BF16),
            shaped(length, 6 * LANES, BF16),
            shaped(full, low_full, BF16),
            shaped(4, low_full, F32),
            shaped(low_full, 6 * LANES, BF16),
        ),
        (place, middle, partial, swap(partial, "core"), proj_rows, proj_got, *dm_parts),
        (both_scratch(dm_parts),),
        scalars=1,
        limit=12,
        cost=5.7,
    )

    d_attended, d_inverse = attention_forward(d_mixed, limits, HD2)
    df_parts = (df_pack, *df_near, *cross_twice(df_near, d_attended))
    own, near_x, near_y, first, second = df_parts
    cut = lambda value, base=0: value[DF_COT - base : DF_END - base]
    cot_rows = jnp.concatenate(
        [cut(own), cut(near_y), cut(near_x), cut(second, second.shape[0])], 0
    )
    cotangent = call(
        cotangent_kernel,
        "cotangent",
        shaped(length, low_full, BF16),
        (place, cot_rows, swap(after(cot_rows, d_attended), "core")),
        scalars=1,
        limit=8,
    )
    partial = call(
        functools.partial(out_product_kernel, decoder_out_rows),
        "decoder_out",
        shaped(length, low_full, BF16),
        (d_attended, *dm_parts),
        (pltpu.VMEM((2 * LANES, low_full), BF16), both_scratch(dm_parts)),
        limit=12,
        cost=1,
    )
    d_middle, d_normed_second, d_active, d_hidden, partial = call(
        decoder_feed_kernel,
        "decoder_feed",
        (
            shaped(length, low_full, F32),
            shaped(length, low_full, BF16),
            shaped(length, d_units, BF16),
            shaped(length, d_units, BF16),
            shaped(length, low_full, BF16),
        ),
        (d_stream, partial, swap(partial, "core"), d_vec, cotangent, *df_parts),
        (pltpu.VMEM((TILE, low_full), F32), both_scratch(df_parts)),
        limit=16,
        cost=8,
    )

    got = swap(partial, "core")
    grads_a = call(
        feed_grads_kernel,
        "decoder_feed_grads",
        shaped(GA_END, LANES, BF16),
        (after(d_active, partial), cotangent, d_normed_second, d_hidden),
        limit=8,
        cost=0.8,
    )
    sum_a = line_first(grads_a, data_size)
    d_middle_grad, d_middle_low, attended_grad, d_second_sums = call(
        functools.partial(middle_back_kernel, decoder_out_rows),
        "decoder_middle_back",
        (
            shaped(length, low_full, F32),
            shaped(length, features, BF16),
            shaped(length, 2 * LANES, F32),
            shaped(2, low_full, F32),
        ),
        (place, after(partial, grads_a), got, d_middle, cotangent, d_vec, *dm_parts),
        (pltpu.VMEM((2 * LANES, low_full), BF16), both_scratch(dm_parts)),
        scalars=1,
        limit=12,
        cost=2.6,
    )
    back = functools.partial(
        attention_backward, d_mixed, d_attended, d_inverse, attended_grad, limits_row, HD2
    )
    d_lows = back(0, 1)
    sum_a = line_across(sum_a, data_size, d_lows)
    d_lows = d_lows + attention_backward(
        d_mixed, d_attended, d_inverse, after(attended_grad, sum_a[0]), limits_row, HD2, 1, 1
    )
    sum_a = line_back(sum_a, data_size)
    sum_a_back = sum_a[0]
    partial = call(
        mixed_back_kernel,
        "decoder_mixed_back",
        shaped(length, low_full, BF16),
        (after(d_lows[0], sum_a_back), *d_lows[1:], d_mixing),
        limit=12,
        cost=1.6,
    )
    got = swap(partial, "core")

    proj_low, encoder_grad, down_low, d_first_sums = call(
        bridge_back_kernel,
        "bridge_back",
        (
            shaped(length, low_full, BF16),
            shaped(length, full, F32),
            shaped(length, full, BF16),
            shaped(2, low_full, F32),
        ),
        (place, partial, got, d_stream, d_middle_grad, d_vec, proj_weight),
        scalars=1,
        limit=12,
        cost=3.9,
    )
    grads_c = call(
        product_kernel,
        "encoder_down_grads",
        shaped(units // 2, width, BF16),
        (active, down_low),
        limit=8,
        cost=1,
    )
    sum_c = line_first(grads_c, data_size)
    grads_b = call(
        mixing_grads_kernel,
        "decoder_mixing_grads",
        shaped(GB_END, LANES, BF16),
        (
            place, d_normed_first, *d_lows[:3], d_attended, d_middle_low, encoder_low,
            after(proj_low, grads_c),
        ),
        scalars=1,
        limit=8,
        cost=1.3,
    )
    sum_b = line_first(grads_b, data_size)
    hidden_low, partial = call(
        feed_back_kernel,
        "feed_back",
        (shaped(length, units, BF16), shaped(length, full, BF16)),
        (after(down_low, grads_b, sum_a), slope, *u_parts, *down_parts),
        (pltpu.VMEM((TILE, full), F32), both_scratch(u_parts), both_scratch(down_parts)),
        limit=16,
        cost=12,
    )
    got = swap(partial, "core")
    sum_c = line_across(sum_c, data_size, partial)
    grads_e = call(
        product_kernel,
        "encoder_up_grads",
        shaped(width, units // 2, BF16),
        (normed_second, after(hidden_low, sum_c[0])),
        limit=8,
        cost=1000,
    )
    sum_e = line_first(grads_e, data_size)
    middle_grad, middle_low, attended_grad, second_sums = call(
        functools.partial(middle_back_kernel, encoder_out_rows),
        "encoder_middle_back",
        (
            shaped(length, full, F32),
            shaped(length, width, BF16),
            shaped(length, 3 * LANES, F32),
            shaped(2, full, F32),
        ),
        (place, after(partial, grads_e), got, middle, encoder_grad, e_vec, *m_parts),
        (pltpu.VMEM((E_ROWS, full), BF16), both_scratch(m_parts)),
        scalars=1,
        limit=12,
        cost=5.5,
    )
    sum_b = line_across(sum_b, data_size, middle_low)
    first = attention_backward(
        mixed, attended, inverse, after(attended_grad, sum_b[0]), limits_row, HD1, 0, 1
    )
    sum_c = line_back(sum_c, data_size, first)
    sum_e = line_across(sum_e, data_size, first)
    second = attention_backward(
        mixed, attended, inverse, after(attended_grad, sum_c[0], sum_e[0]), limits_row, HD1, 1, 1
    )
    grads_d = call(
        encoder_grads_kernel,
        "encoder_mixing_grads",
        shaped(M_END, LANES, BF16),
        (normed_first, *first, *second, attended, middle_low),
        limit=12,
        cost=1.1,
    )
    sum_d = line_first(grads_d, data_size)
    third = attention_backward(
        mixed, attended, inverse, after(attended_grad, grads_d), limits_row, HD1, 2, 1
    )
    sum_b = line_back(sum_b, data_size, third)
    sum_e = line_back(sum_e, data_size, third)
    lows = (*first, *second, after(third[0], sum_b[0], sum_e[0]), *third[1:])
    keep, send = call(
        mixed_last_kernel,
        "encoder_mixed_back",
        (shaped(own_rows, full, BF16),) * 2,
        (place, *lows, e_mixing),
        scalars=1,
        limit=12,
        cost=1.8,
    )
    got = swap(send, "core")
    own_input_grad, first_sums = call(
        input_back_kernel,
        "input_back",
        (shaped(own_rows, width, F32), shaped(2, full, F32)),
        (place, keep, got, stream, middle_grad, e_vec),
        scalars=1,
        limit=8,
        cost=1.8,
    )

    def in_order(value, index):
        half = value.shape[1] // 2
        return jnp.where(index == 0, value, jnp.concatenate([value[:, half:], value[:, :half]], 1))

    e_sums = in_order(jnp.concatenate([first_sums, second_sums], 0), row)
    d_sums = in_order(jnp.concatenate([d_first_sums, d_second_sums], 0), y)
    sums = jnp.concatenate([e_sums, jnp.pad(d_sums, ((0, 0), (0, full - low_full)))], 0)
    sum_d = line_across(sum_d, data_size, own_input_grad)
    sums = after(sums, sum_d[0])
    sums = jnp.sum(lax.all_gather(sums, ("row", "y", "core")), 0)
    sums = jnp.sum(lax.all_gather(sums, "dp"), 0)
    e_sums = lax.dynamic_slice_in_dim(sums[:4], row * width, width, 1)
    share = decoder_attention_gain.shape[0]
    d_sums = lax.dynamic_slice_in_dim(sums[4:], block * share, share, 1)

    own, near_x = after(df_parts[:2], sums)
    out_rows, out_columns = output_cotangent.shape
    active_rows = lax.dynamic_slice_in_dim(d_active, row * out_rows, out_rows, 0)
    span = DF_DOWN + d_units // 2
    down = jnp.concatenate(
        [
            jnp.concatenate([p[DF_DOWN:span], p[span : span + d_units // 2]], 1)
            for p in (own, near_x)
        ],
        0,
    )
    last = mm(active_rows, down)
    mine = lax.dynamic_slice_in_dim(last, core * out_columns, out_columns, 1)
    others = lax.dynamic_slice_in_dim(last, (1 - core) * out_columns, out_columns, 1)
    own_decoder_out = (
        lax.dynamic_slice(d_middle, (row * out_rows, core * out_columns), (out_rows, out_columns))
        + mine
        + swap(others.astype(BF16), "core").astype(F32)
    )

    grads_a = line_last(sum_a, data_size, sums)
    grads_b = line_last(sum_b, data_size, sums)
    send = call(
        decoder_send_kernel,
        "decoder_send",
        shaped(12 * LANES, LANES, BF16),
        (place, grads_a, grads_b),
        scalars=1,
        limit=8,
    )
    d_mixing_grad, d_out_grad, d_up_grad, d_down_grad, proj_grad = call(
        decoder_unpack_kernel,
        "decoder_unpack",
        (
            jax.ShapeDtypeStruct((3, LANES, 2 * LANES), F32),
            shaped(2 * LANES, LANES, F32),
            shaped(LANES, d_units, F32),
            shaped(d_units, LANES, F32),
            shaped(width, LANES, F32),
        ),
        (place, grads_a, grads_b, swap(send, "core")),
        scalars=1,
        limit=8,
        cost=1.9,
    )
    grads_c = line_last(sum_c, data_size, sums).astype(F32)
    grads_e = line_last(sum_e, data_size, sums).astype(F32)
    sum_d = line_back(sum_d, data_size, sums)
    grads_d = line_last(sum_d, data_size, d_down_grad, grads_c, grads_e)
    mixing_grad, out_grad = call(
        encoder_unpack_kernel,
        "encoder_unpack",
        (
            jax.ShapeDtypeStruct((3, width, width // 2), F32),
            shaped(width // 2, width, F32),
        ),
        (grads_d,),
        limit=8,
    )
    return (
        own_encoder_out,
        own_decoder_out,
        own_input_grad,
        e_sums[0],
        e_sums[1],
        jnp.transpose(mixing_grad, (1, 0, 2)),
        out_grad,
        e_sums[2],
        e_sums[3],
        grads_e,
        grads_c,
        proj_grad,
        d_sums[0],
        d_sums[1],
        jnp.transpose(d_mixing_grad, (1, 0, 2)),
        d_out_grad,
        d_sums[2],
        d_sums[3],
        d_up_grad,
        d_down_grad,
    )


def solution(mesh):
    data, row, col = (mesh.shape[name] for name in ("dp", "row", "col"))
    split = Mesh(mesh.devices.reshape(data, row, col // 2, 2), ("dp", "row", "y", "core"))
    c = ("y", "core")
    in_specs = (
        P(("dp", *c), "row"),
        P("dp"),
        P("row"),
        P("row"),
        P("row", None, c),
        P(c, "row"),
        P("row"),
        P("row"),
        P("row", c),
        P(c, "row"),
        P("row", c),
        P(c),
        P(c),
        P(c, None, "row"),
        P("row", c),
        P(c),
        P(c),
        P(c, "row"),
        P("row", c),
        P(("dp", "row"), c),
    )
    out_specs = (
        P(("dp", *c), "row"),
        P(("dp", "row"), c),
        P(("dp", *c), "row"),
        P("row"),
        P("row"),
        P("row", None, c),
        P(c, "row"),
        P("row"),
        P("row"),
        P("row", c),
        P(c, "row"),
        P("row", c),
        P(c),
        P(c),
        P(c, None, "row"),
        P("row", c),
        P(c),
        P(c),
        P(c, "row"),
        P("row", c),
    )
    return jax.shard_map(
        functools.partial(per_device, data),
        mesh=split,
        in_specs=in_specs,
        out_specs=out_specs,
        check_vma=False,
    )
```

```python
import functools
import math

import jax
import jax.numpy as jnp
from jax import lax
from jax.experimental import pallas as pl
from jax.experimental.pallas import tpu as pltpu
from jax.sharding import Mesh, PartitionSpec as P

D1 = 768
D2 = 512
HD1 = 64
HD2 = 32
EPSILON = 1e-06
BLOCK = 512
LANES = 128
LOG2E = 1.4426950408889634
SWAP = [(0, 1), (1, 0)]
BF16 = jnp.bfloat16
F32 = jnp.float32


def mm(left, right):
    return jnp.dot(left, right, preferred_element_type=F32)


def mm_nt(left, right):
    return lax.dot_general(left, right, (((1,), (1,)), ((), ())), preferred_element_type=F32)


def mm_tn(left, right):
    return lax.dot_general(left, right, (((0,), (0,)), ((), ())), preferred_element_type=F32)


def head_lanes(head, head_size, rows):
    lane = lax.broadcasted_iota(jnp.int32, (rows, LANES), 1)
    return (lane >= head * head_size) & (lane < (head + 1) * head_size)


def attention_forward_kernel(head_size, q_ref, k_ref, v_ref, limit_ref, out_ref, inv_ref, aug_ref):
    tile = pl.program_id(1)
    rows = q_ref.shape[0]
    heads = LANES // head_size
    per_block = BLOCK // rows
    scale = head_size ** (-0.5) * LOG2E

    @pl.when(tile == 0)
    def _():
        aug_ref[:, :LANES] = v_ref[...]
        aug_ref[:, LANES:] = jnp.ones_like(v_ref)

    def run(block):
        queries = q_ref[...]
        limits = limit_ref[...]
        places = block * BLOCK + lax.broadcasted_iota(jnp.int32, (rows, BLOCK), 1)
        visible = places <= limits
        result = jnp.zeros((rows, LANES), F32)
        inverses = jnp.zeros((rows, LANES), F32)
        for head in range(heads):
            own = head_lanes(head, head_size, rows)
            masked = jnp.where(own, queries, jnp.zeros_like(queries))
            total = jnp.zeros((rows, 2 * LANES), F32)
            for part in range(block + 1):
                span = slice(part * BLOCK, (part + 1) * BLOCK)
                weights = jnp.exp2(mm_nt(masked, k_ref[span, :]) * scale)
                if part == block:
                    weights = jnp.where(visible, weights, 0.0)
                total = total + mm(weights.astype(BF16), aug_ref[span, :])
            inverse = 1.0 / total[:, LANES:]
            result = jnp.where(own, total[:, :LANES] * inverse, result)
            inverses = jnp.where(own, inverse, inverses)
        out_ref[...] = result.astype(BF16)
        inv_ref[...] = inverses

    for block in range(k_ref.shape[0] // BLOCK):
        pl.when(tile // per_block == block)(functools.partial(run, block))


def attention_forward(mixed, limits, head_size):
    length, width = mixed.shape[0], mixed.shape[1] // 3
    groups = width // LANES
    rows = 256
    return pl.pallas_call(
        functools.partial(attention_forward_kernel, head_size),
        out_shape=(
            jax.ShapeDtypeStruct((length, width), BF16),
            jax.ShapeDtypeStruct((length, width), F32),
        ),
        grid=(groups, length // rows),
        in_specs=[
            pl.BlockSpec((rows, LANES), lambda g, t: (t, g)),
            pl.BlockSpec((length, LANES), lambda g, t: (0, groups + g)),
            pl.BlockSpec((length, LANES), lambda g, t: (0, 2 * groups + g)),
            pl.BlockSpec((rows, 1), lambda g, t: (t, 0)),
        ],
        out_specs=[
            pl.BlockSpec((rows, LANES), lambda g, t: (t, g)),
            pl.BlockSpec((rows, LANES), lambda g, t: (t, g)),
        ],
        scratch_shapes=[pltpu.VMEM((length, 2 * LANES), BF16)],
        compiler_params=pltpu.CompilerParams(vmem_limit_bytes=24 << 20),
        cost_estimate=pl.CostEstimate(flops=int(10.5 * COST), bytes_accessed=1, transcendentals=0),
        name="attention_forward",
    )(mixed, mixed, mixed, limits)


def attention_backward_kernel(
    head_size,
    pairs,
    q_ref,
    k_ref,
    v_ref,
    att_ref,
    inv_ref,
    grad_ref,
    limit_ref,
    dq_ref,
    dk_ref,
    dv_ref,
    vaug_ref,
    naug_ref,
    dq_acc,
    dk_acc,
    dv_acc,
):
    step = pl.program_id(1)
    length = q_ref.shape[0]
    heads = LANES // head_size
    scaling = head_size ** (-0.5)

    @pl.when(step == 0)
    def _():
        lane = lax.broadcasted_iota(jnp.int32, (length, LANES), 1)
        vaug_ref[:, :LANES] = v_ref[...]
        vaug_ref[:, LANES:] = jnp.where(lane < 2, 1.0, 0.0).astype(BF16)
        scaled = grad_ref[...] * inv_ref[...]
        terms = scaled * att_ref[...].astype(F32)
        low = scaled.astype(BF16)
        for head in range(heads):
            own = head_lanes(head, head_size, length)
            total = -jnp.sum(jnp.where(own, terms, 0.0), 1, keepdims=True)
            high = total.astype(BF16).astype(F32)
            rest = total - high
            naug_ref[head, :, :LANES] = jnp.where(own, low, jnp.zeros_like(low))
            naug_ref[head, :, LANES:] = jnp.where(
                lane == 0, high, jnp.where(lane == 1, rest, 0.0)
            ).astype(BF16)
        dq_acc[...] = jnp.zeros_like(dq_acc)
        dk_acc[...] = jnp.zeros_like(dk_acc)
        dv_acc[...] = jnp.zeros_like(dv_acc)

    def run(key_block, query_block):
        keys = slice(key_block * BLOCK, (key_block + 1) * BLOCK)
        queries = slice(query_block * BLOCK, (query_block + 1) * BLOCK)
        key_rows = k_ref[keys, :]
        query_rows = q_ref[queries, :]
        key_flipped = key_rows.astype(F32).T.astype(BF16)
        if key_block == query_block:
            places = key_block * BLOCK + lax.broadcasted_iota(jnp.int32, (BLOCK, BLOCK), 0)
            visible = places <= limit_ref[:, queries]
        dq = jnp.zeros((LANES, BLOCK), F32)
        dk = jnp.zeros((BLOCK, LANES), F32)
        dv = jnp.zeros((BLOCK, LANES), F32)
        for head in range(heads):
            own = head_lanes(head, head_size, BLOCK)
            masked = jnp.where(own, query_rows, jnp.zeros_like(query_rows))
            weights = jnp.exp2(mm_nt(key_rows, masked) * (scaling * LOG2E))
            if key_block == query_block:
                weights = jnp.where(visible, weights, 0.0)
            naug = naug_ref[head, queries, :]
            slopes = mm_nt(vaug_ref[keys, :], naug)
            scores = (weights * slopes).astype(BF16)
            dv += mm(weights.astype(BF16), naug[:, :LANES])
            dk += mm(scores, masked)
            row = lax.broadcasted_iota(jnp.int32, (LANES, BLOCK), 0)
            mine = (row >= head * head_size) & (row < (head + 1) * head_size)
            dq += mm(jnp.where(mine, key_flipped, jnp.zeros_like(key_flipped)), scores)
        dq_acc[:, queries] += dq
        dk_acc[keys, :] += dk
        dv_acc[keys, :] += dv

    for number, (key_block, query_block) in enumerate(pairs):
        pl.when(step == number)(functools.partial(run, key_block, query_block))

    @pl.when(step == len(pairs) - 1)
    def _():
        dq_ref[...] = (dq_acc[...].T * scaling).astype(BF16)
        dk_ref[...] = (dk_acc[...] * scaling).astype(BF16)
        dv_ref[...] = dv_acc[...].astype(BF16)


def attention_backward(
    mixed, attended, inverse, grad, limits_row, head_size, start=0, count=None
):
    length, width = attended.shape
    groups = width // LANES
    count = groups if count is None else count
    blocks = length // BLOCK
    pairs = [(k, q) for q in range(blocks) for k in range(q + 1)]
    whole = lambda offset: pl.BlockSpec((length, LANES), lambda g, s: (0, offset + g))
    results = pl.pallas_call(
        functools.partial(attention_backward_kernel, head_size, pairs),
        out_shape=(jax.ShapeDtypeStruct((length, count * LANES), BF16),) * 3,
        grid=(count, len(pairs)),
        in_specs=[
            whole(start),
            whole(groups + start),
            whole(2 * groups + start),
            whole(start),
            whole(start),
            whole(start),
            pl.BlockSpec((1, length), lambda g, s: (0, 0)),
        ],
        out_specs=[whole(0), whole(0), whole(0)],
        scratch_shapes=[
            pltpu.VMEM((length, 2 * LANES), BF16),
            pltpu.VMEM((LANES // head_size, length, 2 * LANES), BF16),
            pltpu.VMEM((LANES, length), F32),
            pltpu.VMEM((length, LANES), F32),
            pltpu.VMEM((length, LANES), F32),
        ],
        compiler_params=pltpu.CompilerParams(vmem_limit_bytes=32 << 20),
        cost_estimate=pl.CostEstimate(
            flops=int(count * (5.2 if head_size == HD1 else 9.6) * COST), bytes_accessed=1, transcendentals=0
        ),
        name="attention_backward",
    )(mixed, mixed, mixed, attended, inverse, grad, limits_row)
    if count == 1:
        return tuple(results)
    return tuple(r[:, g * LANES : (g + 1) * LANES] for g in range(count) for r in results)


def swap(value, axis):
    return lax.ppermute(value, axis, SWAP)


def after(value, *others):
    return lax.optimization_barrier((value, *others))[0]


def near(pack):
    return (swap(pack, "row"), swap(pack, "y"))


def across_by_row(pair, *others):
    return swap(after(pair[0], *others), "y")


def across_by_y(pair, *others):
    return swap(after(pair[1], *others), "row")


def across_both(pair, split, *others):
    first, second = after((pair[0][:split], pair[1][split:]), *others)
    return (swap(first, "y"), swap(second, "row"))


class Parts:
    def __init__(self, refs, start=0, far=None):
        own, by_row, by_y, across = refs
        self.refs = ((own, by_y), (by_row, across))
        self.start = start
        self.far = start if far is None else far

    def rows(self, by_row, by_y, base, count, offset=0):
        start = self.far if by_row and by_y else self.start
        return self.refs[by_row][by_y][pl.ds(start + base + offset, count), :]


class Pair:
    def __init__(self, refs, split):
        own, by_row, by_y, first, second = refs
        self.first = Parts((own, by_row, by_y, first))
        self.second = Parts((own, by_row, by_y, second), split, 0)


COST = 1e7
VMEM = pl.BlockSpec(memory_space=pltpu.VMEM)
SMEM = pl.BlockSpec(memory_space=pltpu.SMEM)


def call(
    kernel, name, outs, args, scratch=(), scalars=0, limit=48, cost=1, needs=(), marks=(), fetch=False
):
    count = len(args)
    arrays = count - scalars
    if needs:
        args = (*args[:scalars], after(args[scalars], *needs), *args[scalars + 1 :])
    scratch = list(scratch)
    if fetch:
        scratch += [pltpu.VMEM(a.shape, a.dtype) for a in args[scalars:]]
        scratch.append(pltpu.SemaphoreType.DMA((arrays,)))

    def body(*refs):
        given, rest = refs[:count], refs[count + len(marks) :]
        if fetch:
            local, semaphores, rest = rest[-arrays - 1 : -1], rest[-1], rest[: -arrays - 1]
            copies = [
                pltpu.make_async_copy(source, target, semaphores.at[i])
                for i, (source, target) in enumerate(zip(given[scalars:], local))
            ]
            for copy in copies:
                copy.start()
            for copy in copies:
                copy.wait()
            given = (*given[:scalars], *local)
        kernel(*given, *rest)

    place = pl.BlockSpec(memory_space=pltpu.HBM) if fetch else VMEM
    return pl.pallas_call(
        body,
        out_shape=outs,
        in_specs=[SMEM] * scalars + [place] * arrays + [VMEM] * len(marks),
        out_specs=jax.tree.map(lambda _: VMEM, outs),
        scratch_shapes=scratch,
        compiler_params=pltpu.CompilerParams(vmem_limit_bytes=limit << 20),
        cost_estimate=pl.CostEstimate(
            flops=int(cost * COST), bytes_accessed=1, transcendentals=0
        ),
        name=name,
    )(*args, *marks)


def marker_kernel(in_ref, out_ref):
    out_ref[...] = in_ref[...]


def marker(value, cost, *others):
    return call(
        marker_kernel,
        "marker",
        jax.ShapeDtypeStruct(value.shape, value.dtype),
        (value,),
        cost=cost,
        limit=4,
        needs=others,
    )


def shaped(rows, columns, kind):
    return jax.ShapeDtypeStruct((rows, columns), kind)


def store_three(ref, base, vectors):
    for tile in range(vectors[0].shape[0]):
        values = jnp.concatenate([v[tile : tile + 1, :] for v in vectors], 0)
        high = values.astype(BF16)
        rest = values - high.astype(F32)
        middle = rest.astype(BF16)
        low = (rest - middle.astype(F32)).astype(BF16)
        ref[base + 16 * tile : base + 16 * (tile + 1), :] = jnp.concatenate(
            [high, middle, low, jnp.zeros_like(high)], 0
        )


def join_three(rows):
    wide = rows.astype(F32)
    return wide[0:4] + wide[4:8] + wide[8:12]


TILE = 256


def lane_roll(values):
    return pltpu.roll(values.astype(F32), LANES // 2, 1)


HALF = LANES // 2
E_ROWS = 3 * LANES
A_LAST = 2 * E_ROWS
A_VEC = 3 * E_ROWS
A_END = A_VEC + 48
B_REST = E_ROWS
B_OUT = B_REST + E_ROWS // 2
B_END = 3 * E_ROWS
E_FEED = 18 * LANES
DA_VEC = 6 * LANES
DA_END = DA_VEC + 32
DB_PROJ = 2 * LANES
DB_END = 8 * LANES
F_COT = 8 * LANES
F_END = 12 * LANES
D_SEND = 19 * LANES + 16


def pack_mixing_kernel(w_ref, out_ref, v1, v2, v3, v4, pack_ref):
    store_three(pack_ref, A_VEC, (v1, v2, v3, v4))
    rows = w_ref.shape[1]
    pack_ref[:rows, :] = w_ref[0, :, :LANES]
    pack_ref[rows : 2 * rows, :] = w_ref[1, :, :LANES]
    pack_ref[A_LAST:A_VEC, :HALF] = w_ref[0, :, LANES:]
    pack_ref[A_LAST:A_VEC, HALF:] = w_ref[1, :, LANES:]
    pack_ref[A_END : A_END + rows, :] = w_ref[2, :, :LANES]
    rest = A_END + B_REST
    pack_ref[rest : rest + rows // 2, :HALF] = w_ref[2, : rows // 2, LANES:]
    pack_ref[rest : rest + rows // 2, HALF:] = w_ref[2, rows // 2 :, LANES:]
    heads = out_ref.shape[0]
    base = A_END + B_OUT
    for tile in range(3):
        pack_ref[base + tile * heads : base + (tile + 1) * heads, :] = out_ref[
            :, tile * LANES : (tile + 1) * LANES
        ]


def pack_encoder_kernel(up_ref, down_ref, mix_ref, first_ref, second_ref):
    for weight_ref, pack_ref in ((up_ref, first_ref), (down_ref, second_ref)):
        rows, columns = weight_ref.shape
        for tile in range(columns // LANES):
            pack_ref[tile * rows : (tile + 1) * rows, :] = weight_ref[
                :, tile * LANES : (tile + 1) * LANES
            ]
    first_ref[E_FEED:, :] = mix_ref[:DA_END, :]
    second_ref[E_FEED:, :] = mix_ref[DA_END:, :]


def pack_decoder_kernel(
    place_ref, mix_ref, out_ref, up_ref, down_ref, v1, v2, v3, v4, proj_ref, cot_ref, keep_ref, send_ref
):
    core = place_ref[0]
    rows = mix_ref.shape[1]
    units = up_ref.shape[1] // 2
    for target, half in ((keep_ref, core), (send_ref, 1 - core)):
        base = 0
        for i in range(3):
            target[base : base + rows, :] = mix_ref[i, :, pl.ds(half * LANES, LANES)]
            base += rows
        target[base : base + LANES, :] = out_ref[pl.ds(half * LANES, LANES), :]
        base += LANES
        for i in range(units // LANES):
            target[base : base + rows, :] = up_ref[:, pl.ds(half * units + i * LANES, LANES)]
            base += rows
        target[base : base + units, :] = down_ref[pl.ds(half * units, units), :]
        base += units
        target[base : base + 3 * LANES, :] = proj_ref[...]
        base += 3 * LANES
        target[base : base + 4 * LANES, :] = cot_ref[...]
        base += 4 * LANES
        store_three(target, base, (v1, v2, v3, v4))


def join_decoder_kernel(place_ref, keep_ref, got_ref, mix_ref, feed_ref):
    core = place_ref[0]
    rows = LANES
    for source, side in ((keep_ref, core), (got_ref, 1 - core)):
        base = 0
        for i in range(3):
            mix_ref[pl.ds(2 * i * rows + side * rows, rows), :] = source[base : base + rows, :]
            base += rows
        mix_ref[pl.ds(DA_END + side * rows, rows), :] = source[base : base + rows, :]
        base += rows
        for i in range(4):
            feed_ref[pl.ds(2 * i * rows + side * rows, rows), :] = source[base : base + rows, :]
            base += rows
        feed_ref[pl.ds(F_END + side * 4 * rows, 4 * rows), :] = source[base : base + 4 * rows, :]
        base += 4 * rows
        mix_ref[pl.ds(DA_END + DB_PROJ + side * 3 * rows, 3 * rows), :] = source[
            base : base + 3 * rows, :
        ]
        base += 3 * rows
        for start in (F_COT, F_END + F_COT):
            feed_ref[pl.ds(start + side * 2 * rows, 2 * rows), :] = source[base : base + 2 * rows, :]
            base += 2 * rows
        mix_ref[pl.ds(DA_VEC + side * 16, 16), :] = source[base : base + 16, :]


def join_input_kernel(place_ref, own, by_row, by_y, first, second, out_ref):
    y = place_ref[3]
    width = own.shape[1]
    split = second.shape[0]
    for right, by_y_side, sources in (
        (0, 0, (own, own)),
        (1, 0, (by_row, by_row)),
        (0, 1, (by_y, by_y)),
        (1, 1, (first, second)),
    ):
        base = (y if by_y_side == 0 else 1 - y) * 2 * split
        for number, source in enumerate(sources):
            start = 0 if source is second else number * first.shape[0]
            at = pl.ds(base + number * split, split)
            out_ref[at, right * width : (right + 1) * width] = source[start : start + split, :]


def norm_rows(values):
    width = values.shape[1]
    average = jnp.sum(values, 1, keepdims=True) / width
    variance = jnp.sum(values * values, 1, keepdims=True) / width - average * average
    inverse = lax.rsqrt(variance + EPSILON)
    return ((values - average) * inverse, inverse)


def first_norm_kernel(core_ref, own, other, vec_own, vec_other, x_ref, normed_ref, vec_ref):
    core = core_ref[0]
    for side, source in ((0, vec_own), (3, vec_other)):
        for tile in range(3):
            vec_ref[:, (side + tile) * LANES : (side + tile + 1) * LANES] = join_three(
                source[A_VEC + 16 * tile : A_VEC + 16 * (tile + 1), :]
            )
    rows = own.shape[0] // 2
    gain, bias = vec_ref[0:1, :], vec_ref[1:2, :]
    for source, place in ((own, core), (other, 1 - core)):
        for y in range(2):
            values = source[y * rows : (y + 1) * rows, :]
            target = pl.ds((2 * y + place) * rows, rows)
            x_ref[target, :] = values
            centred, _ = norm_rows(values.astype(F32))
            normed_ref[target, :] = (centred * gain + bias).astype(BF16)


def encoder_mixing_kernel(normed_ref, *refs):
    pair = Pair(refs[:5], A_END)
    first, second = pair.first, pair.second
    mixed_ref, weight_ref, out_ref = refs[5:8]
    out_ref[...] = encoder_out_rows(second)
    rows = E_ROWS
    low = lax.broadcasted_iota(jnp.int32, (rows, LANES), 1) < HALF
    for half in range(2):
        at = slice(half * rows, (half + 1) * rows)
        for kind, parts, base in ((0, first, 0), (1, first, rows), (2, second, 0)):
            for group, side in ((0, 0), (2, 1)):
                tile = (3 * kind + group) * LANES
                weight_ref[at, tile : tile + LANES] = parts.rows(half, side, base, rows)
        mine = first.rows(half, 0, A_LAST, rows).astype(F32)
        theirs = first.rows(half, 1, A_LAST, rows).astype(F32)
        weight_ref[at, LANES : 2 * LANES] = jnp.where(low, mine, lane_roll(theirs)).astype(BF16)
        weight_ref[at, 4 * LANES : 5 * LANES] = jnp.where(low, lane_roll(mine), theirs).astype(BF16)
        mine = second.rows(half, 0, B_REST, rows // 2).astype(F32)
        theirs = second.rows(half, 1, B_REST, rows // 2).astype(F32)
        mine = jnp.concatenate([mine, lane_roll(mine)], 0)
        theirs = jnp.concatenate([lane_roll(theirs), theirs], 0)
        weight_ref[at, 7 * LANES : 8 * LANES] = jnp.where(low, mine, theirs).astype(BF16)

    @pl.loop(0, normed_ref.shape[0] // TILE)
    def _(tile):
        at = pl.ds(tile * TILE, TILE)
        mixed_ref[at, :] = mm(normed_ref[at, :], weight_ref[...]).astype(BF16)


def encoder_out_rows(parts):
    heads = 3 * LANES // 2
    sides = [
        jnp.concatenate(
            [parts.rows(i, j, B_OUT + t * heads, heads) for i in range(2) for t in range(3)], 1
        )
        for j in range(2)
    ]
    return jnp.concatenate([sides[0], sides[1][LANES:], sides[1][:LANES]], 0)


def decoder_out_rows(parts):
    return jnp.concatenate(
        [
            jnp.concatenate(
                [parts.rows(i, j, t * LANES, LANES) for j in range(2) for t in range(2)], 1
            )
            for i in range(2)
        ],
        0,
    )


def attend_kernel(
    head_size, mixed_ref, limit_ref, weight_ref, attended_ref, inverse_ref, partial_ref, aug_ref
):
    length, width = attended_ref.shape
    groups, heads = width // LANES, LANES // head_size
    scale = head_size ** (-0.5) * LOG2E
    for group in range(groups):
        at = (2 * groups + group) * LANES
        aug_ref[group, :, :LANES] = mixed_ref[:, at : at + LANES]
        aug_ref[group, :, LANES:] = jnp.ones((length, LANES), BF16)

    for block in range(length // BLOCK):

        @pl.loop(0, BLOCK // TILE)
        def _(step):
            at = pl.ds(block * BLOCK + step * TILE, TILE)
            limits = limit_ref[at, :]
            places = block * BLOCK + lax.broadcasted_iota(jnp.int32, (TILE, BLOCK), 1)
            visible = places <= limits

            @pl.loop(0, groups)
            def _(group):
                queries = mixed_ref[at, pl.ds(group * LANES, LANES)]
                result = jnp.zeros((TILE, LANES), F32)
                inverses = jnp.zeros((TILE, LANES), F32)
                for head in range(heads):
                    own = head_lanes(head, head_size, TILE)
                    masked = jnp.where(own, queries, jnp.zeros_like(queries))
                    total = jnp.zeros((TILE, 2 * LANES), F32)
                    for part in range(block + 1):
                        span = slice(part * BLOCK, (part + 1) * BLOCK)
                        keys = mixed_ref[span, pl.ds((groups + group) * LANES, LANES)]
                        weights = jnp.exp2(mm_nt(masked, keys) * scale)
                        if part == block:
                            weights = jnp.where(visible, weights, 0.0)
                        total = total + mm(weights.astype(BF16), aug_ref[group, span, :])
                    inverse = 1.0 / total[:, LANES:]
                    result = jnp.where(own, total[:, :LANES] * inverse, result)
                    inverses = jnp.where(own, inverse, inverses)
                lanes = pl.ds(group * LANES, LANES)
                attended_ref[at, lanes] = result.astype(BF16)
                inverse_ref[at, lanes] = inverses

            partial_ref[at, :] = mm(attended_ref[at, :], weight_ref[...]).astype(BF16)


def gelu_pair(values):
    area = 0.5 * (1.0 + lax.erf(values * (0.5**0.5)))
    slope = area + values * jnp.exp2(values * values * (-0.5 * LOG2E)) * (0.5 / math.pi) ** 0.5
    return (values * area, slope)


class Feed:
    def __init__(self, up_parts, down_parts, decoder):
        self.up_parts = up_parts
        self.down_parts = down_parts
        self.decoder = decoder
        self.features = 2 * LANES if decoder else 3 * LANES
        self.units = 4 * LANES if decoder else 6 * LANES
        self.down = 0
        self.chunks = self.units // (2 * LANES)

    def rows(self, parts, feature, unit, base, count, offset):
        if self.decoder:
            return parts.rows(unit, feature, base, count, offset)
        return parts.rows(feature, unit, base, count, offset)

    def up_chunk(self, unit, chunk):
        f = self.features
        return jnp.concatenate(
            [
                jnp.concatenate(
                    [
                        self.rows(
                            self.up_parts, i, unit, 0, f, pl.multiple_of((2 * chunk + t) * f, f)
                        )
                        for t in range(2)
                    ],
                    1,
                )
                for i in range(2)
            ],
            0,
        )

    def down_chunk(self, unit, chunk):
        return jnp.concatenate(
            [
                self.rows(
                    self.down_parts,
                    i,
                    unit,
                    self.down + t * self.units,
                    2 * LANES,
                    pl.multiple_of(chunk * 2 * LANES, 2 * LANES),
                )
                for i in range(2)
                for t in range(self.features // LANES)
            ],
            1,
        )


def feed_forward_kernel(stream_ref, mine_ref, got_ref, vec_ref, *refs):
    middle_ref, normed_ref, active_ref, slope_ref, partial_ref, total_ref = refs[8:14]
    feed = Feed(Parts(refs[:4]), Parts(refs[4:8]), False)
    gain, bias = vec_ref[2:3, :], vec_ref[3:4, :]

    @pl.loop(0, stream_ref.shape[0] // TILE)
    def _(tile):
        at = pl.ds(tile * TILE, TILE)
        middle = stream_ref[at, :].astype(F32) + (
            mine_ref[at, :].astype(F32) + got_ref[at, :].astype(F32)
        )
        middle_ref[at, :] = middle
        centred, _ = norm_rows(middle)
        normed_ref[at, :] = (centred * gain + bias).astype(BF16)
        total_ref[...] = jnp.zeros_like(total_ref)

        @pl.loop(0, feed.chunks)
        def _(chunk):
            for unit in range(2):
                hidden = mm(normed_ref[at, :], feed.up_chunk(unit, chunk))
                active, slope = gelu_pair(hidden)
                lanes = pl.ds(unit * feed.units + chunk * 2 * LANES, 2 * LANES)
                low = active.astype(BF16)
                active_ref[at, lanes] = low
                slope_ref[at, lanes] = slope.astype(BF16)
                total_ref[...] += mm(low, feed.down_chunk(unit, chunk))

        partial_ref[at, :] = total_ref[...].astype(BF16)


def decoder_feed_kernel(
    place_ref, stream_ref, mine_ref, got_ref, vec_ref, *refs
):
    middle_ref, normed_ref, active_ref, hidden_ref, partial_ref, cot_ref, total_ref = refs[5:12]
    pair = Pair(refs[:5], F_END)
    first, second = pair.first, pair.second
    row = place_ref[2]
    for i in range(2):
        for number, parts in enumerate((first, second)):
            at = pl.ds((row if i == 0 else 1 - row) * 4 * LANES + number * 2 * LANES, 2 * LANES)
            for tile in range(4):
                cot_ref[at, tile * LANES : (tile + 1) * LANES] = parts.rows(
                    i, tile // 2, F_COT + (tile % 2) * 2 * LANES, 2 * LANES
                )
    feed = Feed(first, second, True)
    gain, bias = vec_ref[2:3, :], vec_ref[3:4, :]

    @pl.loop(0, stream_ref.shape[0] // TILE)
    def _(tile):
        at = pl.ds(tile * TILE, TILE)
        middle = stream_ref[at, :] + (mine_ref[at, :].astype(F32) + got_ref[at, :].astype(F32))
        middle_ref[at, :] = middle
        centred, _ = norm_rows(middle)
        normed_ref[at, :] = (centred * gain + bias).astype(BF16)
        total_ref[...] = jnp.zeros_like(total_ref)

        @pl.loop(0, feed.chunks)
        def _(chunk):
            for unit in range(2):
                upward = feed.up_chunk(unit, chunk)
                hidden = mm(normed_ref[at, :], upward)
                active, slope = gelu_pair(hidden)
                lanes = pl.ds(unit * feed.units + chunk * 2 * LANES, 2 * LANES)
                active_ref[at, lanes] = active.astype(BF16)
                grad = mm_nt(cot_ref[at, :], feed.down_chunk(unit, chunk))
                low = (grad * slope).astype(BF16)
                hidden_ref[at, lanes] = low
                total_ref[...] += mm_nt(low, upward)

        partial_ref[at, :] = total_ref[...].astype(BF16)


def bridge_kernel(place_ref, middle_ref, mine_ref, got_ref, *refs):
    (
        out_ref, low_ref, stream_ref, normed_ref, mixed_ref, weight_ref, vec_ref, mixing_ref,
        back_ref,
    ) = refs[8:17]
    block = place_ref[1]
    first, second = Parts(refs[:4], E_FEED), Parts(refs[4:8], E_FEED)
    back_ref[...] = decoder_out_rows(second)
    rows = E_ROWS
    for j in range(2):
        for c in range(2):
            tile = (2 * j + c) * LANES
            for i in range(2):
                weight_ref[i * rows : (i + 1) * rows, tile : tile + LANES] = second.rows(
                    i, j, DB_PROJ + c * rows, rows
                )
            vec_ref[:, tile : tile + LANES] = join_three(first.rows(0, j, DA_VEC + 16 * c, 16))
    for kind in range(3):
        for i in range(2):
            tile = (2 * kind + i) * LANES
            for j in range(2):
                mixing_ref[2 * j * LANES : 2 * (j + 1) * LANES, tile : tile + LANES] = first.rows(
                    i, j, 2 * kind * LANES, 2 * LANES
                )
    gain, bias = vec_ref[0:1, :], vec_ref[1:2, :]
    width = low_ref.shape[1]

    @pl.loop(0, middle_ref.shape[0] // TILE)
    def _(tile):
        at = pl.ds(tile * TILE, TILE)
        total = middle_ref[at, :] + (mine_ref[at, :].astype(F32) + got_ref[at, :].astype(F32))
        low = total.astype(BF16)

        @pl.when(tile == block)
        def _():
            out_ref[...] = total[:, :width]

        low_ref[at, :] = low[:, :width]
        stream = mm(low, weight_ref[...])
        stream_ref[at, :] = stream
        centred, _ = norm_rows(stream)
        normed = (centred * gain + bias).astype(BF16)
        normed_ref[at, :] = normed
        mixed_ref[at, :] = mm(normed, mixing_ref[...]).astype(BF16)


def norm_back(incoming, centred, inverse, gain):
    width = incoming.shape[1]
    scaled = incoming * gain
    first = jnp.sum(scaled, 1, keepdims=True) / width
    second = jnp.sum(scaled * centred, 1, keepdims=True) / width
    return inverse * (scaled - first - centred * second)


def store_sums(sums_ref, incoming, centred):
    sums_ref[0:1, :] = jnp.sum(incoming * centred, 0, keepdims=True)
    sums_ref[1:2, :] = jnp.sum(incoming, 0, keepdims=True)


def own_sums(place_ref, tile, sums_ref, incoming, centred):
    half = TILE // 2

    @pl.when((tile == place_ref[1]) & (place_ref[2] == 0))
    def _():
        store_sums(sums_ref, incoming[:half], centred[:half])

    @pl.when((tile == place_ref[1]) & (place_ref[2] == 1))
    def _():
        store_sums(sums_ref, incoming[half:], centred[half:])


def middle_back_kernel(
    place_ref, mine_ref, got_ref, middle_ref, grad_ref, vec_ref, weight_ref,
    total_ref, low_ref, attended_ref, sums_ref,
):
    gain = vec_ref[2:3, :]
    width = low_ref.shape[1]

    @pl.loop(0, middle_ref.shape[0] // TILE)
    def _(tile):
        at = pl.ds(tile * TILE, TILE)
        incoming = mine_ref[at, :].astype(F32) + got_ref[at, :].astype(F32)
        centred, inverse = norm_rows(middle_ref[at, :])
        total = grad_ref[at, :].astype(F32) + norm_back(incoming, centred, inverse, gain)
        total_ref[at, :] = total
        low = total.astype(BF16)
        low_ref[at, :] = low[:, :width]
        attended_ref[at, :] = mm_nt(low, weight_ref[...])
        own_sums(place_ref, tile, sums_ref, incoming, centred)


def mixed_low(refs, at):
    kinds = len(refs) // 3
    return jnp.concatenate([refs[3 * g + i][at, :] for i in range(3) for g in range(kinds)], 1)


def mixed_back_kernel(*refs):
    lows, weight_ref, partial_ref = refs[:-2], refs[-2], refs[-1]

    @pl.loop(0, partial_ref.shape[0] // TILE)
    def _(tile):
        at = pl.ds(tile * TILE, TILE)
        partial_ref[at, :] = mm_nt(mixed_low(lows, at), weight_ref[...]).astype(BF16)


def mixed_last_kernel(place_ref, *refs):
    core, y = place_ref[0], place_ref[3]
    lows, weight_ref, keep_ref, send_ref = refs[:-3], refs[-3], refs[-2], refs[-1]
    for target, side in ((keep_ref, core), (send_ref, 1 - core)):
        at = pl.ds((2 * y + side) * TILE, TILE)
        target[...] = mm_nt(mixed_low(lows, at), weight_ref[...]).astype(BF16)


def bridge_back_kernel(
    place_ref, mine_ref, got_ref, stream_ref, grad_ref, vec_ref, proj_ref,
    low_ref, encoder_ref, down_ref, sums_ref,
):
    gain = vec_ref[0:1, :]

    @pl.loop(0, stream_ref.shape[0] // TILE)
    def _(tile):
        at = pl.ds(tile * TILE, TILE)
        incoming = mine_ref[at, :].astype(F32) + got_ref[at, :].astype(F32)
        centred, inverse = norm_rows(stream_ref[at, :])
        grad = grad_ref[at, :] + norm_back(incoming, centred, inverse, gain)
        own_sums(place_ref, tile, sums_ref, incoming, centred)
        low = grad.astype(BF16)
        low_ref[at, :] = low
        encoder = mm_nt(low, proj_ref[...])
        encoder_ref[at, :] = encoder
        down_ref[at, :] = encoder.astype(BF16)


def feed_back_kernel(down_ref, slope_ref, *refs):
    hidden_ref, partial_ref, total_ref = refs[8:11]
    feed = Feed(Parts(refs[:4]), Parts(refs[4:8]), False)

    @pl.loop(0, down_ref.shape[0] // TILE)
    def _(tile):
        at = pl.ds(tile * TILE, TILE)
        total_ref[...] = jnp.zeros_like(total_ref)

        @pl.loop(0, feed.chunks)
        def _(chunk):
            for unit in range(2):
                lanes = pl.ds(unit * feed.units + chunk * 2 * LANES, 2 * LANES)
                back = mm_nt(down_ref[at, :], feed.down_chunk(unit, chunk))
                hidden = (back * slope_ref[at, lanes].astype(F32)).astype(BF16)
                hidden_ref[at, lanes] = hidden
                total_ref[...] += mm_nt(hidden, feed.up_chunk(unit, chunk))

        partial_ref[at, :] = total_ref[...].astype(BF16)


def input_back_kernel(place_ref, mine_ref, got_ref, x_ref, grad_ref, vec_ref, out_ref, sums_ref):
    at = pl.ds(place_ref[1] * TILE, TILE)
    incoming = mine_ref[...].astype(F32) + got_ref[...].astype(F32)
    centred, inverse = norm_rows(x_ref[at, :].astype(F32))
    total = grad_ref[at, :] + norm_back(incoming, centred, inverse, vec_ref[0:1, :])
    out_ref[...] = total[:, : out_ref.shape[1]]
    own_sums(place_ref, place_ref[1], sums_ref, incoming, centred)


def store_tiles(ref, base, value):
    rows = value.shape[0]
    for tile in range(value.shape[1] // LANES):
        ref[base + tile * rows : base + (tile + 1) * rows, :] = value[
            :, tile * LANES : (tile + 1) * LANES
        ].astype(BF16)


G_LAST = 3 * E_ROWS
G_REST = 4 * E_ROWS
G_OUT = G_REST + E_ROWS // 2
G_END = 6 * E_ROWS
GA_UP = 8 * LANES
GA_END = 16 * LANES
GB_OUT = 6 * LANES
GB_PROJ = 8 * LANES
GB_END = 11 * LANES


def feed_grads_kernel(active_ref, cot_ref, normed_ref, hidden_ref, pack_ref):
    units, features = 4 * LANES, 2 * LANES
    store_tiles(pack_ref, 0, mm_tn(active_ref[:, :units], cot_ref[:, :features]))
    store_tiles(pack_ref, GA_UP, mm_tn(normed_ref[:, :features], hidden_ref[:, :units]))


def mixing_grads_kernel(
    place_ref, normed_ref, q_ref, k_ref, v_ref, attended_ref, middle_ref, encoder_ref, proj_ref, pack_ref
):
    lows = jnp.concatenate([q_ref[:, :LANES], k_ref[:, :LANES], v_ref[:, :LANES]], 1)
    store_tiles(pack_ref, 0, mm_tn(normed_ref[:, : 2 * LANES], lows))
    store_tiles(pack_ref, GB_OUT, mm_tn(attended_ref[:, :LANES], middle_ref[...]))
    own = proj_ref[:, pl.ds(place_ref[0] * LANES, LANES)]
    store_tiles(pack_ref, GB_PROJ, mm_tn(encoder_ref[...], own))


def product_kernel(left_ref, right_ref, out_ref):
    rows, columns = out_ref.shape
    out_ref[...] = mm_tn(left_ref[:, :rows], right_ref[:, :columns]).astype(BF16)


def encoder_grads_kernel(
    normed_ref, q_ref, k_ref, v_ref, q2_ref, k2_ref, v2_ref, attended_ref, middle_ref, pack_ref
):
    low = lax.broadcasted_iota(jnp.int32, q2_ref.shape, 1) < HALF
    last = jnp.where(low, q2_ref[...].astype(F32), lane_roll(k2_ref[...])).astype(BF16)
    lows = jnp.concatenate([q_ref[...], k_ref[...], v_ref[...], last, v2_ref[...]], 1)
    grads = mm_tn(normed_ref[:, :E_ROWS], lows)
    store_tiles(pack_ref, 0, grads[:, : 4 * LANES])
    rest = grads[:, 4 * LANES :]
    half = E_ROWS // 2
    low = lax.broadcasted_iota(jnp.int32, (half, LANES), 1) < HALF
    pack_ref[G_REST:G_OUT, :] = jnp.where(low, rest[:half], lane_roll(rest[half:])).astype(BF16)
    grads = mm_tn(attended_ref[:, : 2 * LANES], middle_ref[...])
    store_tiles(pack_ref, G_OUT, grads[:half])


def encoder_unpack_kernel(pack_ref, mixing_ref, out_ref):
    rows, half = E_ROWS, E_ROWS // 2
    for kind in range(3):
        mixing_ref[kind, :, :LANES] = pack_ref[kind * rows : (kind + 1) * rows, :].astype(F32)
    last = pack_ref[G_LAST:G_REST, :].astype(F32)
    mixing_ref[0, :, LANES:] = last[:, :HALF]
    mixing_ref[1, :, LANES:] = last[:, HALF:]
    rest = pack_ref[G_REST:G_OUT, :].astype(F32)
    mixing_ref[2, :half, LANES:] = rest[:, :HALF]
    mixing_ref[2, half:, LANES:] = rest[:, HALF:]
    for tile in range(3):
        at = slice(G_OUT + tile * half, G_OUT + (tile + 1) * half)
        out_ref[:, tile * LANES : (tile + 1) * LANES] = pack_ref[at, :].astype(F32)


def decoder_send_kernel(place_ref, feed_ref, mix_ref, send_ref):
    other = 1 - place_ref[0]
    rows = LANES
    send_ref[: 4 * rows, :] = feed_ref[pl.ds(other * 4 * rows, 4 * rows), :]
    for tile in range(4):
        send_ref[(4 + tile) * rows : (5 + tile) * rows, :] = feed_ref[
            pl.ds(GA_UP + 2 * tile * rows + other * rows, rows), :
        ]
    for tile in range(3):
        send_ref[(8 + tile) * rows : (9 + tile) * rows, :] = mix_ref[
            pl.ds(2 * tile * rows + other * rows, rows), :
        ]
    send_ref[11 * rows : 12 * rows, :] = mix_ref[pl.ds(GB_OUT + other * rows, rows), :]


def decoder_unpack_kernel(
    place_ref, feed_ref, mix_ref, got_ref, mixing_ref, out_ref, up_ref, down_ref, proj_ref
):
    core = place_ref[0]
    rows = LANES
    units = 4 * rows
    down_ref[pl.ds(core * units, units), :] = feed_ref[pl.ds(core * units, units), :].astype(F32)
    down_ref[pl.ds((1 - core) * units, units), :] = got_ref[:units, :].astype(F32)
    for tile in range(4):
        up_ref[:, pl.ds(core * units + tile * rows, rows)] = feed_ref[
            pl.ds(GA_UP + 2 * tile * rows + core * rows, rows), :
        ].astype(F32)
        up_ref[:, pl.ds((1 - core) * units + tile * rows, rows)] = got_ref[
            (4 + tile) * rows : (5 + tile) * rows, :
        ].astype(F32)
    for tile in range(3):
        mixing_ref[tile, :, pl.ds(core * rows, rows)] = mix_ref[
            pl.ds(2 * tile * rows + core * rows, rows), :
        ].astype(F32)
        mixing_ref[tile, :, pl.ds((1 - core) * rows, rows)] = got_ref[
            (8 + tile) * rows : (9 + tile) * rows, :
        ].astype(F32)
    out_ref[pl.ds(core * rows, rows), :] = mix_ref[pl.ds(GB_OUT + core * rows, rows), :].astype(F32)
    out_ref[pl.ds((1 - core) * rows, rows), :] = got_ref[11 * rows : 12 * rows, :].astype(F32)
    proj_ref[...] = mix_ref[GB_PROJ:GB_END, :].astype(F32)


def line_first(value, size):
    if size == 4:
        return (value, lax.ppermute(value, "dp", [(0, 1), (3, 2)]))
    if size & (size - 1):
        return lax.psum(value, "dp")
    distance = 1
    while distance < size:
        got = lax.ppermute(value, "dp", [(i, i ^ distance) for i in range(size)])
        value = (value.astype(F32) + got.astype(F32)).astype(BF16)
        distance *= 2
    return value


def line_next(state, size, pairs, *others):
    if size != 4:
        return state
    mine, got = after(state, *others)
    total = (mine.astype(F32) + got.astype(F32)).astype(BF16)
    return (total, lax.ppermute(total, "dp", pairs))


def line_across(state, size, *others):
    return line_next(state, size, [(1, 2), (2, 1)], *others)


def line_back(state, size, *others):
    return line_next(state, size, [(1, 0), (2, 3)], *others)


def line_last(state, size, *others):
    if size != 4:
        return state
    mine, got = after(state, *others)
    place = lax.axis_index("dp")
    return jnp.where((place == 0) | (place == 3), got, mine)


def dp_sum(value, size):
    place = lax.axis_index("dp")
    terms = [value] + [
        lax.ppermute(value, "dp", [(i, (i + step) % size) for i in range(size)])
        for step in range(1, size)
    ]
    terms = terms[::-1]
    return jnp.sum(lax.dynamic_slice_in_dim(jnp.stack(terms + terms), size - 1 - place, size, 0), 0)


def per_device(
    data_size,
    block_input,
    span_end,
    encoder_attention_gain,
    encoder_attention_bias,
    encoder_query_key_value,
    encoder_output_weight,
    encoder_feedforward_gain,
    encoder_feedforward_bias,
    encoder_up_weight,
    encoder_down_weight,
    projection,
    decoder_attention_gain,
    decoder_attention_bias,
    decoder_query_key_value,
    decoder_output_weight,
    decoder_feedforward_gain,
    decoder_feedforward_bias,
    decoder_up_weight,
    decoder_down_weight,
    output_cotangent,
):
    row = lax.axis_index("row").astype(jnp.int32)
    y = lax.axis_index("y").astype(jnp.int32)
    core = lax.axis_index("core").astype(jnp.int32)
    length = span_end.shape[0]
    own_rows, width = block_input.shape
    block = 2 * y + core
    place = jnp.stack([core, block, row, y])
    limits = span_end.reshape(length, 1)
    limits_row = span_end.reshape(1, length)
    full = 2 * width
    low_full = 4 * LANES
    units = 2 * encoder_up_weight.shape[1]
    d_units = decoder_up_weight.shape[1]
    features = 2 * LANES

    half = own_rows // 2
    x_near = near(block_input)
    tick = jnp.zeros((8, LANES), F32)
    row_of = lambda vector: vector.reshape(-1, LANES)
    keep, send = call(
        pack_decoder_kernel,
        "pack_decoder",
        (shaped(D_SEND, LANES, BF16),) * 2,
        (
            place,
            jnp.transpose(decoder_query_key_value, (1, 0, 2)),
            decoder_output_weight,
            decoder_up_weight,
            decoder_down_weight,
            row_of(decoder_attention_gain),
            row_of(decoder_attention_bias),
            row_of(decoder_feedforward_gain),
            row_of(decoder_feedforward_bias),
            projection,
            output_cotangent,
        ),
        scalars=1,
        limit=56,
        fetch=True,
    )
    m_pack = call(
        pack_mixing_kernel,
        "pack_mixing",
        shaped(A_END + B_END, LANES, BF16),
        (
            jnp.transpose(encoder_query_key_value, (1, 0, 2)),
            encoder_output_weight,
            row_of(encoder_attention_gain),
            row_of(encoder_attention_bias),
            row_of(encoder_feedforward_gain),
            row_of(encoder_feedforward_bias),
        ),
        limit=56,
        fetch=True,
        needs=(x_near, keep),
    )
    m_near = near(m_pack)
    d_got = swap(send, "core")
    dm_pack, f_pack = call(
        join_decoder_kernel,
        "join_decoder",
        (shaped(DA_END + DB_END, LANES, BF16), shaped(2 * F_END, LANES, BF16)),
        (place, keep, d_got),
        scalars=1,
        limit=8,
    )
    up, down = call(
        pack_encoder_kernel,
        "pack_encoder",
        (shaped(E_FEED + DA_END, LANES, BF16), shaped(E_FEED + DB_END, LANES, BF16)),
        (encoder_up_weight, encoder_down_weight, dm_pack),
        limit=56,
        fetch=True,
    )
    x_far = across_both(x_near, half, up)
    m_far = across_both(m_near, A_END, x_far)
    sides = call(
        join_input_kernel,
        "join_input",
        shaped(2 * own_rows, full, BF16),
        (place, block_input, *x_near, *x_far),
        scalars=1,
        limit=56,
        fetch=True,
        needs=(m_near,),
    )
    m_parts = (m_pack, *m_near, *m_far)
    up_near, down_near = near(after(up, sides)), near(after(down, sides))
    mark = marker(tick, 5000, m_far)
    stream, normed_first, e_vec = call(
        first_norm_kernel,
        "first_norm",
        (shaped(length, full, BF16), shaped(length, full, BF16), shaped(4, full, F32)),
        (place, sides, swap(sides, "core"), m_pack, m_near[0]),
        scalars=1,
        limit=8,
        marks=(mark,),
    )
    mixed, e_mixing, e_out = call(
        encoder_mixing_kernel,
        "encoder_mixing",
        (
            shaped(length, 9 * LANES, BF16),
            shaped(full, 9 * LANES, BF16),
            shaped(E_ROWS, full, BF16),
        ),
        (normed_first, *m_parts),
        limit=12,
        cost=3,
    )
    attended, inverse, partial = call(
        functools.partial(attend_kernel, HD1),
        "encoder_attend",
        (
            shaped(length, E_ROWS, BF16),
            shaped(length, E_ROWS, F32),
            shaped(length, full, BF16),
        ),
        (mixed, limits, e_out),
        (pltpu.VMEM((3, length, 2 * LANES), BF16),),
        limit=16,
        cost=12,
    )
    got = swap(partial, "core")
    up_parts = (up, *up_near, across_by_row(up_near, attended, down_near))
    down_parts = (down, *down_near, across_by_y(down_near, attended, up_near))
    f_near = near(after(f_pack, down_near))
    mark = marker(tick, 10000, up_parts[1:], down_parts[1:])
    middle, normed_second, active, slope, partial = call(
        feed_forward_kernel,
        "feed_forward",
        (
            shaped(length, full, F32),
            shaped(length, full, BF16),
            shaped(length, units, BF16),
            shaped(length, units, BF16),
            shaped(length, full, BF16),
        ),
        (stream, partial, got, e_vec, *up_parts, *down_parts),
        (pltpu.VMEM((TILE, full), F32),),
        limit=16,
        cost=12,
        marks=(mark,),
    )
    mark = marker(tick, 10000, middle)
    (
        own_encoder_out, encoder_low, d_stream, d_normed_first, d_mixed, proj_weight, d_vec, d_mixing,
        d_out,
    ) = call(
        bridge_kernel,
        "bridge",
        (
            shaped(own_rows, width, F32),
            shaped(length, width, BF16),
            shaped(length, low_full, F32),
            shaped(length, low_full, BF16),
            shaped(length, 6 * LANES, BF16),
            shaped(full, low_full, BF16),
            shaped(4, low_full, F32),
            shaped(low_full, 6 * LANES, BF16),
            shaped(2 * LANES, low_full, BF16),
        ),
        (place, middle, partial, swap(partial, "core"), *up_parts, *down_parts),
        scalars=1,
        limit=12,
        marks=(mark,),
        cost=5.7,
    )

    d_attended, d_inverse, partial = call(
        functools.partial(attend_kernel, HD2),
        "decoder_attend",
        (
            shaped(length, 2 * LANES, BF16),
            shaped(length, 2 * LANES, F32),
            shaped(length, low_full, BF16),
        ),
        (d_mixed, limits, d_out),
        (pltpu.VMEM((2, length, 2 * LANES), BF16),),
        limit=16,
        cost=11,
    )
    f_parts = (f_pack, *f_near, *across_both(f_near, F_END, d_mixed))
    d_middle, d_normed_second, d_active, d_hidden, partial, cotangent = call(
        decoder_feed_kernel,
        "decoder_feed",
        (
            shaped(length, low_full, F32),
            shaped(length, low_full, BF16),
            shaped(length, d_units, BF16),
            shaped(length, d_units, BF16),
            shaped(length, low_full, BF16),
            shaped(length, low_full, BF16),
        ),
        (place, d_stream, partial, swap(partial, "core"), d_vec, *f_parts),
        (pltpu.VMEM((TILE, low_full), F32),),
        scalars=1,
        limit=16,
        cost=8,
    )

    got = swap(partial, "core")
    grads_a = call(
        feed_grads_kernel,
        "decoder_feed_grads",
        shaped(GA_END, LANES, BF16),
        (after(d_active, partial), cotangent, d_normed_second, d_hidden),
        limit=8,
        cost=0.8,
    )
    sum_a = line_first(grads_a, data_size)
    d_middle_grad, d_middle_low, attended_grad, d_second_sums = call(
        middle_back_kernel,
        "decoder_middle_back",
        (
            shaped(length, low_full, F32),
            shaped(length, features, BF16),
            shaped(length, 2 * LANES, F32),
            shaped(2, low_full, F32),
        ),
        (place, after(partial, grads_a), got, d_middle, cotangent, d_vec, d_out),
        scalars=1,
        limit=12,
        cost=2.6,
    )
    d_lows = attention_backward(
        d_mixed, d_attended, d_inverse, attended_grad, limits_row, HD2, 0, 1
    )
    sum_a = line_across(sum_a, data_size, d_lows)
    d_lows = d_lows + attention_backward(
        d_mixed, d_attended, d_inverse, after(attended_grad, sum_a[0]), limits_row, HD2, 1, 1
    )
    sum_a = line_back(sum_a, data_size, d_lows)
    partial = call(
        mixed_back_kernel,
        "decoder_mixed_back",
        shaped(length, low_full, BF16),
        (after(d_lows[0], sum_a[0]), *d_lows[1:], d_mixing),
        limit=12,
        cost=1.6,
    )
    got = swap(partial, "core")

    proj_low, encoder_grad, down_low, d_first_sums = call(
        bridge_back_kernel,
        "bridge_back",
        (
            shaped(length, low_full, BF16),
            shaped(length, full, F32),
            shaped(length, full, BF16),
            shaped(2, low_full, F32),
        ),
        (place, partial, got, d_stream, d_middle_grad, d_vec, proj_weight),
        scalars=1,
        limit=12,
        cost=3.9,
    )
    grads_c = call(
        product_kernel,
        "encoder_down_grads",
        shaped(units // 2, width, BF16),
        (active, down_low),
        limit=8,
        cost=1,
    )
    sum_c = line_first(grads_c, data_size)
    grads_b = call(
        mixing_grads_kernel,
        "decoder_mixing_grads",
        shaped(GB_END, LANES, BF16),
        (
            place, d_normed_first, *d_lows[:3], d_attended, d_middle_low, encoder_low,
            after(proj_low, grads_c),
        ),
        scalars=1,
        limit=8,
        cost=1.3,
    )
    sum_b = line_first(grads_b, data_size)
    hidden_low, partial = call(
        feed_back_kernel,
        "feed_back",
        (shaped(length, units, BF16), shaped(length, full, BF16)),
        (after(down_low, grads_b), slope, *up_parts, *down_parts),
        (pltpu.VMEM((TILE, full), F32),),
        limit=16,
        cost=12,
    )
    got = swap(partial, "core")
    sum_c = line_across(sum_c, data_size, partial)
    grads_e = call(
        product_kernel,
        "encoder_up_grads",
        shaped(width, units // 2, BF16),
        (normed_second, after(hidden_low, sum_c[0])),
        limit=8,
        cost=1000,
    )
    sum_e = line_first(grads_e, data_size)
    middle_grad, middle_low, attended_grad, second_sums = call(
        middle_back_kernel,
        "encoder_middle_back",
        (
            shaped(length, full, F32),
            shaped(length, width, BF16),
            shaped(length, 3 * LANES, F32),
            shaped(2, full, F32),
        ),
        (place, after(partial, grads_e), got, middle, encoder_grad, e_vec, e_out),
        scalars=1,
        limit=12,
        cost=5.5,
    )
    first = attention_backward(
        mixed, attended, inverse, attended_grad, limits_row, HD1, 0, 1
    )
    sum_c = line_back(sum_c, data_size, first)
    sum_b = line_across(sum_b, data_size, first)
    sum_e = line_across(sum_e, data_size, first)
    second = attention_backward(
        mixed,
        attended,
        inverse,
        after(attended_grad, sum_c[0], sum_b[0], sum_e[0], sum_a),
        limits_row,
        HD1,
        1,
        1,
    )
    grads_d = call(
        encoder_grads_kernel,
        "encoder_mixing_grads",
        shaped(G_END, LANES, BF16),
        (normed_first, *first, *second, attended, middle_low),
        limit=12,
        cost=1.1,
    )
    sum_d = line_first(grads_d, data_size)
    sum_e = line_back(sum_e, data_size, grads_d)
    third = attention_backward(
        mixed, attended, inverse, after(attended_grad, grads_d, sum_c, sum_e[0]), limits_row, HD1, 2, 1
    )
    sum_d = line_across(sum_d, data_size, third)
    lows = (*first, *second, after(third[0], sum_d[0]), *third[1:])
    keep, send = call(
        mixed_last_kernel,
        "encoder_mixed_back",
        (shaped(own_rows, full, BF16),) * 2,
        (place, *lows, e_mixing),
        scalars=1,
        limit=12,
        cost=1.8,
    )
    got = swap(send, "core")
    sum_b = line_back(sum_b, data_size, send)
    own_input_grad, first_sums = call(
        input_back_kernel,
        "input_back",
        (shaped(own_rows, width, F32), shaped(2, full, F32)),
        (place, after(keep, sum_b[0]), got, stream, middle_grad, e_vec),
        scalars=1,
        limit=8,
        cost=1.8,
    )

    def in_order(value, index):
        half = value.shape[1] // 2
        return jnp.where(index == 0, value, jnp.concatenate([value[:, half:], value[:, :half]], 1))

    e_sums = in_order(jnp.concatenate([first_sums, second_sums], 0), row)
    d_sums = in_order(jnp.concatenate([d_first_sums, d_second_sums], 0), y)
    sums = jnp.concatenate([e_sums, jnp.pad(d_sums, ((0, 0), (0, full - low_full)))], 0)
    sums = jnp.sum(lax.all_gather(sums, ("row", "y", "core")), 0)
    sum_d = line_back(sum_d, data_size, sums)
    sums = dp_sum(after(sums, sum_d[0]), data_size)
    e_sums = lax.dynamic_slice_in_dim(sums[:4], row * width, width, 1)
    share = decoder_attention_gain.shape[0]
    d_sums = lax.dynamic_slice_in_dim(sums[4:], block * share, share, 1)

    own, by_row = after(f_parts[:2], sum_d[0])
    out_rows, out_columns = output_cotangent.shape
    active_rows = lax.dynamic_slice_in_dim(d_active, row * out_rows, out_rows, 0)
    half = d_units // 2
    span = F_END + half
    down = jnp.concatenate(
        [jnp.concatenate([p[F_END:span], p[span : span + half]], 1) for p in (own, by_row)], 0
    )
    last = mm(active_rows, down)
    mine = lax.dynamic_slice_in_dim(last, core * out_columns, out_columns, 1)
    others = lax.dynamic_slice_in_dim(last, (1 - core) * out_columns, out_columns, 1)
    own_decoder_out = (
        lax.dynamic_slice(d_middle, (row * out_rows, core * out_columns), (out_rows, out_columns))
        + mine
        + swap(others.astype(BF16), "core").astype(F32)
    )

    grads_a = line_last(sum_a, data_size, own_input_grad)
    grads_b = line_last(sum_b, data_size, sum_d[0])
    send = call(
        decoder_send_kernel,
        "decoder_send",
        shaped(12 * LANES, LANES, BF16),
        (place, grads_a, grads_b),
        scalars=1,
        limit=8,
    )
    d_mixing_grad, d_out_grad, d_up_grad, d_down_grad, proj_grad = call(
        decoder_unpack_kernel,
        "decoder_unpack",
        (
            jax.ShapeDtypeStruct((3, LANES, 2 * LANES), F32),
            shaped(2 * LANES, LANES, F32),
            shaped(LANES, d_units, F32),
            shaped(d_units, LANES, F32),
            shaped(width, LANES, F32),
        ),
        (place, grads_a, grads_b, swap(send, "core")),
        scalars=1,
        limit=8,
        cost=1.9,
    )
    grads_c = line_last(sum_c, data_size, sum_d[0]).astype(F32)
    grads_e = line_last(sum_e, data_size, sum_d[0]).astype(F32)
    grads_d = line_last(sum_d, data_size, d_down_grad, grads_c, grads_e)
    mixing_grad, out_grad = call(
        encoder_unpack_kernel,
        "encoder_unpack",
        (
            jax.ShapeDtypeStruct((3, width, width // 2), F32),
            shaped(width // 2, width, F32),
        ),
        (grads_d,),
        limit=8,
    )
    return (
        own_encoder_out,
        own_decoder_out,
        own_input_grad,
        e_sums[0],
        e_sums[1],
        jnp.transpose(mixing_grad, (1, 0, 2)),
        out_grad,
        e_sums[2],
        e_sums[3],
        grads_e,
        grads_c,
        proj_grad,
        d_sums[0],
        d_sums[1],
        jnp.transpose(d_mixing_grad, (1, 0, 2)),
        d_out_grad,
        d_sums[2],
        d_sums[3],
        d_up_grad,
        d_down_grad,
    )


def solution(mesh):
    data, row, col = (mesh.shape[name] for name in ("dp", "row", "col"))
    split = Mesh(mesh.devices.reshape(data, row, col // 2, 2), ("dp", "row", "y", "core"))
    c = ("y", "core")
    in_specs = (
        P(("dp", *c), "row"),
        P("dp"),
        P("row"),
        P("row"),
        P("row", None, c),
        P(c, "row"),
        P("row"),
        P("row"),
        P("row", c),
        P(c, "row"),
        P("row", c),
        P(c),
        P(c),
        P(c, None, "row"),
        P("row", c),
        P(c),
        P(c),
        P(c, "row"),
        P("row", c),
        P(("dp", "row"), c),
    )
    out_specs = (
        P(("dp", *c), "row"),
        P(("dp", "row"), c),
        P(("dp", *c), "row"),
        P("row"),
        P("row"),
        P("row", None, c),
        P(c, "row"),
        P("row"),
        P("row"),
        P("row", c),
        P(c, "row"),
        P("row", c),
        P(c),
        P(c),
        P(c, None, "row"),
        P("row", c),
        P(c),
        P(c),
        P(c, "row"),
        P("row", c),
    )
    return jax.shard_map(
        functools.partial(per_device, data),
        mesh=split,
        in_specs=in_specs,
        out_specs=out_specs,
        check_vma=False,
    )
```

```python
import functools
import math

import jax
import jax.numpy as jnp
from jax import lax
from jax.experimental import pallas as pl
from jax.experimental.pallas import tpu as pltpu
from jax.sharding import Mesh, PartitionSpec as P

D1 = 768
D2 = 512
HD1 = 64
HD2 = 32
EPSILON = 1e-06
BLOCK = 512
LANES = 128
LOG2E = 1.4426950408889634
SWAP = [(0, 1), (1, 0)]
BF16 = jnp.bfloat16
F32 = jnp.float32


def mm(left, right):
    return jnp.dot(left, right, preferred_element_type=F32)


def mm_nt(left, right):
    return lax.dot_general(left, right, (((1,), (1,)), ((), ())), preferred_element_type=F32)


def mm_tn(left, right):
    return lax.dot_general(left, right, (((0,), (0,)), ((), ())), preferred_element_type=F32)


def head_lanes(head, head_size, rows):
    lane = lax.broadcasted_iota(jnp.int32, (rows, LANES), 1)
    return (lane >= head * head_size) & (lane < (head + 1) * head_size)


def attention_forward_kernel(head_size, q_ref, k_ref, v_ref, limit_ref, out_ref, inv_ref, aug_ref):
    tile = pl.program_id(1)
    rows = q_ref.shape[0]
    heads = LANES // head_size
    per_block = BLOCK // rows
    scale = head_size ** (-0.5) * LOG2E

    @pl.when(tile == 0)
    def _():
        aug_ref[:, :LANES] = v_ref[...]
        aug_ref[:, LANES:] = jnp.ones_like(v_ref)

    def run(block):
        queries = q_ref[...]
        limits = limit_ref[...]
        places = block * BLOCK + lax.broadcasted_iota(jnp.int32, (rows, BLOCK), 1)
        visible = places <= limits
        result = jnp.zeros((rows, LANES), F32)
        inverses = jnp.zeros((rows, LANES), F32)
        for head in range(heads):
            own = head_lanes(head, head_size, rows)
            masked = jnp.where(own, queries, jnp.zeros_like(queries))
            total = jnp.zeros((rows, 2 * LANES), F32)
            for part in range(block + 1):
                span = slice(part * BLOCK, (part + 1) * BLOCK)
                weights = jnp.exp2(mm_nt(masked, k_ref[span, :]) * scale)
                if part == block:
                    weights = jnp.where(visible, weights, 0.0)
                total = total + mm(weights.astype(BF16), aug_ref[span, :])
            inverse = 1.0 / total[:, LANES:]
            result = jnp.where(own, total[:, :LANES] * inverse, result)
            inverses = jnp.where(own, inverse, inverses)
        out_ref[...] = result.astype(BF16)
        inv_ref[...] = inverses

    for block in range(k_ref.shape[0] // BLOCK):
        pl.when(tile // per_block == block)(functools.partial(run, block))


def attention_forward(mixed, limits, head_size):
    length, width = mixed.shape[0], mixed.shape[1] // 3
    groups = width // LANES
    rows = 256
    return pl.pallas_call(
        functools.partial(attention_forward_kernel, head_size),
        out_shape=(
            jax.ShapeDtypeStruct((length, width), BF16),
            jax.ShapeDtypeStruct((length, width), F32),
        ),
        grid=(groups, length // rows),
        in_specs=[
            pl.BlockSpec((rows, LANES), lambda g, t: (t, g)),
            pl.BlockSpec((length, LANES), lambda g, t: (0, groups + g)),
            pl.BlockSpec((length, LANES), lambda g, t: (0, 2 * groups + g)),
            pl.BlockSpec((rows, 1), lambda g, t: (t, 0)),
        ],
        out_specs=[
            pl.BlockSpec((rows, LANES), lambda g, t: (t, g)),
            pl.BlockSpec((rows, LANES), lambda g, t: (t, g)),
        ],
        scratch_shapes=[pltpu.VMEM((length, 2 * LANES), BF16)],
        compiler_params=pltpu.CompilerParams(vmem_limit_bytes=24 << 20),
        cost_estimate=pl.CostEstimate(flops=int(10.5 * COST), bytes_accessed=1, transcendentals=0),
        name="attention_forward",
    )(mixed, mixed, mixed, limits)


def attention_backward_kernel(
    head_size,
    pairs,
    q_ref,
    k_ref,
    v_ref,
    att_ref,
    inv_ref,
    grad_ref,
    limit_ref,
    dq_ref,
    dk_ref,
    dv_ref,
    vaug_ref,
    naug_ref,
    dq_acc,
    dk_acc,
    dv_acc,
):
    step = pl.program_id(1)
    length = q_ref.shape[0]
    heads = LANES // head_size
    scaling = head_size ** (-0.5)

    @pl.when(step == 0)
    def _():
        lane = lax.broadcasted_iota(jnp.int32, (length, LANES), 1)
        vaug_ref[:, :LANES] = v_ref[...]
        vaug_ref[:, LANES:] = jnp.where(lane < 2, 1.0, 0.0).astype(BF16)
        scaled = grad_ref[...] * inv_ref[...]
        terms = scaled * att_ref[...].astype(F32)
        low = scaled.astype(BF16)
        for head in range(heads):
            own = head_lanes(head, head_size, length)
            total = -jnp.sum(jnp.where(own, terms, 0.0), 1, keepdims=True)
            high = total.astype(BF16).astype(F32)
            rest = total - high
            naug_ref[head, :, :LANES] = jnp.where(own, low, jnp.zeros_like(low))
            naug_ref[head, :, LANES:] = jnp.where(
                lane == 0, high, jnp.where(lane == 1, rest, 0.0)
            ).astype(BF16)
        dq_acc[...] = jnp.zeros_like(dq_acc)
        dk_acc[...] = jnp.zeros_like(dk_acc)
        dv_acc[...] = jnp.zeros_like(dv_acc)

    def run(key_block, query_block):
        keys = slice(key_block * BLOCK, (key_block + 1) * BLOCK)
        queries = slice(query_block * BLOCK, (query_block + 1) * BLOCK)
        key_rows = k_ref[keys, :]
        query_rows = q_ref[queries, :]
        key_flipped = key_rows.astype(F32).T.astype(BF16)
        if key_block == query_block:
            places = key_block * BLOCK + lax.broadcasted_iota(jnp.int32, (BLOCK, BLOCK), 0)
            visible = places <= limit_ref[:, queries]
        dq = jnp.zeros((LANES, BLOCK), F32)
        dk = jnp.zeros((BLOCK, LANES), F32)
        dv = jnp.zeros((BLOCK, LANES), F32)
        for head in range(heads):
            own = head_lanes(head, head_size, BLOCK)
            masked = jnp.where(own, query_rows, jnp.zeros_like(query_rows))
            weights = jnp.exp2(mm_nt(key_rows, masked) * (scaling * LOG2E))
            if key_block == query_block:
                weights = jnp.where(visible, weights, 0.0)
            naug = naug_ref[head, queries, :]
            slopes = mm_nt(vaug_ref[keys, :], naug)
            scores = (weights * slopes).astype(BF16)
            dv += mm(weights.astype(BF16), naug[:, :LANES])
            dk += mm(scores, masked)
            row = lax.broadcasted_iota(jnp.int32, (LANES, BLOCK), 0)
            mine = (row >= head * head_size) & (row < (head + 1) * head_size)
            dq += mm(jnp.where(mine, key_flipped, jnp.zeros_like(key_flipped)), scores)
        dq_acc[:, queries] += dq
        dk_acc[keys, :] += dk
        dv_acc[keys, :] += dv

    for number, (key_block, query_block) in enumerate(pairs):
        pl.when(step == number)(functools.partial(run, key_block, query_block))

    @pl.when(step == len(pairs) - 1)
    def _():
        dq_ref[...] = (dq_acc[...].T * scaling).astype(BF16)
        dk_ref[...] = (dk_acc[...] * scaling).astype(BF16)
        dv_ref[...] = dv_acc[...].astype(BF16)


def attention_backward(
    mixed, attended, inverse, grad, limits_row, head_size, start=0, count=None
):
    length, width = attended.shape
    groups = width // LANES
    count = groups if count is None else count
    blocks = length // BLOCK
    pairs = [(k, q) for q in range(blocks) for k in range(q + 1)]
    whole = lambda offset: pl.BlockSpec((length, LANES), lambda g, s: (0, offset + g))
    results = pl.pallas_call(
        functools.partial(attention_backward_kernel, head_size, pairs),
        out_shape=(jax.ShapeDtypeStruct((length, count * LANES), BF16),) * 3,
        grid=(count, len(pairs)),
        in_specs=[
            whole(start),
            whole(groups + start),
            whole(2 * groups + start),
            whole(start),
            whole(start),
            whole(start),
            pl.BlockSpec((1, length), lambda g, s: (0, 0)),
        ],
        out_specs=[whole(0), whole(0), whole(0)],
        scratch_shapes=[
            pltpu.VMEM((length, 2 * LANES), BF16),
            pltpu.VMEM((LANES // head_size, length, 2 * LANES), BF16),
            pltpu.VMEM((LANES, length), F32),
            pltpu.VMEM((length, LANES), F32),
            pltpu.VMEM((length, LANES), F32),
        ],
        compiler_params=pltpu.CompilerParams(vmem_limit_bytes=32 << 20),
        cost_estimate=pl.CostEstimate(
            flops=int(count * (5.2 if head_size == HD1 else 9.6) * COST), bytes_accessed=1, transcendentals=0
        ),
        name="attention_backward",
    )(mixed, mixed, mixed, attended, inverse, grad, limits_row)
    if count == 1:
        return tuple(results)
    return tuple(r[:, g * LANES : (g + 1) * LANES] for g in range(count) for r in results)


def swap(value, axis):
    return lax.ppermute(value, axis, SWAP)


def after(value, *others):
    return lax.optimization_barrier((value, *others))[0]


def near(pack):
    return (swap(pack, "row"), swap(pack, "y"))


def across_by_row(pair, *others):
    return swap(after(pair[0], *others), "y")


def across_by_y(pair, *others):
    return swap(after(pair[1], *others), "row")


def across_direct(pack):
    return lax.ppermute(pack, ("row", "y"), [(i, 3 - i) for i in range(4)])


def across_both(pair, split, *others):
    first, second = after((pair[0][:split], pair[1][split:]), *others)
    return (swap(first, "y"), swap(second, "row"))


class Parts:
    def __init__(self, refs, start=0, far=None):
        own, by_row, by_y, across = refs
        self.refs = ((own, by_y), (by_row, across))
        self.start = start
        self.far = start if far is None else far

    def rows(self, by_row, by_y, base, count, offset=0):
        start = self.far if by_row and by_y else self.start
        return self.refs[by_row][by_y][pl.ds(start + base + offset, count), :]


class Pair:
    def __init__(self, refs, split):
        own, by_row, by_y, first, second = refs
        self.first = Parts((own, by_row, by_y, first))
        self.second = Parts((own, by_row, by_y, second), split, 0)


COST = 1e7
VMEM = pl.BlockSpec(memory_space=pltpu.VMEM)
SMEM = pl.BlockSpec(memory_space=pltpu.SMEM)


def call(
    kernel, name, outs, args, scratch=(), scalars=0, limit=48, cost=1, needs=(), marks=(), fetch=False
):
    count = len(args)
    arrays = count - scalars
    if needs:
        args = (*args[:scalars], after(args[scalars], *needs), *args[scalars + 1 :])
    scratch = list(scratch)
    if fetch:
        scratch += [pltpu.VMEM(a.shape, a.dtype) for a in args[scalars:]]
        scratch.append(pltpu.SemaphoreType.DMA((arrays,)))

    def body(*refs):
        given, rest = refs[:count], refs[count + len(marks) :]
        if fetch:
            local, semaphores, rest = rest[-arrays - 1 : -1], rest[-1], rest[: -arrays - 1]
            copies = [
                pltpu.make_async_copy(source, target, semaphores.at[i])
                for i, (source, target) in enumerate(zip(given[scalars:], local))
            ]
            for copy in copies:
                copy.start()
            for copy in copies:
                copy.wait()
            given = (*given[:scalars], *local)
        kernel(*given, *rest)

    place = pl.BlockSpec(memory_space=pltpu.HBM) if fetch else VMEM
    return pl.pallas_call(
        body,
        out_shape=outs,
        in_specs=[SMEM] * scalars + [place] * arrays + [VMEM] * len(marks),
        out_specs=jax.tree.map(lambda _: VMEM, outs),
        scratch_shapes=scratch,
        compiler_params=pltpu.CompilerParams(vmem_limit_bytes=limit << 20),
        cost_estimate=pl.CostEstimate(
            flops=int(cost * COST), bytes_accessed=1, transcendentals=0
        ),
        name=name,
    )(*args, *marks)


def marker_kernel(in_ref, out_ref):
    out_ref[...] = in_ref[...]


def marker(value, cost, *others):
    return call(
        marker_kernel,
        "marker",
        jax.ShapeDtypeStruct(value.shape, value.dtype),
        (value,),
        cost=cost,
        limit=4,
        needs=others,
    )


def shaped(rows, columns, kind):
    return jax.ShapeDtypeStruct((rows, columns), kind)


def store_three(ref, base, vectors):
    for tile in range(vectors[0].shape[0]):
        values = jnp.concatenate([v[tile : tile + 1, :] for v in vectors], 0)
        high = values.astype(BF16)
        rest = values - high.astype(F32)
        middle = rest.astype(BF16)
        low = (rest - middle.astype(F32)).astype(BF16)
        ref[base + 16 * tile : base + 16 * (tile + 1), :] = jnp.concatenate(
            [high, middle, low, jnp.zeros_like(high)], 0
        )


def join_three(rows):
    wide = rows.astype(F32)
    return wide[0:4] + wide[4:8] + wide[8:12]


TILE = 256
FEED = 512


def lane_roll(values):
    return pltpu.roll(values.astype(F32), LANES // 2, 1)


HALF = LANES // 2
E_ROWS = 3 * LANES
A_LAST = 2 * E_ROWS
A_VEC = 3 * E_ROWS
A_END = A_VEC + 48
B_REST = E_ROWS
B_OUT = B_REST + E_ROWS // 2
B_END = 3 * E_ROWS
E_FEED = 18 * LANES
DA_VEC = 6 * LANES
DA_END = DA_VEC + 32
DB_PROJ = 2 * LANES
DB_END = 8 * LANES
F_COT = 8 * LANES
F_END = 12 * LANES
D_SEND = 19 * LANES + 16


def pack_mixing_kernel(w_ref, out_ref, v1, v2, v3, v4, pack_ref):
    store_three(pack_ref, A_VEC, (v1, v2, v3, v4))
    rows = w_ref.shape[1]
    pack_ref[:rows, :] = w_ref[0, :, :LANES]
    pack_ref[rows : 2 * rows, :] = w_ref[1, :, :LANES]
    pack_ref[A_LAST:A_VEC, :HALF] = w_ref[0, :, LANES:]
    pack_ref[A_LAST:A_VEC, HALF:] = w_ref[1, :, LANES:]
    pack_ref[A_END : A_END + rows, :] = w_ref[2, :, :LANES]
    rest = A_END + B_REST
    pack_ref[rest : rest + rows // 2, :HALF] = w_ref[2, : rows // 2, LANES:]
    pack_ref[rest : rest + rows // 2, HALF:] = w_ref[2, rows // 2 :, LANES:]
    heads = out_ref.shape[0]
    base = A_END + B_OUT
    for tile in range(3):
        pack_ref[base + tile * heads : base + (tile + 1) * heads, :] = out_ref[
            :, tile * LANES : (tile + 1) * LANES
        ]


def pack_encoder_kernel(up_ref, down_ref, pack_ref):
    base = 0
    for weight_ref in (up_ref, down_ref):
        rows, columns = weight_ref.shape
        for tile in range(columns // LANES):
            pack_ref[base : base + rows, :] = weight_ref[:, tile * LANES : (tile + 1) * LANES]
            base += rows


def pack_decoder_kernel(
    place_ref, mix_ref, out_ref, up_ref, down_ref, v1, v2, v3, v4, proj_ref, cot_ref, keep_ref, send_ref
):
    core = place_ref[0]
    rows = mix_ref.shape[1]
    units = up_ref.shape[1] // 2
    for target, half in ((keep_ref, core), (send_ref, 1 - core)):
        base = 0
        for i in range(3):
            target[base : base + rows, :] = mix_ref[i, :, pl.ds(half * LANES, LANES)]
            base += rows
        target[base : base + LANES, :] = out_ref[pl.ds(half * LANES, LANES), :]
        base += LANES
        for i in range(units // LANES):
            target[base : base + rows, :] = up_ref[:, pl.ds(half * units + i * LANES, LANES)]
            base += rows
        target[base : base + units, :] = down_ref[pl.ds(half * units, units), :]
        base += units
        target[base : base + 3 * LANES, :] = proj_ref[...]
        base += 3 * LANES
        target[base : base + 4 * LANES, :] = cot_ref[...]
        base += 4 * LANES
        store_three(target, base, (v1, v2, v3, v4))


def join_decoder_kernel(place_ref, keep_ref, got_ref, mix_ref, feed_ref):
    core = place_ref[0]
    rows = LANES
    for source, side in ((keep_ref, core), (got_ref, 1 - core)):
        base = 0
        for i in range(3):
            mix_ref[pl.ds(2 * i * rows + side * rows, rows), :] = source[base : base + rows, :]
            base += rows
        mix_ref[pl.ds(DA_END + side * rows, rows), :] = source[base : base + rows, :]
        base += rows
        for i in range(4):
            feed_ref[pl.ds(2 * i * rows + side * rows, rows), :] = source[base : base + rows, :]
            base += rows
        feed_ref[pl.ds(F_END + side * 4 * rows, 4 * rows), :] = source[base : base + 4 * rows, :]
        base += 4 * rows
        mix_ref[pl.ds(DA_END + DB_PROJ + side * 3 * rows, 3 * rows), :] = source[
            base : base + 3 * rows, :
        ]
        base += 3 * rows
        for start in (F_COT, F_END + F_COT):
            feed_ref[pl.ds(start + side * 2 * rows, 2 * rows), :] = source[base : base + 2 * rows, :]
            base += 2 * rows
        mix_ref[pl.ds(DA_VEC + side * 16, 16), :] = source[base : base + 16, :]


def join_input_kernel(place_ref, own, by_row, by_y, first, second, out_ref):
    y = place_ref[3]
    width = own.shape[1]
    split = second.shape[0]
    for right, by_y_side, sources in (
        (0, 0, (own, own)),
        (1, 0, (by_row, by_row)),
        (0, 1, (by_y, by_y)),
        (1, 1, (first, second)),
    ):
        base = (y if by_y_side == 0 else 1 - y) * 2 * split
        for number, source in enumerate(sources):
            start = 0 if source is second else number * first.shape[0]
            at = pl.ds(base + number * split, split)
            out_ref[at, right * width : (right + 1) * width] = source[start : start + split, :]


def norm_rows(values):
    width = values.shape[1]
    average = jnp.sum(values, 1, keepdims=True) / width
    variance = jnp.sum(values * values, 1, keepdims=True) / width - average * average
    inverse = lax.rsqrt(variance + EPSILON)
    return ((values - average) * inverse, inverse)


def first_norm_kernel(core_ref, own, other, vec_own, vec_other, x_ref, normed_ref, vec_ref):
    core = core_ref[0]
    for side, source in ((0, vec_own), (3, vec_other)):
        for tile in range(3):
            vec_ref[:, (side + tile) * LANES : (side + tile + 1) * LANES] = join_three(
                source[A_VEC + 16 * tile : A_VEC + 16 * (tile + 1), :]
            )
    rows = own.shape[0] // 2
    gain, bias = vec_ref[0:1, :], vec_ref[1:2, :]
    for source, place in ((own, core), (other, 1 - core)):
        for y in range(2):
            values = source[y * rows : (y + 1) * rows, :]
            target = pl.ds((2 * y + place) * rows, rows)
            x_ref[target, :] = values
            centred, _ = norm_rows(values.astype(F32))
            normed_ref[target, :] = (centred * gain + bias).astype(BF16)


def encoder_mixing_kernel(normed_ref, *refs):
    pair = Pair(refs[:5], A_END)
    first, second = pair.first, pair.second
    mixed_ref, weight_ref, out_ref = refs[5:8]
    out_ref[...] = encoder_out_rows(second)
    rows = E_ROWS
    low = lax.broadcasted_iota(jnp.int32, (rows, LANES), 1) < HALF
    for half in range(2):
        at = slice(half * rows, (half + 1) * rows)
        for kind, parts, base in ((0, first, 0), (1, first, rows), (2, second, 0)):
            for group, side in ((0, 0), (2, 1)):
                tile = (3 * kind + group) * LANES
                weight_ref[at, tile : tile + LANES] = parts.rows(half, side, base, rows)
        mine = first.rows(half, 0, A_LAST, rows).astype(F32)
        theirs = first.rows(half, 1, A_LAST, rows).astype(F32)
        weight_ref[at, LANES : 2 * LANES] = jnp.where(low, mine, lane_roll(theirs)).astype(BF16)
        weight_ref[at, 4 * LANES : 5 * LANES] = jnp.where(low, lane_roll(mine), theirs).astype(BF16)
        mine = second.rows(half, 0, B_REST, rows // 2).astype(F32)
        theirs = second.rows(half, 1, B_REST, rows // 2).astype(F32)
        mine = jnp.concatenate([mine, lane_roll(mine)], 0)
        theirs = jnp.concatenate([lane_roll(theirs), theirs], 0)
        weight_ref[at, 7 * LANES : 8 * LANES] = jnp.where(low, mine, theirs).astype(BF16)

    @pl.loop(0, normed_ref.shape[0] // FEED)
    def _(tile):
        at = pl.ds(tile * FEED, FEED)
        mixed_ref[at, :] = mm(normed_ref[at, :], weight_ref[...]).astype(BF16)


def encoder_out_rows(parts):
    heads = 3 * LANES // 2
    sides = [
        jnp.concatenate(
            [parts.rows(i, j, B_OUT + t * heads, heads) for i in range(2) for t in range(3)], 1
        )
        for j in range(2)
    ]
    return jnp.concatenate([sides[0], sides[1][LANES:], sides[1][:LANES]], 0)


def decoder_out_rows(parts):
    return jnp.concatenate(
        [
            jnp.concatenate(
                [parts.rows(i, j, t * LANES, LANES) for j in range(2) for t in range(2)], 1
            )
            for i in range(2)
        ],
        0,
    )


def attend_kernel(
    head_size, mixed_ref, limit_ref, weight_ref, attended_ref, inverse_ref, partial_ref, aug_ref
):
    length, width = attended_ref.shape
    groups, heads = width // LANES, LANES // head_size
    scale = head_size ** (-0.5) * LOG2E
    for group in range(groups):
        at = (2 * groups + group) * LANES
        aug_ref[group, :, :LANES] = mixed_ref[:, at : at + LANES]
        aug_ref[group, :, LANES:] = jnp.ones((length, LANES), BF16)

    for block in range(length // BLOCK):

        @pl.loop(0, BLOCK // TILE)
        def _(step):
            at = pl.ds(block * BLOCK + step * TILE, TILE)
            limits = limit_ref[at, :]
            places = block * BLOCK + lax.broadcasted_iota(jnp.int32, (TILE, BLOCK), 1)
            visible = places <= limits

            @pl.loop(0, groups)
            def _(group):
                queries = mixed_ref[at, pl.ds(group * LANES, LANES)]
                result = jnp.zeros((TILE, LANES), F32)
                inverses = jnp.zeros((TILE, LANES), F32)
                for head in range(heads):
                    own = head_lanes(head, head_size, TILE)
                    masked = jnp.where(own, queries, jnp.zeros_like(queries))
                    total = jnp.zeros((TILE, 2 * LANES), F32)
                    for part in range(block + 1):
                        span = slice(part * BLOCK, (part + 1) * BLOCK)
                        keys = mixed_ref[span, pl.ds((groups + group) * LANES, LANES)]
                        weights = jnp.exp2(mm_nt(masked, keys) * scale)
                        if part == block:
                            weights = jnp.where(visible, weights, 0.0)
                        total = total + mm(weights.astype(BF16), aug_ref[group, span, :])
                    inverse = 1.0 / total[:, LANES:]
                    result = jnp.where(own, total[:, :LANES] * inverse, result)
                    inverses = jnp.where(own, inverse, inverses)
                lanes = pl.ds(group * LANES, LANES)
                attended_ref[at, lanes] = result.astype(BF16)
                inverse_ref[at, lanes] = inverses

            partial_ref[at, :] = mm(attended_ref[at, :], weight_ref[...]).astype(BF16)


def gelu_pair(values):
    area = 0.5 * (1.0 + lax.erf(values * (0.5**0.5)))
    slope = area + values * jnp.exp2(values * values * (-0.5 * LOG2E)) * (0.5 / math.pi) ** 0.5
    return (values * area, slope)


class Feed:
    def __init__(self, up_parts, down_parts, decoder):
        self.up_parts = up_parts
        self.down_parts = down_parts
        self.decoder = decoder
        self.features = 2 * LANES if decoder else 3 * LANES
        self.units = 4 * LANES if decoder else 6 * LANES
        self.down = 0
        self.chunks = self.units // (2 * LANES)

    def rows(self, parts, feature, unit, base, count, offset):
        if self.decoder:
            return parts.rows(unit, feature, base, count, offset)
        return parts.rows(feature, unit, base, count, offset)

    def up_chunk(self, unit, chunk):
        f = self.features
        return jnp.concatenate(
            [
                jnp.concatenate(
                    [
                        self.rows(
                            self.up_parts, i, unit, 0, f, pl.multiple_of((2 * chunk + t) * f, f)
                        )
                        for t in range(2)
                    ],
                    1,
                )
                for i in range(2)
            ],
            0,
        )

    def up_both(self, chunk):
        return jnp.concatenate([self.up_chunk(unit, chunk) for unit in range(2)], 1)

    def down_both(self, chunk):
        return jnp.concatenate([self.down_chunk(unit, chunk) for unit in range(2)], 0)

    def down_chunk(self, unit, chunk):
        return jnp.concatenate(
            [
                self.rows(
                    self.down_parts,
                    i,
                    unit,
                    self.down + t * self.units,
                    2 * LANES,
                    pl.multiple_of(chunk * 2 * LANES, 2 * LANES),
                )
                for i in range(2)
                for t in range(self.features // LANES)
            ],
            1,
        )


def feed_forward_kernel(stream_ref, mine_ref, got_ref, vec_ref, *refs):
    middle_ref, normed_ref, active_ref, slope_ref, partial_ref, total_ref = refs[5:11]
    pair = Pair(refs[:5], E_FEED)
    feed = Feed(pair.first, pair.second, False)
    gain, bias = vec_ref[2:3, :], vec_ref[3:4, :]

    @pl.loop(0, stream_ref.shape[0] // FEED)
    def _(tile):
        at = pl.ds(tile * FEED, FEED)
        middle = stream_ref[at, :].astype(F32) + (
            mine_ref[at, :].astype(F32) + got_ref[at, :].astype(F32)
        )
        middle_ref[at, :] = middle
        centred, _ = norm_rows(middle)
        normed_ref[at, :] = (centred * gain + bias).astype(BF16)
        total_ref[...] = jnp.zeros_like(total_ref)

        @pl.loop(0, feed.chunks)
        def _(chunk):
            hidden = mm(normed_ref[at, :], feed.up_both(chunk))
            active, slope = gelu_pair(hidden)
            low = active.astype(BF16)
            slope = slope.astype(BF16)
            for unit in range(2):
                lanes = pl.ds(unit * feed.units + chunk * 2 * LANES, 2 * LANES)
                part = slice(unit * 2 * LANES, (unit + 1) * 2 * LANES)
                active_ref[at, lanes] = low[:, part]
                slope_ref[at, lanes] = slope[:, part]
            total_ref[...] += mm(low, feed.down_both(chunk))

        partial_ref[at, :] = total_ref[...].astype(BF16)


def decoder_feed_kernel(
    place_ref, stream_ref, mine_ref, got_ref, vec_ref, *refs
):
    middle_ref, normed_ref, active_ref, hidden_ref, partial_ref, cot_ref, total_ref = refs[4:11]
    first, second = Parts(refs[:4]), Parts(refs[:4], F_END)
    row = place_ref[2]
    for i in range(2):
        for number, parts in enumerate((first, second)):
            at = pl.ds((row if i == 0 else 1 - row) * 4 * LANES + number * 2 * LANES, 2 * LANES)
            for tile in range(4):
                cot_ref[at, tile * LANES : (tile + 1) * LANES] = parts.rows(
                    i, tile // 2, F_COT + (tile % 2) * 2 * LANES, 2 * LANES
                )
    feed = Feed(first, second, True)
    gain, bias = vec_ref[2:3, :], vec_ref[3:4, :]

    @pl.loop(0, stream_ref.shape[0] // FEED)
    def _(tile):
        at = pl.ds(tile * FEED, FEED)
        middle = stream_ref[at, :] + (mine_ref[at, :].astype(F32) + got_ref[at, :].astype(F32))
        middle_ref[at, :] = middle
        centred, _ = norm_rows(middle)
        normed_ref[at, :] = (centred * gain + bias).astype(BF16)
        total_ref[...] = jnp.zeros_like(total_ref)

        @pl.loop(0, feed.chunks)
        def _(chunk):
            upward = feed.up_both(chunk)
            hidden = mm(normed_ref[at, :], upward)
            active, slope = gelu_pair(hidden)
            active = active.astype(BF16)
            grad = mm_nt(cot_ref[at, :], feed.down_both(chunk))
            low = (grad * slope).astype(BF16)
            for unit in range(2):
                lanes = pl.ds(unit * feed.units + chunk * 2 * LANES, 2 * LANES)
                part = slice(unit * 2 * LANES, (unit + 1) * 2 * LANES)
                active_ref[at, lanes] = active[:, part]
                hidden_ref[at, lanes] = low[:, part]
            total_ref[...] += mm_nt(low, upward)

        partial_ref[at, :] = total_ref[...].astype(BF16)


def bridge_kernel(place_ref, middle_ref, mine_ref, got_ref, *refs):
    (
        out_ref, low_ref, stream_ref, normed_ref, mixed_ref, weight_ref, vec_ref, mixing_ref,
        back_ref,
    ) = refs[5:14]
    block = place_ref[1]
    pair = Pair(refs[:5], DA_END)
    first, second = pair.first, pair.second
    back_ref[...] = decoder_out_rows(second)
    rows = E_ROWS
    for j in range(2):
        for c in range(2):
            tile = (2 * j + c) * LANES
            for i in range(2):
                weight_ref[i * rows : (i + 1) * rows, tile : tile + LANES] = second.rows(
                    i, j, DB_PROJ + c * rows, rows
                )
            vec_ref[:, tile : tile + LANES] = join_three(first.rows(0, j, DA_VEC + 16 * c, 16))
    for kind in range(3):
        for i in range(2):
            tile = (2 * kind + i) * LANES
            for j in range(2):
                mixing_ref[2 * j * LANES : 2 * (j + 1) * LANES, tile : tile + LANES] = first.rows(
                    i, j, 2 * kind * LANES, 2 * LANES
                )
    gain, bias = vec_ref[0:1, :], vec_ref[1:2, :]
    width = low_ref.shape[1]

    @pl.loop(0, middle_ref.shape[0] // TILE)
    def _(tile):
        at = pl.ds(tile * TILE, TILE)
        total = middle_ref[at, :] + (mine_ref[at, :].astype(F32) + got_ref[at, :].astype(F32))
        low = total.astype(BF16)

        @pl.when(tile == block)
        def _():
            out_ref[...] = total[:, :width]

        low_ref[at, :] = low[:, :width]
        stream = mm(low, weight_ref[...])
        stream_ref[at, :] = stream
        centred, _ = norm_rows(stream)
        normed = (centred * gain + bias).astype(BF16)
        normed_ref[at, :] = normed
        mixed_ref[at, :] = mm(normed, mixing_ref[...]).astype(BF16)


def norm_back(incoming, centred, inverse, gain):
    width = incoming.shape[1]
    scaled = incoming * gain
    first = jnp.sum(scaled, 1, keepdims=True) / width
    second = jnp.sum(scaled * centred, 1, keepdims=True) / width
    return inverse * (scaled - first - centred * second)


def store_sums(sums_ref, incoming, centred):
    sums_ref[0:1, :] = jnp.sum(incoming * centred, 0, keepdims=True)
    sums_ref[1:2, :] = jnp.sum(incoming, 0, keepdims=True)


def own_sums(place_ref, tile, sums_ref, incoming, centred):
    half = TILE // 2

    @pl.when((tile == place_ref[1]) & (place_ref[2] == 0))
    def _():
        store_sums(sums_ref, incoming[:half], centred[:half])

    @pl.when((tile == place_ref[1]) & (place_ref[2] == 1))
    def _():
        store_sums(sums_ref, incoming[half:], centred[half:])


def middle_back_kernel(
    place_ref, mine_ref, got_ref, middle_ref, grad_ref, vec_ref, weight_ref,
    total_ref, low_ref, attended_ref, sums_ref,
):
    gain = vec_ref[2:3, :]
    width = low_ref.shape[1]

    @pl.loop(0, middle_ref.shape[0] // TILE)
    def _(tile):
        at = pl.ds(tile * TILE, TILE)
        incoming = mine_ref[at, :].astype(F32) + got_ref[at, :].astype(F32)
        centred, inverse = norm_rows(middle_ref[at, :])
        total = grad_ref[at, :].astype(F32) + norm_back(incoming, centred, inverse, gain)
        total_ref[at, :] = total
        low = total.astype(BF16)
        low_ref[at, :] = low[:, :width]
        attended_ref[at, :] = mm_nt(low, weight_ref[...])
        own_sums(place_ref, tile, sums_ref, incoming, centred)


def mixed_low(refs, at):
    kinds = len(refs) // 3
    return jnp.concatenate([refs[3 * g + i][at, :] for i in range(3) for g in range(kinds)], 1)


def mixed_back_kernel(*refs):
    lows, weight_ref, partial_ref = refs[:-2], refs[-2], refs[-1]

    @pl.loop(0, partial_ref.shape[0] // FEED)
    def _(tile):
        at = pl.ds(tile * FEED, FEED)
        partial_ref[at, :] = mm_nt(mixed_low(lows, at), weight_ref[...]).astype(BF16)


def mixed_last_kernel(place_ref, *refs):
    core, y = place_ref[0], place_ref[3]
    lows, weight_ref, keep_ref, send_ref = refs[:-3], refs[-3], refs[-2], refs[-1]
    for target, side in ((keep_ref, core), (send_ref, 1 - core)):
        at = pl.ds((2 * y + side) * TILE, TILE)
        target[...] = mm_nt(mixed_low(lows, at), weight_ref[...]).astype(BF16)


def bridge_back_kernel(
    place_ref, mine_ref, got_ref, stream_ref, grad_ref, vec_ref, proj_ref,
    low_ref, encoder_ref, down_ref, sums_ref,
):
    gain = vec_ref[0:1, :]

    @pl.loop(0, stream_ref.shape[0] // TILE)
    def _(tile):
        at = pl.ds(tile * TILE, TILE)
        incoming = mine_ref[at, :].astype(F32) + got_ref[at, :].astype(F32)
        centred, inverse = norm_rows(stream_ref[at, :])
        grad = grad_ref[at, :] + norm_back(incoming, centred, inverse, gain)
        own_sums(place_ref, tile, sums_ref, incoming, centred)
        low = grad.astype(BF16)
        low_ref[at, :] = low
        encoder = mm_nt(low, proj_ref[...])
        encoder_ref[at, :] = encoder
        down_ref[at, :] = encoder.astype(BF16)


def feed_back_kernel(down_ref, slope_ref, *refs):
    hidden_ref, partial_ref, total_ref = refs[5:8]
    pair = Pair(refs[:5], E_FEED)
    feed = Feed(pair.first, pair.second, False)

    @pl.loop(0, down_ref.shape[0] // FEED)
    def _(tile):
        at = pl.ds(tile * FEED, FEED)
        total_ref[...] = jnp.zeros_like(total_ref)

        @pl.loop(0, feed.chunks)
        def _(chunk):
            back = mm_nt(down_ref[at, :], feed.down_both(chunk))
            parts = []
            for unit in range(2):
                lanes = pl.ds(unit * feed.units + chunk * 2 * LANES, 2 * LANES)
                part = slice(unit * 2 * LANES, (unit + 1) * 2 * LANES)
                hidden = (back[:, part] * slope_ref[at, lanes].astype(F32)).astype(BF16)
                hidden_ref[at, lanes] = hidden
                parts.append(hidden)
            total_ref[...] += mm_nt(jnp.concatenate(parts, 1), feed.up_both(chunk))

        partial_ref[at, :] = total_ref[...].astype(BF16)


def input_back_kernel(place_ref, mine_ref, got_ref, x_ref, grad_ref, vec_ref, out_ref, sums_ref):
    at = pl.ds(place_ref[1] * TILE, TILE)
    incoming = mine_ref[...].astype(F32) + got_ref[...].astype(F32)
    centred, inverse = norm_rows(x_ref[at, :].astype(F32))
    total = grad_ref[at, :] + norm_back(incoming, centred, inverse, vec_ref[0:1, :])
    out_ref[...] = total[:, : out_ref.shape[1]]
    own_sums(place_ref, place_ref[1], sums_ref, incoming, centred)


def store_tiles(ref, base, value):
    rows = value.shape[0]
    for tile in range(value.shape[1] // LANES):
        ref[base + tile * rows : base + (tile + 1) * rows, :] = value[
            :, tile * LANES : (tile + 1) * LANES
        ].astype(BF16)


G_LAST = 3 * E_ROWS
G_REST = 4 * E_ROWS
G_OUT = G_REST + E_ROWS // 2
G_END = 6 * E_ROWS
GA_UP = 8 * LANES
GA_END = 16 * LANES
GB_OUT = 6 * LANES
GB_PROJ = 8 * LANES
GB_END = 11 * LANES


def feed_grads_kernel(active_ref, cot_ref, normed_ref, hidden_ref, pack_ref):
    units, features = 4 * LANES, 2 * LANES
    store_tiles(pack_ref, 0, mm_tn(active_ref[:, :units], cot_ref[:, :features]))
    store_tiles(pack_ref, GA_UP, mm_tn(normed_ref[:, :features], hidden_ref[:, :units]))


def mixing_grads_kernel(
    place_ref, normed_ref, q_ref, k_ref, v_ref, attended_ref, middle_ref, encoder_ref, proj_ref, pack_ref
):
    lows = jnp.concatenate([q_ref[:, :LANES], k_ref[:, :LANES], v_ref[:, :LANES]], 1)
    store_tiles(pack_ref, 0, mm_tn(normed_ref[:, : 2 * LANES], lows))
    store_tiles(pack_ref, GB_OUT, mm_tn(attended_ref[:, :LANES], middle_ref[...]))
    own = proj_ref[:, pl.ds(place_ref[0] * LANES, LANES)]
    store_tiles(pack_ref, GB_PROJ, mm_tn(encoder_ref[...], own))


def product_kernel(left_ref, right_ref, out_ref):
    rows, columns = out_ref.shape
    out_ref[...] = mm_tn(left_ref[:, :rows], right_ref[:, :columns]).astype(BF16)


def encoder_grads_kernel(
    normed_ref, q_ref, k_ref, v_ref, q2_ref, k2_ref, v2_ref, attended_ref, middle_ref, pack_ref
):
    low = lax.broadcasted_iota(jnp.int32, q2_ref.shape, 1) < HALF
    last = jnp.where(low, q2_ref[...].astype(F32), lane_roll(k2_ref[...])).astype(BF16)
    lows = jnp.concatenate([q_ref[...], k_ref[...], v_ref[...], last, v2_ref[...]], 1)
    grads = mm_tn(normed_ref[:, :E_ROWS], lows)
    store_tiles(pack_ref, 0, grads[:, : 4 * LANES])
    rest = grads[:, 4 * LANES :]
    half = E_ROWS // 2
    low = lax.broadcasted_iota(jnp.int32, (half, LANES), 1) < HALF
    pack_ref[G_REST:G_OUT, :] = jnp.where(low, rest[:half], lane_roll(rest[half:])).astype(BF16)
    grads = mm_tn(attended_ref[:, : 2 * LANES], middle_ref[...])
    store_tiles(pack_ref, G_OUT, grads[:half])


def encoder_unpack_kernel(pack_ref, mixing_ref, out_ref):
    rows, half = E_ROWS, E_ROWS // 2
    for kind in range(3):
        mixing_ref[kind, :, :LANES] = pack_ref[kind * rows : (kind + 1) * rows, :].astype(F32)
    last = pack_ref[G_LAST:G_REST, :].astype(F32)
    mixing_ref[0, :, LANES:] = last[:, :HALF]
    mixing_ref[1, :, LANES:] = last[:, HALF:]
    rest = pack_ref[G_REST:G_OUT, :].astype(F32)
    mixing_ref[2, :half, LANES:] = rest[:, :HALF]
    mixing_ref[2, half:, LANES:] = rest[:, HALF:]
    for tile in range(3):
        at = slice(G_OUT + tile * half, G_OUT + (tile + 1) * half)
        out_ref[:, tile * LANES : (tile + 1) * LANES] = pack_ref[at, :].astype(F32)


def decoder_send_kernel(place_ref, feed_ref, mix_ref, send_ref):
    other = 1 - place_ref[0]
    rows = LANES
    send_ref[: 4 * rows, :] = feed_ref[pl.ds(other * 4 * rows, 4 * rows), :]
    for tile in range(4):
        send_ref[(4 + tile) * rows : (5 + tile) * rows, :] = feed_ref[
            pl.ds(GA_UP + 2 * tile * rows + other * rows, rows), :
        ]
    for tile in range(3):
        send_ref[(8 + tile) * rows : (9 + tile) * rows, :] = mix_ref[
            pl.ds(2 * tile * rows + other * rows, rows), :
        ]
    send_ref[11 * rows : 12 * rows, :] = mix_ref[pl.ds(GB_OUT + other * rows, rows), :]


def decoder_unpack_kernel(
    place_ref, feed_ref, mix_ref, got_ref, mixing_ref, out_ref, up_ref, down_ref, proj_ref
):
    core = place_ref[0]
    rows = LANES
    units = 4 * rows
    down_ref[pl.ds(core * units, units), :] = feed_ref[pl.ds(core * units, units), :].astype(F32)
    down_ref[pl.ds((1 - core) * units, units), :] = got_ref[:units, :].astype(F32)
    for tile in range(4):
        up_ref[:, pl.ds(core * units + tile * rows, rows)] = feed_ref[
            pl.ds(GA_UP + 2 * tile * rows + core * rows, rows), :
        ].astype(F32)
        up_ref[:, pl.ds((1 - core) * units + tile * rows, rows)] = got_ref[
            (4 + tile) * rows : (5 + tile) * rows, :
        ].astype(F32)
    for tile in range(3):
        mixing_ref[tile, :, pl.ds(core * rows, rows)] = mix_ref[
            pl.ds(2 * tile * rows + core * rows, rows), :
        ].astype(F32)
        mixing_ref[tile, :, pl.ds((1 - core) * rows, rows)] = got_ref[
            (8 + tile) * rows : (9 + tile) * rows, :
        ].astype(F32)
    out_ref[pl.ds(core * rows, rows), :] = mix_ref[pl.ds(GB_OUT + core * rows, rows), :].astype(F32)
    out_ref[pl.ds((1 - core) * rows, rows), :] = got_ref[11 * rows : 12 * rows, :].astype(F32)
    proj_ref[...] = mix_ref[GB_PROJ:GB_END, :].astype(F32)


def line_first(value, size):
    if size == 4:
        return (value, lax.ppermute(value, "dp", [(0, 1), (3, 2)]))
    if size & (size - 1):
        return lax.psum(value, "dp")
    distance = 1
    while distance < size:
        got = lax.ppermute(value, "dp", [(i, i ^ distance) for i in range(size)])
        value = (value.astype(F32) + got.astype(F32)).astype(BF16)
        distance *= 2
    return value


def line_next(state, size, pairs, *others):
    if size != 4:
        return state
    mine, got = after(state, *others)
    total = (mine.astype(F32) + got.astype(F32)).astype(BF16)
    return (total, lax.ppermute(total, "dp", pairs))


def line_across(state, size, *others):
    return line_next(state, size, [(1, 2), (2, 1)], *others)


def line_back(state, size, *others):
    return line_next(state, size, [(1, 0), (2, 3)], *others)


def line_last(state, size, *others):
    if size != 4:
        return state
    mine, got = after(state, *others)
    place = lax.axis_index("dp")
    return jnp.where((place == 0) | (place == 3), got, mine)


def dp_sum(value, size):
    place = lax.axis_index("dp")
    terms = [value] + [
        lax.ppermute(value, "dp", [(i, (i + step) % size) for i in range(size)])
        for step in range(1, size)
    ]
    terms = terms[::-1]
    return jnp.sum(lax.dynamic_slice_in_dim(jnp.stack(terms + terms), size - 1 - place, size, 0), 0)


def per_device(
    data_size,
    block_input,
    span_end,
    encoder_attention_gain,
    encoder_attention_bias,
    encoder_query_key_value,
    encoder_output_weight,
    encoder_feedforward_gain,
    encoder_feedforward_bias,
    encoder_up_weight,
    encoder_down_weight,
    projection,
    decoder_attention_gain,
    decoder_attention_bias,
    decoder_query_key_value,
    decoder_output_weight,
    decoder_feedforward_gain,
    decoder_feedforward_bias,
    decoder_up_weight,
    decoder_down_weight,
    output_cotangent,
):
    row = lax.axis_index("row").astype(jnp.int32)
    y = lax.axis_index("y").astype(jnp.int32)
    core = lax.axis_index("core").astype(jnp.int32)
    length = span_end.shape[0]
    own_rows, width = block_input.shape
    block = 2 * y + core
    place = jnp.stack([core, block, row, y])
    limits = span_end.reshape(length, 1)
    limits_row = span_end.reshape(1, length)
    full = 2 * width
    low_full = 4 * LANES
    units = 2 * encoder_up_weight.shape[1]
    d_units = decoder_up_weight.shape[1]
    features = 2 * LANES

    half = own_rows // 2
    x_near = near(block_input)
    tick = jnp.zeros((8, LANES), F32)
    row_of = lambda vector: vector.reshape(-1, LANES)
    keep, send = call(
        pack_decoder_kernel,
        "pack_decoder",
        (shaped(D_SEND, LANES, BF16),) * 2,
        (
            place,
            jnp.transpose(decoder_query_key_value, (1, 0, 2)),
            decoder_output_weight,
            decoder_up_weight,
            decoder_down_weight,
            row_of(decoder_attention_gain),
            row_of(decoder_attention_bias),
            row_of(decoder_feedforward_gain),
            row_of(decoder_feedforward_bias),
            projection,
            output_cotangent,
        ),
        scalars=1,
        limit=56,
        fetch=True,
    )
    m_pack = call(
        pack_mixing_kernel,
        "pack_mixing",
        shaped(A_END + B_END, LANES, BF16),
        (
            jnp.transpose(encoder_query_key_value, (1, 0, 2)),
            encoder_output_weight,
            row_of(encoder_attention_gain),
            row_of(encoder_attention_bias),
            row_of(encoder_feedforward_gain),
            row_of(encoder_feedforward_bias),
        ),
        limit=56,
        fetch=True,
        needs=(x_near, keep),
    )
    m_near = near(m_pack)
    d_got = swap(send, "core")
    dm_pack, f_pack = call(
        join_decoder_kernel,
        "join_decoder",
        (shaped(DA_END + DB_END, LANES, BF16), shaped(2 * F_END, LANES, BF16)),
        (place, keep, d_got),
        scalars=1,
        limit=8,
    )
    e_pack = call(
        pack_encoder_kernel,
        "pack_encoder",
        shaped(2 * E_FEED, LANES, BF16),
        (encoder_up_weight, encoder_down_weight),
        limit=56,
        fetch=True,
    )
    x_far = across_both(x_near, half, e_pack, dm_pack)
    m_far = across_both(m_near, A_END, x_far)
    sides = call(
        join_input_kernel,
        "join_input",
        shaped(2 * own_rows, full, BF16),
        (place, block_input, *x_near, *x_far),
        scalars=1,
        limit=56,
        fetch=True,
        needs=(m_near,),
    )
    m_parts = (m_pack, *m_near, *m_far)
    e_near = near(after(e_pack, sides))
    dm_near = near(after(dm_pack, sides))
    mark = marker(tick, 5000, m_far)
    stream, normed_first, e_vec = call(
        first_norm_kernel,
        "first_norm",
        (shaped(length, full, BF16), shaped(length, full, BF16), shaped(4, full, F32)),
        (place, sides, swap(sides, "core"), m_pack, m_near[0]),
        scalars=1,
        limit=8,
        marks=(mark,),
    )
    mixed, e_mixing, e_out = call(
        encoder_mixing_kernel,
        "encoder_mixing",
        (
            shaped(length, 9 * LANES, BF16),
            shaped(full, 9 * LANES, BF16),
            shaped(E_ROWS, full, BF16),
        ),
        (normed_first, *m_parts),
        limit=12,
        cost=3,
    )
    attended, inverse, partial = call(
        functools.partial(attend_kernel, HD1),
        "encoder_attend",
        (
            shaped(length, E_ROWS, BF16),
            shaped(length, E_ROWS, F32),
            shaped(length, full, BF16),
        ),
        (mixed, limits, e_out),
        (pltpu.VMEM((3, length, 2 * LANES), BF16),),
        limit=16,
        cost=12,
    )
    got = swap(partial, "core")
    e_far = across_both(e_near, E_FEED, attended, dm_near)
    e_parts = (e_pack, *e_near, *e_far)
    dm_far = across_both(dm_near, DA_END, attended)
    f_go = after(f_pack, e_far)
    f_parts = (f_pack, *near(f_go), across_direct(f_go))
    mark = marker(tick, 10000, e_far)
    middle, normed_second, active, slope, partial = call(
        feed_forward_kernel,
        "feed_forward",
        (
            shaped(length, full, F32),
            shaped(length, full, BF16),
            shaped(length, units, BF16),
            shaped(length, units, BF16),
            shaped(length, full, BF16),
        ),
        (stream, partial, got, e_vec, *e_parts),
        (pltpu.VMEM((FEED, full), F32),),
        limit=16,
        cost=12,
        marks=(mark,),
    )
    mark = marker(tick, 10000, middle)
    (
        own_encoder_out, encoder_low, d_stream, d_normed_first, d_mixed, proj_weight, d_vec, d_mixing,
        d_out,
    ) = call(
        bridge_kernel,
        "bridge",
        (
            shaped(own_rows, width, F32),
            shaped(length, width, BF16),
            shaped(length, low_full, F32),
            shaped(length, low_full, BF16),
            shaped(length, 6 * LANES, BF16),
            shaped(full, low_full, BF16),
            shaped(4, low_full, F32),
            shaped(low_full, 6 * LANES, BF16),
            shaped(2 * LANES, low_full, BF16),
        ),
        (place, middle, partial, swap(partial, "core"), dm_pack, *dm_near, *dm_far),
        scalars=1,
        limit=12,
        marks=(mark,),
        cost=5.7,
    )

    d_attended, d_inverse, partial = call(
        functools.partial(attend_kernel, HD2),
        "decoder_attend",
        (
            shaped(length, 2 * LANES, BF16),
            shaped(length, 2 * LANES, F32),
            shaped(length, low_full, BF16),
        ),
        (d_mixed, limits, d_out),
        (pltpu.VMEM((2, length, 2 * LANES), BF16),),
        limit=16,
        cost=11,
    )
    mark = marker(tick, 10000, partial)
    d_middle, d_normed_second, d_active, d_hidden, partial, cotangent = call(
        decoder_feed_kernel,
        "decoder_feed",
        (
            shaped(length, low_full, F32),
            shaped(length, low_full, BF16),
            shaped(length, d_units, BF16),
            shaped(length, d_units, BF16),
            shaped(length, low_full, BF16),
            shaped(length, low_full, BF16),
        ),
        (place, d_stream, partial, swap(partial, "core"), d_vec, *f_parts),
        (pltpu.VMEM((FEED, low_full), F32),),
        scalars=1,
        limit=16,
        marks=(mark,),
        cost=8,
    )

    got = swap(partial, "core")
    grads_a = call(
        feed_grads_kernel,
        "decoder_feed_grads",
        shaped(GA_END, LANES, BF16),
        (after(d_active, partial), cotangent, d_normed_second, d_hidden),
        limit=8,
        cost=0.8,
    )
    sum_a = line_first(grads_a, data_size)
    d_middle_grad, d_middle_low, attended_grad, d_second_sums = call(
        middle_back_kernel,
        "decoder_middle_back",
        (
            shaped(length, low_full, F32),
            shaped(length, features, BF16),
            shaped(length, 2 * LANES, F32),
            shaped(2, low_full, F32),
        ),
        (place, after(partial, grads_a), got, d_middle, cotangent, d_vec, d_out),
        scalars=1,
        limit=12,
        cost=2.6,
    )
    d_lows = attention_backward(
        d_mixed, d_attended, d_inverse, attended_grad, limits_row, HD2, 0, 1
    )
    sum_a = line_across(sum_a, data_size, d_lows)
    d_lows = d_lows + attention_backward(
        d_mixed, d_attended, d_inverse, after(attended_grad, sum_a[0]), limits_row, HD2, 1, 1
    )
    sum_a = line_back(sum_a, data_size, d_lows)
    partial = call(
        mixed_back_kernel,
        "decoder_mixed_back",
        shaped(length, low_full, BF16),
        (after(d_lows[0], sum_a[0]), *d_lows[1:], d_mixing),
        limit=12,
        cost=1.6,
    )
    got = swap(partial, "core")

    proj_low, encoder_grad, down_low, d_first_sums = call(
        bridge_back_kernel,
        "bridge_back",
        (
            shaped(length, low_full, BF16),
            shaped(length, full, F32),
            shaped(length, full, BF16),
            shaped(2, low_full, F32),
        ),
        (place, partial, got, d_stream, d_middle_grad, d_vec, proj_weight),
        scalars=1,
        limit=12,
        cost=3.9,
    )
    grads_c = call(
        product_kernel,
        "encoder_down_grads",
        shaped(units // 2, width, BF16),
        (active, down_low),
        limit=8,
        cost=1,
    )
    sum_c = line_first(grads_c, data_size)
    grads_b = call(
        mixing_grads_kernel,
        "decoder_mixing_grads",
        shaped(GB_END, LANES, BF16),
        (
            place, d_normed_first, *d_lows[:3], d_attended, d_middle_low, encoder_low,
            after(proj_low, grads_c),
        ),
        scalars=1,
        limit=8,
        cost=1.3,
    )
    sum_b = line_first(grads_b, data_size)
    hidden_low, partial = call(
        feed_back_kernel,
        "feed_back",
        (shaped(length, units, BF16), shaped(length, full, BF16)),
        (after(down_low, grads_b), slope, *e_parts),
        (pltpu.VMEM((FEED, full), F32),),
        limit=16,
        cost=12,
    )
    got = swap(partial, "core")
    sum_c = line_across(sum_c, data_size, partial)
    grads_e = call(
        product_kernel,
        "encoder_up_grads",
        shaped(width, units // 2, BF16),
        (normed_second, after(hidden_low, sum_c[0])),
        limit=8,
        cost=1000,
    )
    sum_e = line_first(grads_e, data_size)
    middle_grad, middle_low, attended_grad, second_sums = call(
        middle_back_kernel,
        "encoder_middle_back",
        (
            shaped(length, full, F32),
            shaped(length, width, BF16),
            shaped(length, 3 * LANES, F32),
            shaped(2, full, F32),
        ),
        (place, after(partial, grads_e), got, middle, encoder_grad, e_vec, e_out),
        scalars=1,
        limit=12,
        cost=5.5,
    )
    first = attention_backward(
        mixed, attended, inverse, attended_grad, limits_row, HD1, 0, 1
    )
    sum_c = line_back(sum_c, data_size, first)
    sum_b = line_across(sum_b, data_size, first)
    sum_e = line_across(sum_e, data_size, first)
    second = attention_backward(
        mixed,
        attended,
        inverse,
        after(attended_grad, sum_c[0], sum_b[0], sum_e[0], sum_a),
        limits_row,
        HD1,
        1,
        1,
    )
    grads_d = call(
        encoder_grads_kernel,
        "encoder_mixing_grads",
        shaped(G_END, LANES, BF16),
        (normed_first, *first, *second, attended, middle_low),
        limit=12,
        cost=1.1,
    )
    sum_d = line_first(grads_d, data_size)
    sum_e = line_back(sum_e, data_size, grads_d)
    third = attention_backward(
        mixed, attended, inverse, after(attended_grad, grads_d, sum_c, sum_e[0]), limits_row, HD1, 2, 1
    )
    sum_d = line_across(sum_d, data_size, third)
    lows = (*first, *second, after(third[0], sum_d[0]), *third[1:])
    keep, send = call(
        mixed_last_kernel,
        "encoder_mixed_back",
        (shaped(own_rows, full, BF16),) * 2,
        (place, *lows, e_mixing),
        scalars=1,
        limit=12,
        cost=1.8,
    )
    got = swap(send, "core")
    sum_b = line_back(sum_b, data_size, send)
    own_input_grad, first_sums = call(
        input_back_kernel,
        "input_back",
        (shaped(own_rows, width, F32), shaped(2, full, F32)),
        (place, after(keep, sum_b[0]), got, stream, middle_grad, e_vec),
        scalars=1,
        limit=8,
        cost=1.8,
    )

    def in_order(value, index):
        half = value.shape[1] // 2
        return jnp.where(index == 0, value, jnp.concatenate([value[:, half:], value[:, :half]], 1))

    e_sums = in_order(jnp.concatenate([first_sums, second_sums], 0), row)
    d_sums = in_order(jnp.concatenate([d_first_sums, d_second_sums], 0), y)
    sums = jnp.concatenate([e_sums, jnp.pad(d_sums, ((0, 0), (0, full - low_full)))], 0)
    sums = jnp.sum(lax.all_gather(sums, ("row", "y", "core")), 0)
    sum_d = line_back(sum_d, data_size, sums)
    sums = dp_sum(after(sums, sum_d[0]), data_size)
    e_sums = lax.dynamic_slice_in_dim(sums[:4], row * width, width, 1)
    share = decoder_attention_gain.shape[0]
    d_sums = lax.dynamic_slice_in_dim(sums[4:], block * share, share, 1)

    own, by_row = after(f_parts[:2], sum_d[0])
    out_rows, out_columns = output_cotangent.shape
    active_rows = lax.dynamic_slice_in_dim(d_active, row * out_rows, out_rows, 0)
    half = d_units // 2
    span = F_END + half
    down = jnp.concatenate(
        [jnp.concatenate([p[F_END:span], p[span : span + half]], 1) for p in (own, by_row)], 0
    )
    last = mm(active_rows, down)
    mine = lax.dynamic_slice_in_dim(last, core * out_columns, out_columns, 1)
    others = lax.dynamic_slice_in_dim(last, (1 - core) * out_columns, out_columns, 1)
    own_decoder_out = (
        lax.dynamic_slice(d_middle, (row * out_rows, core * out_columns), (out_rows, out_columns))
        + mine
        + swap(others.astype(BF16), "core").astype(F32)
    )

    grads_a = line_last(sum_a, data_size, own_input_grad)
    grads_b = line_last(sum_b, data_size, sum_d[0])
    send = call(
        decoder_send_kernel,
        "decoder_send",
        shaped(12 * LANES, LANES, BF16),
        (place, grads_a, grads_b),
        scalars=1,
        limit=8,
    )
    d_mixing_grad, d_out_grad, d_up_grad, d_down_grad, proj_grad = call(
        decoder_unpack_kernel,
        "decoder_unpack",
        (
            jax.ShapeDtypeStruct((3, LANES, 2 * LANES), F32),
            shaped(2 * LANES, LANES, F32),
            shaped(LANES, d_units, F32),
            shaped(d_units, LANES, F32),
            shaped(width, LANES, F32),
        ),
        (place, grads_a, grads_b, swap(send, "core")),
        scalars=1,
        limit=8,
        cost=1.9,
    )
    grads_c = line_last(sum_c, data_size, sum_d[0]).astype(F32)
    grads_e = line_last(sum_e, data_size, sum_d[0]).astype(F32)
    grads_d = line_last(sum_d, data_size, d_down_grad, grads_c, grads_e)
    mixing_grad, out_grad = call(
        encoder_unpack_kernel,
        "encoder_unpack",
        (
            jax.ShapeDtypeStruct((3, width, width // 2), F32),
            shaped(width // 2, width, F32),
        ),
        (grads_d,),
        limit=8,
    )
    return (
        own_encoder_out,
        own_decoder_out,
        own_input_grad,
        e_sums[0],
        e_sums[1],
        jnp.transpose(mixing_grad, (1, 0, 2)),
        out_grad,
        e_sums[2],
        e_sums[3],
        grads_e,
        grads_c,
        proj_grad,
        d_sums[0],
        d_sums[1],
        jnp.transpose(d_mixing_grad, (1, 0, 2)),
        d_out_grad,
        d_sums[2],
        d_sums[3],
        d_up_grad,
        d_down_grad,
    )


def solution(mesh):
    data, row, col = (mesh.shape[name] for name in ("dp", "row", "col"))
    split = Mesh(mesh.devices.reshape(data, row, col // 2, 2), ("dp", "row", "y", "core"))
    c = ("y", "core")
    in_specs = (
        P(("dp", *c), "row"),
        P("dp"),
        P("row"),
        P("row"),
        P("row", None, c),
        P(c, "row"),
        P("row"),
        P("row"),
        P("row", c),
        P(c, "row"),
        P("row", c),
        P(c),
        P(c),
        P(c, None, "row"),
        P("row", c),
        P(c),
        P(c),
        P(c, "row"),
        P("row", c),
        P(("dp", "row"), c),
    )
    out_specs = (
        P(("dp", *c), "row"),
        P(("dp", "row"), c),
        P(("dp", *c), "row"),
        P("row"),
        P("row"),
        P("row", None, c),
        P(c, "row"),
        P("row"),
        P("row"),
        P("row", c),
        P(c, "row"),
        P("row", c),
        P(c),
        P(c),
        P(c, None, "row"),
        P("row", c),
        P(c),
        P(c),
        P(c, "row"),
        P("row", c),
    )
    return jax.shard_map(
        functools.partial(per_device, data),
        mesh=split,
        in_specs=in_specs,
        out_specs=out_specs,
        check_vma=False,
    )
```

```python
import functools
import math

import jax
import jax.numpy as jnp
from jax import lax
from jax.experimental import pallas as pl
from jax.experimental.pallas import tpu as pltpu
from jax.sharding import Mesh, PartitionSpec as P

D1 = 768
D2 = 512
HD1 = 64
HD2 = 32
EPSILON = 1e-06
BLOCK = 512
LANES = 128
LOG2E = 1.4426950408889634
SWAP = [(0, 1), (1, 0)]
BF16 = jnp.bfloat16
F32 = jnp.float32


def mm(left, right):
    return jnp.dot(left, right, preferred_element_type=F32)


def mm_nt(left, right):
    return lax.dot_general(left, right, (((1,), (1,)), ((), ())), preferred_element_type=F32)


def mm_tn(left, right):
    return lax.dot_general(left, right, (((0,), (0,)), ((), ())), preferred_element_type=F32)


def head_lanes(head, head_size, rows):
    lane = lax.broadcasted_iota(jnp.int32, (rows, LANES), 1)
    return (lane >= head * head_size) & (lane < (head + 1) * head_size)


def attention_forward_kernel(head_size, q_ref, k_ref, v_ref, limit_ref, out_ref, inv_ref, aug_ref):
    tile = pl.program_id(1)
    rows = q_ref.shape[0]
    heads = LANES // head_size
    per_block = BLOCK // rows
    scale = head_size ** (-0.5) * LOG2E

    @pl.when(tile == 0)
    def _():
        aug_ref[:, :LANES] = v_ref[...]
        aug_ref[:, LANES:] = jnp.ones_like(v_ref)

    def run(block):
        queries = q_ref[...]
        limits = limit_ref[...]
        places = block * BLOCK + lax.broadcasted_iota(jnp.int32, (rows, BLOCK), 1)
        visible = places <= limits
        result = jnp.zeros((rows, LANES), F32)
        inverses = jnp.zeros((rows, LANES), F32)
        for head in range(heads):
            own = head_lanes(head, head_size, rows)
            masked = jnp.where(own, queries, jnp.zeros_like(queries))
            total = jnp.zeros((rows, 2 * LANES), F32)
            for part in range(block + 1):
                span = slice(part * BLOCK, (part + 1) * BLOCK)
                weights = jnp.exp2(mm_nt(masked, k_ref[span, :]) * scale)
                if part == block:
                    weights = jnp.where(visible, weights, 0.0)
                total = total + mm(weights.astype(BF16), aug_ref[span, :])
            inverse = 1.0 / total[:, LANES:]
            result = jnp.where(own, total[:, :LANES] * inverse, result)
            inverses = jnp.where(own, inverse, inverses)
        out_ref[...] = result.astype(BF16)
        inv_ref[...] = inverses

    for block in range(k_ref.shape[0] // BLOCK):
        pl.when(tile // per_block == block)(functools.partial(run, block))


def attention_forward(mixed, limits, head_size):
    length, width = mixed.shape[0], mixed.shape[1] // 3
    groups = width // LANES
    rows = 256
    return pl.pallas_call(
        functools.partial(attention_forward_kernel, head_size),
        out_shape=(
            jax.ShapeDtypeStruct((length, width), BF16),
            jax.ShapeDtypeStruct((length, width), F32),
        ),
        grid=(groups, length // rows),
        in_specs=[
            pl.BlockSpec((rows, LANES), lambda g, t: (t, g)),
            pl.BlockSpec((length, LANES), lambda g, t: (0, groups + g)),
            pl.BlockSpec((length, LANES), lambda g, t: (0, 2 * groups + g)),
            pl.BlockSpec((rows, 1), lambda g, t: (t, 0)),
        ],
        out_specs=[
            pl.BlockSpec((rows, LANES), lambda g, t: (t, g)),
            pl.BlockSpec((rows, LANES), lambda g, t: (t, g)),
        ],
        scratch_shapes=[pltpu.VMEM((length, 2 * LANES), BF16)],
        compiler_params=pltpu.CompilerParams(vmem_limit_bytes=24 << 20),
        cost_estimate=pl.CostEstimate(flops=int(10.5 * COST), bytes_accessed=1, transcendentals=0),
        name="attention_forward",
    )(mixed, mixed, mixed, limits)


def attention_backward_kernel(
    head_size,
    pairs,
    q_ref,
    k_ref,
    v_ref,
    att_ref,
    inv_ref,
    grad_ref,
    limit_ref,
    dq_ref,
    dk_ref,
    dv_ref,
    vaug_ref,
    naug_ref,
    dq_acc,
    dk_acc,
    dv_acc,
):
    step = pl.program_id(1)
    length = q_ref.shape[0]
    heads = LANES // head_size
    scaling = head_size ** (-0.5)

    @pl.when(step == 0)
    def _():
        lane = lax.broadcasted_iota(jnp.int32, (length, LANES), 1)
        vaug_ref[:, :LANES] = v_ref[...]
        vaug_ref[:, LANES:] = jnp.where(lane < 2, 1.0, 0.0).astype(BF16)
        scaled = grad_ref[...] * inv_ref[...]
        terms = scaled * att_ref[...].astype(F32)
        low = scaled.astype(BF16)
        for head in range(heads):
            own = head_lanes(head, head_size, length)
            total = -jnp.sum(jnp.where(own, terms, 0.0), 1, keepdims=True)
            high = total.astype(BF16).astype(F32)
            rest = total - high
            naug_ref[head, :, :LANES] = jnp.where(own, low, jnp.zeros_like(low))
            naug_ref[head, :, LANES:] = jnp.where(
                lane == 0, high, jnp.where(lane == 1, rest, 0.0)
            ).astype(BF16)
        dq_acc[...] = jnp.zeros_like(dq_acc)
        dk_acc[...] = jnp.zeros_like(dk_acc)
        dv_acc[...] = jnp.zeros_like(dv_acc)

    def run(key_block, query_block):
        keys = slice(key_block * BLOCK, (key_block + 1) * BLOCK)
        queries = slice(query_block * BLOCK, (query_block + 1) * BLOCK)
        key_rows = k_ref[keys, :]
        query_rows = q_ref[queries, :]
        key_flipped = key_rows.astype(F32).T.astype(BF16)
        if key_block == query_block:
            places = key_block * BLOCK + lax.broadcasted_iota(jnp.int32, (BLOCK, BLOCK), 0)
            visible = places <= limit_ref[:, queries]
        dq = jnp.zeros((LANES, BLOCK), F32)
        dk = jnp.zeros((BLOCK, LANES), F32)
        dv = jnp.zeros((BLOCK, LANES), F32)
        for head in range(heads):
            own = head_lanes(head, head_size, BLOCK)
            masked = jnp.where(own, query_rows, jnp.zeros_like(query_rows))
            weights = jnp.exp2(mm_nt(key_rows, masked) * (scaling * LOG2E))
            if key_block == query_block:
                weights = jnp.where(visible, weights, 0.0)
            naug = naug_ref[head, queries, :]
            slopes = mm_nt(vaug_ref[keys, :], naug)
            scores = (weights * slopes).astype(BF16)
            dv += mm(weights.astype(BF16), naug[:, :LANES])
            dk += mm(scores, masked)
            row = lax.broadcasted_iota(jnp.int32, (LANES, BLOCK), 0)
            mine = (row >= head * head_size) & (row < (head + 1) * head_size)
            dq += mm(jnp.where(mine, key_flipped, jnp.zeros_like(key_flipped)), scores)
        dq_acc[:, queries] += dq
        dk_acc[keys, :] += dk
        dv_acc[keys, :] += dv

    for number, (key_block, query_block) in enumerate(pairs):
        pl.when(step == number)(functools.partial(run, key_block, query_block))

    @pl.when(step == len(pairs) - 1)
    def _():
        dq_ref[...] = (dq_acc[...].T * scaling).astype(BF16)
        dk_ref[...] = (dk_acc[...] * scaling).astype(BF16)
        dv_ref[...] = dv_acc[...].astype(BF16)


def attention_backward(
    mixed, attended, inverse, grad, limits_row, head_size, start=0, count=None
):
    length, width = attended.shape
    groups = width // LANES
    count = groups if count is None else count
    blocks = length // BLOCK
    pairs = [(k, q) for q in range(blocks) for k in range(q + 1)]
    whole = lambda offset: pl.BlockSpec((length, LANES), lambda g, s: (0, offset + g))
    results = pl.pallas_call(
        functools.partial(attention_backward_kernel, head_size, pairs),
        out_shape=(jax.ShapeDtypeStruct((length, count * LANES), BF16),) * 3,
        grid=(count, len(pairs)),
        in_specs=[
            whole(start),
            whole(groups + start),
            whole(2 * groups + start),
            whole(start),
            whole(start),
            whole(start),
            pl.BlockSpec((1, length), lambda g, s: (0, 0)),
        ],
        out_specs=[whole(0), whole(0), whole(0)],
        scratch_shapes=[
            pltpu.VMEM((length, 2 * LANES), BF16),
            pltpu.VMEM((LANES // head_size, length, 2 * LANES), BF16),
            pltpu.VMEM((LANES, length), F32),
            pltpu.VMEM((length, LANES), F32),
            pltpu.VMEM((length, LANES), F32),
        ],
        compiler_params=pltpu.CompilerParams(vmem_limit_bytes=32 << 20),
        cost_estimate=pl.CostEstimate(
            flops=int(count * (5.2 if head_size == HD1 else 9.6) * COST), bytes_accessed=1, transcendentals=0
        ),
        name="attention_backward",
    )(mixed, mixed, mixed, attended, inverse, grad, limits_row)
    if count == 1:
        return tuple(results)
    return tuple(r[:, g * LANES : (g + 1) * LANES] for g in range(count) for r in results)


def swap(value, axis):
    return lax.ppermute(value, axis, SWAP)


def after(value, *others):
    return lax.optimization_barrier((value, *others))[0]


def near(pack):
    return (swap(pack, "row"), swap(pack, "y"))


def across_by_row(pair, *others):
    return swap(after(pair[0], *others), "y")


def across_by_y(pair, *others):
    return swap(after(pair[1], *others), "row")


def across_direct(pack):
    return lax.ppermute(pack, ("row", "y"), [(i, 3 - i) for i in range(4)])


def across_both(pair, split, *others):
    first, second = after((pair[0][:split], pair[1][split:]), *others)
    return (swap(first, "y"), swap(second, "row"))


class Parts:
    def __init__(self, refs, start=0, far=None):
        own, by_row, by_y, across = refs
        self.refs = ((own, by_y), (by_row, across))
        self.start = start
        self.far = start if far is None else far

    def rows(self, by_row, by_y, base, count, offset=0):
        start = self.far if by_row and by_y else self.start
        return self.refs[by_row][by_y][pl.ds(start + base + offset, count), :]


class Pair:
    def __init__(self, refs, split):
        own, by_row, by_y, first, second = refs
        self.first = Parts((own, by_row, by_y, first))
        self.second = Parts((own, by_row, by_y, second), split, 0)


COST = 1e7
VMEM = pl.BlockSpec(memory_space=pltpu.VMEM)
SMEM = pl.BlockSpec(memory_space=pltpu.SMEM)


def call(
    kernel, name, outs, args, scratch=(), scalars=0, limit=48, cost=1, needs=(), marks=(), fetch=False
):
    count = len(args)
    arrays = count - scalars
    if needs:
        args = (*args[:scalars], after(args[scalars], *needs), *args[scalars + 1 :])
    scratch = list(scratch)
    if fetch:
        scratch += [pltpu.VMEM(a.shape, a.dtype) for a in args[scalars:]]
        scratch.append(pltpu.SemaphoreType.DMA((arrays,)))

    def body(*refs):
        given, rest = refs[:count], refs[count + len(marks) :]
        if fetch:
            local, semaphores, rest = rest[-arrays - 1 : -1], rest[-1], rest[: -arrays - 1]
            copies = [
                pltpu.make_async_copy(source, target, semaphores.at[i])
                for i, (source, target) in enumerate(zip(given[scalars:], local))
            ]
            for copy in copies:
                copy.start()
            for copy in copies:
                copy.wait()
            given = (*given[:scalars], *local)
        kernel(*given, *rest)

    place = pl.BlockSpec(memory_space=pltpu.HBM) if fetch else VMEM
    return pl.pallas_call(
        body,
        out_shape=outs,
        in_specs=[SMEM] * scalars + [place] * arrays + [VMEM] * len(marks),
        out_specs=jax.tree.map(lambda _: VMEM, outs),
        scratch_shapes=scratch,
        compiler_params=pltpu.CompilerParams(vmem_limit_bytes=limit << 20),
        cost_estimate=pl.CostEstimate(
            flops=int(cost * COST), bytes_accessed=1, transcendentals=0
        ),
        name=name,
    )(*args, *marks)


def marker_kernel(in_ref, out_ref):
    out_ref[...] = in_ref[...]


def marker(value, cost, *others):
    return call(
        marker_kernel,
        "marker",
        jax.ShapeDtypeStruct(value.shape, value.dtype),
        (value,),
        cost=cost,
        limit=4,
        needs=others,
    )


def shaped(rows, columns, kind):
    return jax.ShapeDtypeStruct((rows, columns), kind)


def store_three(ref, base, vectors):
    for tile in range(vectors[0].shape[0]):
        values = jnp.concatenate([v[tile : tile + 1, :] for v in vectors], 0)
        high = values.astype(BF16)
        rest = values - high.astype(F32)
        middle = rest.astype(BF16)
        low = (rest - middle.astype(F32)).astype(BF16)
        ref[base + 16 * tile : base + 16 * (tile + 1), :] = jnp.concatenate(
            [high, middle, low, jnp.zeros_like(high)], 0
        )


def join_three(rows):
    wide = rows.astype(F32)
    return wide[0:4] + wide[4:8] + wide[8:12]


TILE = 256
FEED = 512


def lane_roll(values):
    return pltpu.roll(values.astype(F32), LANES // 2, 1)


HALF = LANES // 2
E_ROWS = 3 * LANES
A_LAST = 2 * E_ROWS
A_VEC = 3 * E_ROWS
A_END = A_VEC + 48
B_REST = E_ROWS
B_OUT = B_REST + E_ROWS // 2
B_END = 3 * E_ROWS
E_FEED = 18 * LANES
DA_VEC = 6 * LANES
DA_END = DA_VEC + 32
DB_PROJ = 2 * LANES
DB_END = 8 * LANES
F_COT = 8 * LANES
F_END = 12 * LANES
D_SEND = 19 * LANES + 16


def pack_mixing_kernel(w_ref, out_ref, v1, v2, v3, v4, pack_ref):
    store_three(pack_ref, A_VEC, (v1, v2, v3, v4))
    rows = w_ref.shape[2]
    parts = [w_ref[kind].astype(F32).T.astype(BF16) for kind in range(3)]
    pack_ref[:rows, :] = parts[0][:, :LANES]
    pack_ref[rows : 2 * rows, :] = parts[1][:, :LANES]
    pack_ref[A_LAST:A_VEC, :HALF] = parts[0][:, LANES:]
    pack_ref[A_LAST:A_VEC, HALF:] = parts[1][:, LANES:]
    pack_ref[A_END : A_END + rows, :] = parts[2][:, :LANES]
    rest = A_END + B_REST
    pack_ref[rest : rest + rows // 2, :HALF] = parts[2][: rows // 2, LANES:]
    pack_ref[rest : rest + rows // 2, HALF:] = parts[2][rows // 2 :, LANES:]
    heads = out_ref.shape[0]
    base = A_END + B_OUT
    for tile in range(3):
        pack_ref[base + tile * heads : base + (tile + 1) * heads, :] = out_ref[
            :, tile * LANES : (tile + 1) * LANES
        ]


def pack_encoder_kernel(up_ref, down_ref, pack_ref):
    base = 0
    for weight_ref in (up_ref, down_ref):
        rows, columns = weight_ref.shape
        for tile in range(columns // LANES):
            pack_ref[base : base + rows, :] = weight_ref[:, tile * LANES : (tile + 1) * LANES]
            base += rows


def pack_decoder_kernel(
    place_ref, mix_ref, out_ref, up_ref, down_ref, v1, v2, v3, v4, proj_ref, cot_ref, keep_ref, send_ref
):
    core = place_ref[0]
    rows = mix_ref.shape[1]
    units = up_ref.shape[1] // 2
    for target, half in ((keep_ref, core), (send_ref, 1 - core)):
        base = 0
        for i in range(3):
            target[base : base + rows, :] = mix_ref[i, :, pl.ds(half * LANES, LANES)]
            base += rows
        target[base : base + LANES, :] = out_ref[pl.ds(half * LANES, LANES), :]
        base += LANES
        for i in range(units // LANES):
            target[base : base + rows, :] = up_ref[:, pl.ds(half * units + i * LANES, LANES)]
            base += rows
        target[base : base + units, :] = down_ref[pl.ds(half * units, units), :]
        base += units
        target[base : base + 3 * LANES, :] = proj_ref[...]
        base += 3 * LANES
        target[base : base + 4 * LANES, :] = cot_ref[...]
        base += 4 * LANES
        store_three(target, base, (v1, v2, v3, v4))


def join_decoder_kernel(place_ref, keep_ref, got_ref, mix_ref, feed_ref):
    core = place_ref[0]
    rows = LANES
    for source, side in ((keep_ref, core), (got_ref, 1 - core)):
        base = 0
        for i in range(3):
            mix_ref[pl.ds(2 * i * rows + side * rows, rows), :] = source[base : base + rows, :]
            base += rows
        mix_ref[pl.ds(DA_END + side * rows, rows), :] = source[base : base + rows, :]
        base += rows
        for i in range(4):
            feed_ref[pl.ds(2 * i * rows + side * rows, rows), :] = source[base : base + rows, :]
            base += rows
        feed_ref[pl.ds(F_END + side * 4 * rows, 4 * rows), :] = source[base : base + 4 * rows, :]
        base += 4 * rows
        mix_ref[pl.ds(DA_END + DB_PROJ + side * 3 * rows, 3 * rows), :] = source[
            base : base + 3 * rows, :
        ]
        base += 3 * rows
        for start in (F_COT, F_END + F_COT):
            feed_ref[pl.ds(start + side * 2 * rows, 2 * rows), :] = source[base : base + 2 * rows, :]
            base += 2 * rows
        mix_ref[pl.ds(DA_VEC + side * 16, 16), :] = source[base : base + 16, :]


def join_input_kernel(place_ref, own, by_row, by_y, first, second, out_ref):
    y = place_ref[3]
    width = own.shape[1]
    split = second.shape[0]
    for right, by_y_side, sources in (
        (0, 0, (own, own)),
        (1, 0, (by_row, by_row)),
        (0, 1, (by_y, by_y)),
        (1, 1, (first, second)),
    ):
        base = (y if by_y_side == 0 else 1 - y) * 2 * split
        for number, source in enumerate(sources):
            start = 0 if source is second else number * first.shape[0]
            at = pl.ds(base + number * split, split)
            out_ref[at, right * width : (right + 1) * width] = source[start : start + split, :]


def norm_rows(values):
    width = values.shape[1]
    average = jnp.sum(values, 1, keepdims=True) / width
    variance = jnp.sum(values * values, 1, keepdims=True) / width - average * average
    inverse = lax.rsqrt(variance + EPSILON)
    return ((values - average) * inverse, inverse)


def first_norm_kernel(core_ref, own, other, vec_own, vec_other, x_ref, normed_ref, vec_ref):
    core = core_ref[0]
    for side, source in ((0, vec_own), (3, vec_other)):
        for tile in range(3):
            vec_ref[:, (side + tile) * LANES : (side + tile + 1) * LANES] = join_three(
                source[A_VEC + 16 * tile : A_VEC + 16 * (tile + 1), :]
            )
    rows = own.shape[0] // 2
    gain, bias = vec_ref[0:1, :], vec_ref[1:2, :]
    for source, place in ((own, core), (other, 1 - core)):
        for y in range(2):
            values = source[y * rows : (y + 1) * rows, :]
            target = pl.ds((2 * y + place) * rows, rows)
            x_ref[target, :] = values
            centred, _ = norm_rows(values.astype(F32))
            normed_ref[target, :] = (centred * gain + bias).astype(BF16)


def encoder_mixing_kernel(normed_ref, *refs):
    pair = Pair(refs[:5], A_END)
    first, second = pair.first, pair.second
    mixed_ref, weight_ref, out_ref = refs[5:8]
    out_ref[...] = encoder_out_rows(second)
    rows = E_ROWS
    low = lax.broadcasted_iota(jnp.int32, (rows, LANES), 1) < HALF
    for half in range(2):
        at = slice(half * rows, (half + 1) * rows)
        for kind, parts, base in ((0, first, 0), (1, first, rows), (2, second, 0)):
            for group, side in ((0, 0), (2, 1)):
                tile = (3 * kind + group) * LANES
                weight_ref[at, tile : tile + LANES] = parts.rows(half, side, base, rows)
        mine = first.rows(half, 0, A_LAST, rows).astype(F32)
        theirs = first.rows(half, 1, A_LAST, rows).astype(F32)
        weight_ref[at, LANES : 2 * LANES] = jnp.where(low, mine, lane_roll(theirs)).astype(BF16)
        weight_ref[at, 4 * LANES : 5 * LANES] = jnp.where(low, lane_roll(mine), theirs).astype(BF16)
        mine = second.rows(half, 0, B_REST, rows // 2).astype(F32)
        theirs = second.rows(half, 1, B_REST, rows // 2).astype(F32)
        mine = jnp.concatenate([mine, lane_roll(mine)], 0)
        theirs = jnp.concatenate([lane_roll(theirs), theirs], 0)
        weight_ref[at, 7 * LANES : 8 * LANES] = jnp.where(low, mine, theirs).astype(BF16)

    @pl.loop(0, normed_ref.shape[0] // FEED)
    def _(tile):
        at = pl.ds(tile * FEED, FEED)
        mixed_ref[at, :] = mm(normed_ref[at, :], weight_ref[...]).astype(BF16)


def encoder_out_rows(parts):
    heads = 3 * LANES // 2
    sides = [
        jnp.concatenate(
            [parts.rows(i, j, B_OUT + t * heads, heads) for i in range(2) for t in range(3)], 1
        )
        for j in range(2)
    ]
    return jnp.concatenate([sides[0], sides[1][LANES:], sides[1][:LANES]], 0)


def decoder_out_rows(parts):
    return jnp.concatenate(
        [
            jnp.concatenate(
                [parts.rows(i, j, t * LANES, LANES) for j in range(2) for t in range(2)], 1
            )
            for i in range(2)
        ],
        0,
    )


def attend_kernel(
    head_size, mixed_ref, limit_ref, weight_ref, attended_ref, inverse_ref, partial_ref, aug_ref
):
    length, width = attended_ref.shape
    groups, heads = width // LANES, LANES // head_size
    scale = head_size ** (-0.5) * LOG2E
    for group in range(groups):
        at = (2 * groups + group) * LANES
        aug_ref[group, :, :LANES] = mixed_ref[:, at : at + LANES]
        aug_ref[group, :, LANES:] = jnp.ones((length, LANES), BF16)

    for block in range(length // BLOCK):

        @pl.loop(0, BLOCK // FEED)
        def _(step):
            at = pl.ds(block * BLOCK + step * FEED, FEED)
            limits = limit_ref[at, :]
            places = block * BLOCK + lax.broadcasted_iota(jnp.int32, (FEED, BLOCK), 1)
            visible = places <= limits

            @pl.loop(0, groups * heads // 2)
            def _(step):
                group, pair = step // (heads // 2), step % (heads // 2)
                lanes = pl.ds(pl.multiple_of(group * LANES, LANES), LANES)
                queries = mixed_ref[at, lanes]
                result = attended_ref[at, lanes]
                inverses = inverse_ref[at, lanes]
                lane = lax.broadcasted_iota(jnp.int32, (FEED, LANES), 1)
                for number in range(2):
                    start = (2 * pair + number) * head_size
                    own = (lane >= start) & (lane < start + head_size)
                    masked = jnp.where(own, queries, jnp.zeros_like(queries))
                    total = jnp.zeros((FEED, 2 * LANES), F32)
                    for part in range(block + 1):
                        span = slice(part * BLOCK, (part + 1) * BLOCK)
                        keys = mixed_ref[span, pl.ds((groups + group) * LANES, LANES)]
                        weights = jnp.exp2(mm_nt(masked, keys) * scale)
                        if part == block:
                            weights = jnp.where(visible, weights, 0.0)
                        total = total + mm(weights.astype(BF16), aug_ref[group, span, :])
                    inverse = 1.0 / total[:, LANES:]
                    result = jnp.where(own, (total[:, :LANES] * inverse).astype(BF16), result)
                    inverses = jnp.where(own, inverse, inverses)
                attended_ref[at, lanes] = result
                inverse_ref[at, lanes] = inverses

            partial_ref[at, :] = mm(attended_ref[at, :], weight_ref[...]).astype(BF16)


def gelu_pair(values):
    area = 0.5 * (1.0 + lax.erf(values * (0.5**0.5)))
    slope = area + values * jnp.exp2(values * values * (-0.5 * LOG2E)) * (0.5 / math.pi) ** 0.5
    return (values * area, slope)


class Feed:
    def __init__(self, up_parts, down_parts, decoder):
        self.up_parts = up_parts
        self.down_parts = down_parts
        self.decoder = decoder
        self.features = 2 * LANES if decoder else 3 * LANES
        self.units = 4 * LANES if decoder else 6 * LANES
        self.down = 0
        self.chunks = self.units // (2 * LANES)

    def rows(self, parts, feature, unit, base, count, offset):
        if self.decoder:
            return parts.rows(unit, feature, base, count, offset)
        return parts.rows(feature, unit, base, count, offset)

    def up_chunk(self, unit, chunk):
        f = self.features
        return jnp.concatenate(
            [
                jnp.concatenate(
                    [
                        self.rows(
                            self.up_parts, i, unit, 0, f, pl.multiple_of((2 * chunk + t) * f, f)
                        )
                        for t in range(2)
                    ],
                    1,
                )
                for i in range(2)
            ],
            0,
        )

    def up_both(self, chunk):
        return jnp.concatenate([self.up_chunk(unit, chunk) for unit in range(2)], 1)

    def down_both(self, chunk):
        return jnp.concatenate([self.down_chunk(unit, chunk) for unit in range(2)], 0)

    def down_chunk(self, unit, chunk):
        return jnp.concatenate(
            [
                self.rows(
                    self.down_parts,
                    i,
                    unit,
                    self.down + t * self.units,
                    2 * LANES,
                    pl.multiple_of(chunk * 2 * LANES, 2 * LANES),
                )
                for i in range(2)
                for t in range(self.features // LANES)
            ],
            1,
        )


def feed_forward_kernel(stream_ref, mine_ref, got_ref, vec_ref, *refs):
    middle_ref, normed_ref, active_ref, slope_ref, partial_ref, total_ref = refs[5:11]
    pair = Pair(refs[:5], E_FEED)
    feed = Feed(pair.first, pair.second, False)
    gain, bias = vec_ref[2:3, :], vec_ref[3:4, :]

    @pl.loop(0, stream_ref.shape[0] // FEED)
    def _(tile):
        at = pl.ds(tile * FEED, FEED)
        middle = stream_ref[at, :].astype(F32) + (
            mine_ref[at, :].astype(F32) + got_ref[at, :].astype(F32)
        )
        middle_ref[at, :] = middle
        centred, _ = norm_rows(middle)
        normed_ref[at, :] = (centred * gain + bias).astype(BF16)
        total_ref[...] = jnp.zeros_like(total_ref)

        @pl.loop(0, feed.chunks)
        def _(chunk):
            hidden = mm(normed_ref[at, :], feed.up_both(chunk))
            active, slope = gelu_pair(hidden)
            low = active.astype(BF16)
            slope = slope.astype(BF16)
            for unit in range(2):
                lanes = pl.ds(unit * feed.units + chunk * 2 * LANES, 2 * LANES)
                part = slice(unit * 2 * LANES, (unit + 1) * 2 * LANES)
                active_ref[at, lanes] = low[:, part]
                slope_ref[at, lanes] = slope[:, part]
            total_ref[...] += mm(low, feed.down_both(chunk))

        partial_ref[at, :] = total_ref[...].astype(BF16)


def decoder_feed_kernel(
    place_ref, stream_ref, mine_ref, got_ref, vec_ref, *refs
):
    middle_ref, normed_ref, active_ref, hidden_ref, partial_ref, cot_ref, total_ref = refs[4:11]
    first, second = Parts(refs[:4]), Parts(refs[:4], F_END)
    row = place_ref[2]
    for i in range(2):
        for number, parts in enumerate((first, second)):
            at = pl.ds((row if i == 0 else 1 - row) * 4 * LANES + number * 2 * LANES, 2 * LANES)
            for tile in range(4):
                cot_ref[at, tile * LANES : (tile + 1) * LANES] = parts.rows(
                    i, tile // 2, F_COT + (tile % 2) * 2 * LANES, 2 * LANES
                )
    feed = Feed(first, second, True)
    gain, bias = vec_ref[2:3, :], vec_ref[3:4, :]

    @pl.loop(0, stream_ref.shape[0] // FEED)
    def _(tile):
        at = pl.ds(tile * FEED, FEED)
        middle = stream_ref[at, :] + (mine_ref[at, :].astype(F32) + got_ref[at, :].astype(F32))
        middle_ref[at, :] = middle
        centred, _ = norm_rows(middle)
        normed_ref[at, :] = (centred * gain + bias).astype(BF16)
        total_ref[...] = jnp.zeros_like(total_ref)

        @pl.loop(0, feed.chunks)
        def _(chunk):
            upward = feed.up_both(chunk)
            hidden = mm(normed_ref[at, :], upward)
            active, slope = gelu_pair(hidden)
            active = active.astype(BF16)
            grad = mm_nt(cot_ref[at, :], feed.down_both(chunk))
            low = (grad * slope).astype(BF16)
            for unit in range(2):
                lanes = pl.ds(unit * feed.units + chunk * 2 * LANES, 2 * LANES)
                part = slice(unit * 2 * LANES, (unit + 1) * 2 * LANES)
                active_ref[at, lanes] = active[:, part]
                hidden_ref[at, lanes] = low[:, part]
            total_ref[...] += mm_nt(low, upward)

        partial_ref[at, :] = total_ref[...].astype(BF16)


def bridge_kernel(place_ref, middle_ref, mine_ref, got_ref, *refs):
    (
        out_ref, low_ref, stream_ref, normed_ref, mixed_ref, weight_ref, vec_ref, mixing_ref,
        back_ref,
    ) = refs[5:14]
    block = place_ref[1]
    pair = Pair(refs[:5], DA_END)
    first, second = pair.first, pair.second
    back_ref[...] = decoder_out_rows(second)
    rows = E_ROWS
    for j in range(2):
        for c in range(2):
            tile = (2 * j + c) * LANES
            for i in range(2):
                weight_ref[i * rows : (i + 1) * rows, tile : tile + LANES] = second.rows(
                    i, j, DB_PROJ + c * rows, rows
                )
            vec_ref[:, tile : tile + LANES] = join_three(first.rows(0, j, DA_VEC + 16 * c, 16))
    for kind in range(3):
        for i in range(2):
            tile = (2 * kind + i) * LANES
            for j in range(2):
                mixing_ref[2 * j * LANES : 2 * (j + 1) * LANES, tile : tile + LANES] = first.rows(
                    i, j, 2 * kind * LANES, 2 * LANES
                )
    gain, bias = vec_ref[0:1, :], vec_ref[1:2, :]
    width = low_ref.shape[1]

    @pl.loop(0, middle_ref.shape[0] // FEED)
    def _(tile):
        at = pl.ds(tile * FEED, FEED)
        total = middle_ref[at, :] + (mine_ref[at, :].astype(F32) + got_ref[at, :].astype(F32))
        low = total.astype(BF16)

        for part in range(FEED // TILE):

            @pl.when(tile * (FEED // TILE) + part == block)
            def _():
                out_ref[...] = total[part * TILE : (part + 1) * TILE, :width]

        low_ref[at, :] = low[:, :width]
        stream = mm(low, weight_ref[...])
        stream_ref[at, :] = stream
        centred, _ = norm_rows(stream)
        normed = (centred * gain + bias).astype(BF16)
        normed_ref[at, :] = normed
        mixed_ref[at, :] = mm(normed, mixing_ref[...]).astype(BF16)


def norm_back(incoming, centred, inverse, gain):
    width = incoming.shape[1]
    scaled = incoming * gain
    first = jnp.sum(scaled, 1, keepdims=True) / width
    second = jnp.sum(scaled * centred, 1, keepdims=True) / width
    return inverse * (scaled - first - centred * second)


def store_sums(sums_ref, incoming, centred):
    sums_ref[0:1, :] = jnp.sum(incoming * centred, 0, keepdims=True)
    sums_ref[1:2, :] = jnp.sum(incoming, 0, keepdims=True)


def own_sums(place_ref, tile, sums_ref, incoming, centred):
    half = TILE // 2

    @pl.when((tile == place_ref[1]) & (place_ref[2] == 0))
    def _():
        store_sums(sums_ref, incoming[:half], centred[:half])

    @pl.when((tile == place_ref[1]) & (place_ref[2] == 1))
    def _():
        store_sums(sums_ref, incoming[half:], centred[half:])


def middle_back_kernel(
    place_ref, mine_ref, got_ref, middle_ref, grad_ref, vec_ref, weight_ref,
    total_ref, low_ref, attended_ref, sums_ref,
):
    gain = vec_ref[2:3, :]
    width = low_ref.shape[1]

    @pl.loop(0, middle_ref.shape[0] // TILE)
    def _(tile):
        at = pl.ds(tile * TILE, TILE)
        incoming = mine_ref[at, :].astype(F32) + got_ref[at, :].astype(F32)
        centred, inverse = norm_rows(middle_ref[at, :])
        total = grad_ref[at, :].astype(F32) + norm_back(incoming, centred, inverse, gain)
        total_ref[at, :] = total
        low = total.astype(BF16)
        low_ref[at, :] = low[:, :width]
        attended_ref[at, :] = mm_nt(low, weight_ref[...])
        own_sums(place_ref, tile, sums_ref, incoming, centred)


def mixed_low(refs, at):
    kinds = len(refs) // 3
    return jnp.concatenate([refs[3 * g + i][at, :] for i in range(3) for g in range(kinds)], 1)


def mixed_back_kernel(*refs):
    lows, weight_ref, partial_ref = refs[:-2], refs[-2], refs[-1]

    @pl.loop(0, partial_ref.shape[0] // FEED)
    def _(tile):
        at = pl.ds(tile * FEED, FEED)
        partial_ref[at, :] = mm_nt(mixed_low(lows, at), weight_ref[...]).astype(BF16)


def mixed_last_kernel(place_ref, *refs):
    core, y = place_ref[0], place_ref[3]
    lows, weight_ref, keep_ref, send_ref = refs[:-3], refs[-3], refs[-2], refs[-1]
    for target, side in ((keep_ref, core), (send_ref, 1 - core)):
        at = pl.ds((2 * y + side) * TILE, TILE)
        target[...] = mm_nt(mixed_low(lows, at), weight_ref[...]).astype(BF16)


def bridge_back_kernel(
    place_ref, mine_ref, got_ref, stream_ref, grad_ref, vec_ref, proj_ref,
    low_ref, encoder_ref, down_ref, sums_ref,
):
    gain = vec_ref[0:1, :]

    @pl.loop(0, stream_ref.shape[0] // TILE)
    def _(tile):
        at = pl.ds(tile * TILE, TILE)
        incoming = mine_ref[at, :].astype(F32) + got_ref[at, :].astype(F32)
        centred, inverse = norm_rows(stream_ref[at, :])
        grad = grad_ref[at, :] + norm_back(incoming, centred, inverse, gain)
        own_sums(place_ref, tile, sums_ref, incoming, centred)
        low = grad.astype(BF16)
        low_ref[at, :] = low
        encoder = mm_nt(low, proj_ref[...])
        encoder_ref[at, :] = encoder
        down_ref[at, :] = encoder.astype(BF16)


def feed_back_kernel(down_ref, slope_ref, *refs):
    hidden_ref, partial_ref, total_ref = refs[5:8]
    pair = Pair(refs[:5], E_FEED)
    feed = Feed(pair.first, pair.second, False)

    @pl.loop(0, down_ref.shape[0] // FEED)
    def _(tile):
        at = pl.ds(tile * FEED, FEED)
        total_ref[...] = jnp.zeros_like(total_ref)

        @pl.loop(0, feed.chunks)
        def _(chunk):
            back = mm_nt(down_ref[at, :], feed.down_both(chunk))
            parts = []
            for unit in range(2):
                lanes = pl.ds(unit * feed.units + chunk * 2 * LANES, 2 * LANES)
                part = slice(unit * 2 * LANES, (unit + 1) * 2 * LANES)
                hidden = (back[:, part] * slope_ref[at, lanes].astype(F32)).astype(BF16)
                hidden_ref[at, lanes] = hidden
                parts.append(hidden)
            total_ref[...] += mm_nt(jnp.concatenate(parts, 1), feed.up_both(chunk))

        partial_ref[at, :] = total_ref[...].astype(BF16)


def input_back_kernel(place_ref, mine_ref, got_ref, x_ref, grad_ref, vec_ref, out_ref, sums_ref):
    at = pl.ds(place_ref[1] * TILE, TILE)
    incoming = mine_ref[...].astype(F32) + got_ref[...].astype(F32)
    centred, inverse = norm_rows(x_ref[at, :].astype(F32))
    total = grad_ref[at, :] + norm_back(incoming, centred, inverse, vec_ref[0:1, :])
    out_ref[...] = total[:, : out_ref.shape[1]]
    own_sums(place_ref, place_ref[1], sums_ref, incoming, centred)


def store_tiles(ref, base, value):
    rows = value.shape[0]
    for tile in range(value.shape[1] // LANES):
        ref[base + tile * rows : base + (tile + 1) * rows, :] = value[
            :, tile * LANES : (tile + 1) * LANES
        ].astype(BF16)


G_LAST = 3 * E_ROWS
G_REST = 4 * E_ROWS
G_OUT = G_REST + E_ROWS // 2
G_END = 6 * E_ROWS
GA_UP = 8 * LANES
GA_END = 16 * LANES
GB_OUT = 6 * LANES
GB_PROJ = 8 * LANES
GB_END = 11 * LANES


def feed_grads_kernel(active_ref, cot_ref, normed_ref, hidden_ref, pack_ref):
    units, features = 4 * LANES, 2 * LANES
    store_tiles(pack_ref, 0, mm_tn(active_ref[:, :units], cot_ref[:, :features]))
    store_tiles(pack_ref, GA_UP, mm_tn(normed_ref[:, :features], hidden_ref[:, :units]))


def mixing_grads_kernel(
    place_ref, normed_ref, q_ref, k_ref, v_ref, attended_ref, middle_ref, encoder_ref, proj_ref, pack_ref
):
    lows = jnp.concatenate([q_ref[:, :LANES], k_ref[:, :LANES], v_ref[:, :LANES]], 1)
    store_tiles(pack_ref, 0, mm_tn(normed_ref[:, : 2 * LANES], lows))
    store_tiles(pack_ref, GB_OUT, mm_tn(attended_ref[:, :LANES], middle_ref[...]))
    own = proj_ref[:, pl.ds(place_ref[0] * LANES, LANES)]
    store_tiles(pack_ref, GB_PROJ, mm_tn(encoder_ref[...], own))


def product_kernel(left_ref, right_ref, out_ref):
    rows, columns = out_ref.shape
    out_ref[...] = mm_tn(left_ref[:, :rows], right_ref[:, :columns]).astype(BF16)


def encoder_grads_kernel(
    normed_ref, q_ref, k_ref, v_ref, q2_ref, k2_ref, v2_ref, attended_ref, middle_ref, pack_ref
):
    low = lax.broadcasted_iota(jnp.int32, q2_ref.shape, 1) < HALF
    last = jnp.where(low, q2_ref[...].astype(F32), lane_roll(k2_ref[...])).astype(BF16)
    lows = jnp.concatenate([q_ref[...], k_ref[...], v_ref[...], last, v2_ref[...]], 1)
    grads = mm_tn(normed_ref[:, :E_ROWS], lows)
    store_tiles(pack_ref, 0, grads[:, : 4 * LANES])
    rest = grads[:, 4 * LANES :]
    half = E_ROWS // 2
    low = lax.broadcasted_iota(jnp.int32, (half, LANES), 1) < HALF
    pack_ref[G_REST:G_OUT, :] = jnp.where(low, rest[:half], lane_roll(rest[half:])).astype(BF16)
    grads = mm_tn(attended_ref[:, : 2 * LANES], middle_ref[...])
    store_tiles(pack_ref, G_OUT, grads[:half])


def encoder_unpack_kernel(pack_ref, mixing_ref, out_ref):
    rows, half = E_ROWS, E_ROWS // 2
    for kind in range(3):
        mixing_ref[kind, :LANES, :] = pack_ref[kind * rows : (kind + 1) * rows, :].astype(F32).T
    last = pack_ref[G_LAST:G_REST, :].astype(F32).T
    mixing_ref[0, LANES:, :] = last[:HALF]
    mixing_ref[1, LANES:, :] = last[HALF:]
    rest = pack_ref[G_REST:G_OUT, :].astype(F32).T
    mixing_ref[2, LANES:, :] = jnp.concatenate([rest[:HALF], rest[HALF:]], 1)
    for tile in range(3):
        at = slice(G_OUT + tile * half, G_OUT + (tile + 1) * half)
        out_ref[:, tile * LANES : (tile + 1) * LANES] = pack_ref[at, :].astype(F32)


def decoder_send_kernel(place_ref, feed_ref, mix_ref, send_ref):
    other = 1 - place_ref[0]
    rows = LANES
    send_ref[: 4 * rows, :] = feed_ref[pl.ds(other * 4 * rows, 4 * rows), :]
    for tile in range(4):
        send_ref[(4 + tile) * rows : (5 + tile) * rows, :] = feed_ref[
            pl.ds(GA_UP + 2 * tile * rows + other * rows, rows), :
        ]
    for tile in range(3):
        send_ref[(8 + tile) * rows : (9 + tile) * rows, :] = mix_ref[
            pl.ds(2 * tile * rows + other * rows, rows), :
        ]
    send_ref[11 * rows : 12 * rows, :] = mix_ref[pl.ds(GB_OUT + other * rows, rows), :]


def decoder_unpack_kernel(
    place_ref, feed_ref, mix_ref, got_ref, mixing_ref, out_ref, up_ref, down_ref, proj_ref
):
    core = place_ref[0]
    rows = LANES
    units = 4 * rows
    down_ref[pl.ds(core * units, units), :] = feed_ref[pl.ds(core * units, units), :].astype(F32)
    down_ref[pl.ds((1 - core) * units, units), :] = got_ref[:units, :].astype(F32)
    for tile in range(4):
        up_ref[:, pl.ds(core * units + tile * rows, rows)] = feed_ref[
            pl.ds(GA_UP + 2 * tile * rows + core * rows, rows), :
        ].astype(F32)
        up_ref[:, pl.ds((1 - core) * units + tile * rows, rows)] = got_ref[
            (4 + tile) * rows : (5 + tile) * rows, :
        ].astype(F32)
    for tile in range(3):
        mixing_ref[tile, :, pl.ds(core * rows, rows)] = mix_ref[
            pl.ds(2 * tile * rows + core * rows, rows), :
        ].astype(F32)
        mixing_ref[tile, :, pl.ds((1 - core) * rows, rows)] = got_ref[
            (8 + tile) * rows : (9 + tile) * rows, :
        ].astype(F32)
    out_ref[pl.ds(core * rows, rows), :] = mix_ref[pl.ds(GB_OUT + core * rows, rows), :].astype(F32)
    out_ref[pl.ds((1 - core) * rows, rows), :] = got_ref[11 * rows : 12 * rows, :].astype(F32)
    proj_ref[...] = mix_ref[GB_PROJ:GB_END, :].astype(F32)


def line_first(value, size):
    if size == 4:
        return (value, lax.ppermute(value, "dp", [(0, 1), (3, 2)]))
    if size & (size - 1):
        return lax.psum(value, "dp")
    distance = 1
    while distance < size:
        got = lax.ppermute(value, "dp", [(i, i ^ distance) for i in range(size)])
        value = (value.astype(F32) + got.astype(F32)).astype(BF16)
        distance *= 2
    return value


def line_next(state, size, pairs, *others):
    if size != 4:
        return state
    mine, got = after(state, *others)
    total = (mine.astype(F32) + got.astype(F32)).astype(BF16)
    return (total, lax.ppermute(total, "dp", pairs))


def line_across(state, size, *others):
    return line_next(state, size, [(1, 2), (2, 1)], *others)


def line_back(state, size, *others):
    return line_next(state, size, [(1, 0), (2, 3)], *others)


def line_last(state, size, *others):
    if size != 4:
        return state
    mine, got = after(state, *others)
    place = lax.axis_index("dp")
    return jnp.where((place == 0) | (place == 3), got, mine)


def dp_sum(value, size):
    place = lax.axis_index("dp")
    terms = [value] + [
        lax.ppermute(value, "dp", [(i, (i + step) % size) for i in range(size)])
        for step in range(1, size)
    ]
    terms = terms[::-1]
    return jnp.sum(lax.dynamic_slice_in_dim(jnp.stack(terms + terms), size - 1 - place, size, 0), 0)


def per_device(
    data_size,
    block_input,
    span_end,
    encoder_attention_gain,
    encoder_attention_bias,
    encoder_query_key_value,
    encoder_output_weight,
    encoder_feedforward_gain,
    encoder_feedforward_bias,
    encoder_up_weight,
    encoder_down_weight,
    projection,
    decoder_attention_gain,
    decoder_attention_bias,
    decoder_query_key_value,
    decoder_output_weight,
    decoder_feedforward_gain,
    decoder_feedforward_bias,
    decoder_up_weight,
    decoder_down_weight,
    output_cotangent,
):
    row = lax.axis_index("row").astype(jnp.int32)
    y = lax.axis_index("y").astype(jnp.int32)
    core = lax.axis_index("core").astype(jnp.int32)
    length = span_end.shape[0]
    own_rows, width = block_input.shape
    block = 2 * y + core
    place = jnp.stack([core, block, row, y])
    limits = span_end.reshape(length, 1)
    limits_row = span_end.reshape(1, length)
    full = 2 * width
    low_full = 4 * LANES
    units = 2 * encoder_up_weight.shape[1]
    d_units = decoder_up_weight.shape[1]
    features = 2 * LANES

    half = own_rows // 2
    x_near = near(block_input)
    tick = jnp.zeros((8, LANES), F32)
    row_of = lambda vector: vector.reshape(-1, LANES)
    keep, send = call(
        pack_decoder_kernel,
        "pack_decoder",
        (shaped(D_SEND, LANES, BF16),) * 2,
        (
            place,
            jnp.transpose(decoder_query_key_value, (1, 0, 2)),
            decoder_output_weight,
            decoder_up_weight,
            decoder_down_weight,
            row_of(decoder_attention_gain),
            row_of(decoder_attention_bias),
            row_of(decoder_feedforward_gain),
            row_of(decoder_feedforward_bias),
            projection,
            output_cotangent,
        ),
        scalars=1,
        limit=56,
        fetch=True,
    )
    m_pack = call(
        pack_mixing_kernel,
        "pack_mixing",
        shaped(A_END + B_END, LANES, BF16),
        (
            jnp.transpose(encoder_query_key_value, (1, 2, 0)),
            encoder_output_weight,
            row_of(encoder_attention_gain),
            row_of(encoder_attention_bias),
            row_of(encoder_feedforward_gain),
            row_of(encoder_feedforward_bias),
        ),
        limit=56,
        fetch=True,
        needs=(x_near, keep),
    )
    m_near = near(m_pack)
    d_got = swap(send, "core")
    dm_pack, f_pack = call(
        join_decoder_kernel,
        "join_decoder",
        (shaped(DA_END + DB_END, LANES, BF16), shaped(2 * F_END, LANES, BF16)),
        (place, keep, d_got),
        scalars=1,
        limit=8,
    )
    e_pack = call(
        pack_encoder_kernel,
        "pack_encoder",
        shaped(2 * E_FEED, LANES, BF16),
        (encoder_up_weight, encoder_down_weight),
        limit=56,
        fetch=True,
    )
    x_far = across_both(x_near, half, e_pack, dm_pack)
    m_far = across_both(m_near, A_END, x_far)
    sides = call(
        join_input_kernel,
        "join_input",
        shaped(2 * own_rows, full, BF16),
        (place, block_input, *x_near, *x_far),
        scalars=1,
        limit=56,
        fetch=True,
        needs=(m_near,),
    )
    m_parts = (m_pack, *m_near, *m_far)
    e_near = near(after(e_pack, sides))
    dm_near = near(after(dm_pack, sides))
    mark = marker(tick, 5000, m_far)
    stream, normed_first, e_vec = call(
        first_norm_kernel,
        "first_norm",
        (shaped(length, full, BF16), shaped(length, full, BF16), shaped(4, full, F32)),
        (place, sides, swap(sides, "core"), m_pack, m_near[0]),
        scalars=1,
        limit=8,
        marks=(mark,),
    )
    mixed, e_mixing, e_out = call(
        encoder_mixing_kernel,
        "encoder_mixing",
        (
            shaped(length, 9 * LANES, BF16),
            shaped(full, 9 * LANES, BF16),
            shaped(E_ROWS, full, BF16),
        ),
        (normed_first, *m_parts),
        limit=12,
        cost=3,
    )
    attended, inverse, partial = call(
        functools.partial(attend_kernel, HD1),
        "encoder_attend",
        (
            shaped(length, E_ROWS, BF16),
            shaped(length, E_ROWS, F32),
            shaped(length, full, BF16),
        ),
        (mixed, limits, e_out),
        (pltpu.VMEM((3, length, 2 * LANES), BF16),),
        limit=16,
        cost=12,
    )
    got = swap(partial, "core")
    e_far = across_both(e_near, E_FEED, attended, dm_near)
    e_parts = (e_pack, *e_near, *e_far)
    dm_far = across_both(dm_near, DA_END, attended)
    f_go = after(f_pack, e_far)
    f_parts = (f_pack, *near(f_go), across_direct(f_go))
    mark = marker(tick, 10000, e_far)
    middle, normed_second, active, slope, partial = call(
        feed_forward_kernel,
        "feed_forward",
        (
            shaped(length, full, F32),
            shaped(length, full, BF16),
            shaped(length, units, BF16),
            shaped(length, units, BF16),
            shaped(length, full, BF16),
        ),
        (stream, partial, got, e_vec, *e_parts),
        (pltpu.VMEM((FEED, full), F32),),
        limit=16,
        cost=12,
        marks=(mark,),
    )
    mark = marker(tick, 10000, middle)
    (
        own_encoder_out, encoder_low, d_stream, d_normed_first, d_mixed, proj_weight, d_vec, d_mixing,
        d_out,
    ) = call(
        bridge_kernel,
        "bridge",
        (
            shaped(own_rows, width, F32),
            shaped(length, width, BF16),
            shaped(length, low_full, F32),
            shaped(length, low_full, BF16),
            shaped(length, 6 * LANES, BF16),
            shaped(full, low_full, BF16),
            shaped(4, low_full, F32),
            shaped(low_full, 6 * LANES, BF16),
            shaped(2 * LANES, low_full, BF16),
        ),
        (place, middle, partial, swap(partial, "core"), dm_pack, *dm_near, *dm_far),
        scalars=1,
        limit=12,
        marks=(mark,),
        cost=5.7,
    )

    d_attended, d_inverse, partial = call(
        functools.partial(attend_kernel, HD2),
        "decoder_attend",
        (
            shaped(length, 2 * LANES, BF16),
            shaped(length, 2 * LANES, F32),
            shaped(length, low_full, BF16),
        ),
        (d_mixed, limits, d_out),
        (pltpu.VMEM((2, length, 2 * LANES), BF16),),
        limit=16,
        cost=11,
    )
    mark = marker(tick, 10000, partial)
    d_middle, d_normed_second, d_active, d_hidden, partial, cotangent = call(
        decoder_feed_kernel,
        "decoder_feed",
        (
            shaped(length, low_full, F32),
            shaped(length, low_full, BF16),
            shaped(length, d_units, BF16),
            shaped(length, d_units, BF16),
            shaped(length, low_full, BF16),
            shaped(length, low_full, BF16),
        ),
        (place, d_stream, partial, swap(partial, "core"), d_vec, *f_parts),
        (pltpu.VMEM((FEED, low_full), F32),),
        scalars=1,
        limit=16,
        marks=(mark,),
        cost=8,
    )

    got = swap(partial, "core")
    grads_a = call(
        feed_grads_kernel,
        "decoder_feed_grads",
        shaped(GA_END, LANES, BF16),
        (after(d_active, partial), cotangent, d_normed_second, d_hidden),
        limit=8,
        cost=0.8,
    )
    sum_a = line_first(grads_a, data_size)
    d_middle_grad, d_middle_low, attended_grad, d_second_sums = call(
        middle_back_kernel,
        "decoder_middle_back",
        (
            shaped(length, low_full, F32),
            shaped(length, features, BF16),
            shaped(length, 2 * LANES, F32),
            shaped(2, low_full, F32),
        ),
        (place, after(partial, grads_a), got, d_middle, cotangent, d_vec, d_out),
        scalars=1,
        limit=12,
        cost=2.6,
    )
    d_lows = attention_backward(
        d_mixed, d_attended, d_inverse, attended_grad, limits_row, HD2, 0, 1
    )
    sum_a = line_across(sum_a, data_size, d_lows)
    d_lows = d_lows + attention_backward(
        d_mixed, d_attended, d_inverse, after(attended_grad, sum_a[0]), limits_row, HD2, 1, 1
    )
    sum_a = line_back(sum_a, data_size, d_lows)
    partial = call(
        mixed_back_kernel,
        "decoder_mixed_back",
        shaped(length, low_full, BF16),
        (after(d_lows[0], sum_a[0]), *d_lows[1:], d_mixing),
        limit=12,
        cost=1.6,
    )
    got = swap(partial, "core")

    proj_low, encoder_grad, down_low, d_first_sums = call(
        bridge_back_kernel,
        "bridge_back",
        (
            shaped(length, low_full, BF16),
            shaped(length, full, F32),
            shaped(length, full, BF16),
            shaped(2, low_full, F32),
        ),
        (place, partial, got, d_stream, d_middle_grad, d_vec, proj_weight),
        scalars=1,
        limit=12,
        cost=3.9,
    )
    grads_b = call(
        mixing_grads_kernel,
        "decoder_mixing_grads",
        shaped(GB_END, LANES, BF16),
        (
            place, d_normed_first, *d_lows[:3], d_attended, d_middle_low, encoder_low,
            proj_low,
        ),
        scalars=1,
        limit=8,
        cost=1.3,
    )
    sum_b = line_first(grads_b, data_size)
    grads_c = call(
        product_kernel,
        "encoder_down_grads",
        shaped(units // 2, width, BF16),
        (after(active, grads_b), down_low),
        limit=8,
        cost=1,
    )
    sum_c = line_first(grads_c, data_size)
    hidden_low, partial = call(
        feed_back_kernel,
        "feed_back",
        (shaped(length, units, BF16), shaped(length, full, BF16)),
        (after(down_low, grads_c), slope, *e_parts),
        (pltpu.VMEM((FEED, full), F32),),
        limit=16,
        cost=12,
    )
    got = swap(partial, "core")
    sum_b = line_across(sum_b, data_size, partial)
    grads_e = call(
        product_kernel,
        "encoder_up_grads",
        shaped(width, units // 2, BF16),
        (normed_second, after(hidden_low, sum_b[0])),
        limit=8,
        cost=1000,
    )
    sum_e = line_first(grads_e, data_size)
    middle_grad, middle_low, attended_grad, second_sums = call(
        middle_back_kernel,
        "encoder_middle_back",
        (
            shaped(length, full, F32),
            shaped(length, width, BF16),
            shaped(length, 3 * LANES, F32),
            shaped(2, full, F32),
        ),
        (place, after(partial, grads_e), got, middle, encoder_grad, e_vec, e_out),
        scalars=1,
        limit=12,
        cost=5.5,
    )
    sum_c = line_across(sum_c, data_size, middle_low)
    first = attention_backward(
        mixed, attended, inverse, after(attended_grad, sum_c[0]), limits_row, HD1, 0, 1
    )
    sum_b = line_back(sum_b, data_size, first)
    sum_e = line_across(sum_e, data_size, first)
    second = attention_backward(
        mixed,
        attended,
        inverse,
        after(attended_grad, sum_b[0], sum_e[0], sum_a),
        limits_row,
        HD1,
        1,
        1,
    )
    grads_d = call(
        encoder_grads_kernel,
        "encoder_mixing_grads",
        shaped(G_END, LANES, BF16),
        (normed_first, *first, *second, attended, middle_low),
        limit=12,
        cost=1.1,
    )
    sum_d = line_first(grads_d, data_size)
    sum_c = line_back(sum_c, data_size, grads_d)
    sum_e = line_back(sum_e, data_size, grads_d)
    third = attention_backward(
        mixed, attended, inverse, after(attended_grad, grads_d, sum_b, sum_c[0], sum_e[0]), limits_row, HD1, 2, 1
    )
    sum_d = line_across(sum_d, data_size, third)
    lows = (*first, *second, after(third[0], sum_d[0]), *third[1:])
    keep, send = call(
        mixed_last_kernel,
        "encoder_mixed_back",
        (shaped(own_rows, full, BF16),) * 2,
        (place, *lows, e_mixing),
        scalars=1,
        limit=12,
        cost=1.8,
    )
    got = swap(send, "core")
    own_input_grad, first_sums = call(
        input_back_kernel,
        "input_back",
        (shaped(own_rows, width, F32), shaped(2, full, F32)),
        (place, after(keep, sum_c), got, stream, middle_grad, e_vec),
        scalars=1,
        limit=8,
        cost=1.8,
    )

    def in_order(value, index):
        half = value.shape[1] // 2
        return jnp.where(index == 0, value, jnp.concatenate([value[:, half:], value[:, :half]], 1))

    e_sums = in_order(jnp.concatenate([first_sums, second_sums], 0), row)
    d_sums = in_order(jnp.concatenate([d_first_sums, d_second_sums], 0), y)
    sums = jnp.concatenate([e_sums, jnp.pad(d_sums, ((0, 0), (0, full - low_full)))], 0)
    sums = jnp.sum(lax.all_gather(sums, ("row", "y", "core")), 0)
    sum_d = line_back(sum_d, data_size, sums)

    own, by_row = after(f_parts[:2], sum_d[0])
    out_rows, out_columns = output_cotangent.shape
    active_rows = lax.dynamic_slice_in_dim(d_active, row * out_rows, out_rows, 0)
    half = d_units // 2
    span = F_END + half
    down = jnp.concatenate(
        [jnp.concatenate([p[F_END:span], p[span : span + half]], 1) for p in (own, by_row)], 0
    )
    last = mm(active_rows, down)
    mine = lax.dynamic_slice_in_dim(last, core * out_columns, out_columns, 1)
    others = lax.dynamic_slice_in_dim(last, (1 - core) * out_columns, out_columns, 1)
    own_decoder_out = (
        lax.dynamic_slice(d_middle, (row * out_rows, core * out_columns), (out_rows, out_columns))
        + mine
        + swap(others.astype(BF16), "core").astype(F32)
    )

    grads_a = line_last(sum_a, data_size, own_input_grad)
    grads_b = line_last(sum_b, data_size, sum_d[0])
    send = call(
        decoder_send_kernel,
        "decoder_send",
        shaped(12 * LANES, LANES, BF16),
        (place, grads_a, grads_b),
        scalars=1,
        limit=8,
    )
    d_mixing_grad, d_out_grad, d_up_grad, d_down_grad, proj_grad = call(
        decoder_unpack_kernel,
        "decoder_unpack",
        (
            jax.ShapeDtypeStruct((3, LANES, 2 * LANES), F32),
            shaped(2 * LANES, LANES, F32),
            shaped(LANES, d_units, F32),
            shaped(d_units, LANES, F32),
            shaped(width, LANES, F32),
        ),
        (place, grads_a, grads_b, swap(send, "core")),
        scalars=1,
        limit=8,
        cost=1.9,
    )
    grads_c = line_last(sum_c, data_size, sum_d[0]).astype(F32)
    grads_e = line_last(sum_e, data_size, sum_d[0]).astype(F32)
    sums = dp_sum(after(sums, sum_d[0], d_down_grad, own_decoder_out), data_size)
    e_sums = lax.dynamic_slice_in_dim(sums[:4], row * width, width, 1)
    share = decoder_attention_gain.shape[0]
    d_sums = lax.dynamic_slice_in_dim(sums[4:], block * share, share, 1)
    grads_d = line_last(sum_d, data_size, d_down_grad, grads_c, grads_e)
    mixing_grad, out_grad = call(
        encoder_unpack_kernel,
        "encoder_unpack",
        (
            jax.ShapeDtypeStruct((3, width // 2, width), F32),
            shaped(width // 2, width, F32),
        ),
        (grads_d,),
        limit=8,
    )
    return (
        own_encoder_out,
        own_decoder_out,
        own_input_grad,
        e_sums[0],
        e_sums[1],
        jnp.transpose(mixing_grad, (2, 0, 1)),
        out_grad,
        e_sums[2],
        e_sums[3],
        grads_e,
        grads_c,
        proj_grad,
        d_sums[0],
        d_sums[1],
        jnp.transpose(d_mixing_grad, (1, 0, 2)),
        d_out_grad,
        d_sums[2],
        d_sums[3],
        d_up_grad,
        d_down_grad,
    )


def solution(mesh):
    data, row, col = (mesh.shape[name] for name in ("dp", "row", "col"))
    split = Mesh(mesh.devices.reshape(data, row, col // 2, 2), ("dp", "row", "y", "core"))
    c = ("y", "core")
    in_specs = (
        P(("dp", *c), "row"),
        P("dp"),
        P("row"),
        P("row"),
        P("row", None, c),
        P(c, "row"),
        P("row"),
        P("row"),
        P("row", c),
        P(c, "row"),
        P("row", c),
        P(c),
        P(c),
        P(c, None, "row"),
        P("row", c),
        P(c),
        P(c),
        P(c, "row"),
        P("row", c),
        P(("dp", "row"), c),
    )
    out_specs = (
        P(("dp", *c), "row"),
        P(("dp", "row"), c),
        P(("dp", *c), "row"),
        P("row"),
        P("row"),
        P("row", None, c),
        P(c, "row"),
        P("row"),
        P("row"),
        P("row", c),
        P(c, "row"),
        P("row", c),
        P(c),
        P(c),
        P(c, None, "row"),
        P("row", c),
        P(c),
        P(c),
        P(c, "row"),
        P("row", c),
    )
    return jax.shard_map(
        functools.partial(per_device, data),
        mesh=split,
        in_specs=in_specs,
        out_specs=out_specs,
        check_vma=False,
    )
```

```python
import functools
import math

import jax
import jax.numpy as jnp
from jax import lax
from jax.experimental import pallas as pl
from jax.experimental.pallas import tpu as pltpu
from jax.sharding import Mesh, PartitionSpec as P

D1 = 768
D2 = 512
HD1 = 64
HD2 = 32
EPSILON = 1e-06
BLOCK = 512
LANES = 128
LOG2E = 1.4426950408889634
SWAP = [(0, 1), (1, 0)]
BF16 = jnp.bfloat16
F32 = jnp.float32


def mm(left, right):
    return jnp.dot(left, right, preferred_element_type=F32)


def mm_nt(left, right):
    return lax.dot_general(left, right, (((1,), (1,)), ((), ())), preferred_element_type=F32)


def mm_tn(left, right):
    return lax.dot_general(left, right, (((0,), (0,)), ((), ())), preferred_element_type=F32)


def head_lanes(head, head_size, rows):
    lane = lax.broadcasted_iota(jnp.int32, (rows, LANES), 1)
    return (lane >= head * head_size) & (lane < (head + 1) * head_size)


def attention_backward_kernel(
    head_size,
    pairs,
    lanes,
    mixed_ref,
    att_all_ref,
    inv_all_ref,
    grad_all_ref,
    limit_ref,
    dq_ref,
    dk_ref,
    dv_ref,
    vaug_ref,
    naug_ref,
    dq_acc,
    dk_acc,
    dv_acc,
):
    q_ref, k_ref, v_ref = (mixed_ref.at[:, pl.ds(start, LANES)] for start in lanes)
    att_ref, inv_ref, grad_ref = (
        ref.at[:, pl.ds(lanes[0], LANES)] for ref in (att_all_ref, inv_all_ref, grad_all_ref)
    )
    length = q_ref.shape[0]
    heads = LANES // head_size
    scaling = head_size ** (-0.5)

    lane = lax.broadcasted_iota(jnp.int32, (length, LANES), 1)
    vaug_ref[:, :LANES] = v_ref[...]
    vaug_ref[:, LANES:] = jnp.where(lane < 2, 1.0, 0.0).astype(BF16)
    scaled = grad_ref[...] * inv_ref[...]
    terms = scaled * att_ref[...].astype(F32)
    low = scaled.astype(BF16)
    for head in range(heads):
        own = head_lanes(head, head_size, length)
        total = -jnp.sum(jnp.where(own, terms, 0.0), 1, keepdims=True)
        high = total.astype(BF16).astype(F32)
        rest = total - high
        naug_ref[head, :, :LANES] = jnp.where(own, low, jnp.zeros_like(low))
        naug_ref[head, :, LANES:] = jnp.where(
            lane == 0, high, jnp.where(lane == 1, rest, 0.0)
        ).astype(BF16)
    dq_acc[...] = jnp.zeros_like(dq_acc)
    dk_acc[...] = jnp.zeros_like(dk_acc)
    dv_acc[...] = jnp.zeros_like(dv_acc)

    def run(key_block, query_block):
        keys = slice(key_block * BLOCK, (key_block + 1) * BLOCK)
        queries = slice(query_block * BLOCK, (query_block + 1) * BLOCK)
        key_rows = k_ref[keys, :]
        query_rows = q_ref[queries, :]
        key_flipped = key_rows.astype(F32).T.astype(BF16)
        if key_block == query_block:
            places = key_block * BLOCK + lax.broadcasted_iota(jnp.int32, (BLOCK, BLOCK), 0)
            visible = places <= limit_ref[:, queries]
        dq = jnp.zeros((LANES, BLOCK), F32)
        dk = jnp.zeros((BLOCK, LANES), F32)
        dv = jnp.zeros((BLOCK, LANES), F32)
        for head in range(heads):
            own = head_lanes(head, head_size, BLOCK)
            masked = jnp.where(own, query_rows, jnp.zeros_like(query_rows))
            weights = jnp.exp2(mm_nt(key_rows, masked) * (scaling * LOG2E))
            if key_block == query_block:
                weights = jnp.where(visible, weights, 0.0)
            naug = naug_ref[head, queries, :]
            slopes = mm_nt(vaug_ref[keys, :], naug)
            scores = (weights * slopes).astype(BF16)
            dv += mm(weights.astype(BF16), naug[:, :LANES])
            dk += mm(scores, masked)
            row = lax.broadcasted_iota(jnp.int32, (LANES, BLOCK), 0)
            mine = (row >= head * head_size) & (row < (head + 1) * head_size)
            dq += mm(jnp.where(mine, key_flipped, jnp.zeros_like(key_flipped)), scores)
        dq_acc[:, queries] += dq
        dk_acc[keys, :] += dk
        dv_acc[keys, :] += dv

    for key_block, query_block in pairs:
        run(key_block, query_block)
    dq_ref[...] = (dq_acc[...].T * scaling).astype(BF16)
    dk_ref[...] = (dk_acc[...] * scaling).astype(BF16)
    dv_ref[...] = dv_acc[...].astype(BF16)


def attention_backward(
    mixed, attended, inverse, grad, limits_row, head_size, start=0, count=None
):
    length, width = attended.shape
    groups = width // LANES
    count = groups if count is None else count
    blocks = length // BLOCK
    pairs = [(k, q) for q in range(blocks) for k in range(q + 1)]
    lanes = tuple((kind * groups + start) * LANES for kind in range(3))
    memory = pl.BlockSpec(memory_space=pltpu.VMEM)
    results = pl.pallas_call(
        functools.partial(attention_backward_kernel, head_size, pairs, lanes),
        out_shape=(jax.ShapeDtypeStruct((length, LANES), BF16),) * 3,
        in_specs=[memory] * 5,
        out_specs=[memory] * 3,
        scratch_shapes=[
            pltpu.VMEM((length, 2 * LANES), BF16),
            pltpu.VMEM((LANES // head_size, length, 2 * LANES), BF16),
            pltpu.VMEM((LANES, length), F32),
            pltpu.VMEM((length, LANES), F32),
            pltpu.VMEM((length, LANES), F32),
        ],
        compiler_params=pltpu.CompilerParams(vmem_limit_bytes=16 << 20),
        cost_estimate=pl.CostEstimate(
            flops=int(count * (5.2 if head_size == HD1 else 9.6) * COST), bytes_accessed=1, transcendentals=0
        ),
        name="attention_backward",
    )(mixed, attended, inverse, grad, limits_row)
    return tuple(results)


def swap(value, axis):
    return lax.ppermute(value, axis, SWAP)


def after(value, *others):
    return lax.optimization_barrier((value, *others))[0]


def near(pack):
    return (swap(pack, "row"), swap(pack, "y"))


def across_by_row(pair, *others):
    return swap(after(pair[0], *others), "y")


def across_by_y(pair, *others):
    return swap(after(pair[1], *others), "row")


def across_direct(pack):
    return lax.ppermute(pack, ("row", "y"), [(i, 3 - i) for i in range(4)])


def across_both(pair, split, *others):
    first, second = after((pair[0][:split], pair[1][split:]), *others)
    return (swap(first, "y"), swap(second, "row"))


class Parts:
    def __init__(self, refs, start=0, far=None):
        own, by_row, by_y, across = refs
        self.refs = ((own, by_y), (by_row, across))
        self.start = start
        self.far = start if far is None else far

    def rows(self, by_row, by_y, base, count, offset=0):
        start = self.far if by_row and by_y else self.start
        return self.refs[by_row][by_y][pl.ds(start + base + offset, count), :]


class Pair:
    def __init__(self, refs, split):
        own, by_row, by_y, first, second = refs
        self.first = Parts((own, by_row, by_y, first))
        self.second = Parts((own, by_row, by_y, second), split, 0)


COST = 1e7
VMEM = pl.BlockSpec(memory_space=pltpu.VMEM)
SMEM = pl.BlockSpec(memory_space=pltpu.SMEM)


def call(
    kernel, name, outs, args, scratch=(), scalars=0, limit=48, cost=1, needs=(), marks=(), fetch=False
):
    count = len(args)
    arrays = count - scalars
    if needs:
        args = (*args[:scalars], after(args[scalars], *needs), *args[scalars + 1 :])
    scratch = list(scratch)
    if fetch:
        scratch += [pltpu.VMEM(a.shape, a.dtype) for a in args[scalars:]]
        scratch.append(pltpu.SemaphoreType.DMA((arrays,)))

    def body(*refs):
        given, rest = refs[:count], refs[count + len(marks) :]
        if fetch:
            local, semaphores, rest = rest[-arrays - 1 : -1], rest[-1], rest[: -arrays - 1]
            copies = [
                pltpu.make_async_copy(source, target, semaphores.at[i])
                for i, (source, target) in enumerate(zip(given[scalars:], local))
            ]
            for copy in copies:
                copy.start()
            for copy in copies:
                copy.wait()
            given = (*given[:scalars], *local)
        kernel(*given, *rest)

    place = pl.BlockSpec(memory_space=pltpu.HBM) if fetch else VMEM
    return pl.pallas_call(
        body,
        out_shape=outs,
        in_specs=[SMEM] * scalars + [place] * arrays + [VMEM] * len(marks),
        out_specs=jax.tree.map(lambda _: VMEM, outs),
        scratch_shapes=scratch,
        compiler_params=pltpu.CompilerParams(vmem_limit_bytes=limit << 20),
        cost_estimate=pl.CostEstimate(
            flops=int(cost * COST), bytes_accessed=1, transcendentals=0
        ),
        name=name,
    )(*args, *marks)


def marker_kernel(in_ref, out_ref):
    out_ref[...] = in_ref[...]


def marker(value, cost, *others):
    return call(
        marker_kernel,
        "marker",
        jax.ShapeDtypeStruct(value.shape, value.dtype),
        (value,),
        cost=cost,
        limit=4,
        needs=others,
    )


def shaped(rows, columns, kind):
    return jax.ShapeDtypeStruct((rows, columns), kind)


def store_three(ref, base, vectors):
    for tile in range(vectors[0].shape[0]):
        values = jnp.concatenate([v[tile : tile + 1, :] for v in vectors], 0)
        high = values.astype(BF16)
        rest = values - high.astype(F32)
        middle = rest.astype(BF16)
        low = (rest - middle.astype(F32)).astype(BF16)
        ref[base + 16 * tile : base + 16 * (tile + 1), :] = jnp.concatenate(
            [high, middle, low, jnp.zeros_like(high)], 0
        )


def join_three(rows):
    wide = rows.astype(F32)
    return wide[0:4] + wide[4:8] + wide[8:12]


TILE = 256
FEED = 512


def lane_roll(values):
    return pltpu.roll(values.astype(F32), LANES // 2, 1)


HALF = LANES // 2
E_ROWS = 3 * LANES
A_LAST = 2 * E_ROWS
A_VEC = 3 * E_ROWS
A_END = A_VEC + 48
B_REST = E_ROWS
B_OUT = B_REST + E_ROWS // 2
B_END = 3 * E_ROWS
E_FEED = 18 * LANES
DA_VEC = 6 * LANES
DA_END = DA_VEC + 32
DB_PROJ = 2 * LANES
DB_END = 8 * LANES
F_COT = 8 * LANES
F_END = 12 * LANES
D_SEND = 19 * LANES + 16


def pack_mixing_kernel(w_ref, out_ref, v1, v2, v3, v4, pack_ref):
    store_three(pack_ref, A_VEC, (v1, v2, v3, v4))
    rows = w_ref.shape[2]
    parts = [w_ref[kind].astype(F32).T.astype(BF16) for kind in range(3)]
    pack_ref[:rows, :] = parts[0][:, :LANES]
    pack_ref[rows : 2 * rows, :] = parts[1][:, :LANES]
    pack_ref[A_LAST:A_VEC, :HALF] = parts[0][:, LANES:]
    pack_ref[A_LAST:A_VEC, HALF:] = parts[1][:, LANES:]
    pack_ref[A_END : A_END + rows, :] = parts[2][:, :LANES]
    rest = A_END + B_REST
    pack_ref[rest : rest + rows // 2, :HALF] = parts[2][: rows // 2, LANES:]
    pack_ref[rest : rest + rows // 2, HALF:] = parts[2][rows // 2 :, LANES:]
    heads = out_ref.shape[0]
    base = A_END + B_OUT
    for tile in range(3):
        pack_ref[base + tile * heads : base + (tile + 1) * heads, :] = out_ref[
            :, tile * LANES : (tile + 1) * LANES
        ]


def pack_encoder_kernel(up_ref, down_ref, pack_ref):
    base = 0
    for weight_ref in (up_ref, down_ref):
        rows, columns = weight_ref.shape
        for tile in range(columns // LANES):
            pack_ref[base : base + rows, :] = weight_ref[:, tile * LANES : (tile + 1) * LANES]
            base += rows


def pack_decoder_kernel(
    place_ref, mix_ref, out_ref, up_ref, down_ref, v1, v2, v3, v4, proj_ref, cot_ref, keep_ref, send_ref
):
    core = place_ref[0]
    rows = mix_ref.shape[1]
    units = up_ref.shape[1] // 2
    for target, half in ((keep_ref, core), (send_ref, 1 - core)):
        base = 0
        for i in range(3):
            target[base : base + rows, :] = mix_ref[i, :, pl.ds(half * LANES, LANES)]
            base += rows
        target[base : base + LANES, :] = out_ref[pl.ds(half * LANES, LANES), :]
        base += LANES
        for i in range(units // LANES):
            target[base : base + rows, :] = up_ref[:, pl.ds(half * units + i * LANES, LANES)]
            base += rows
        target[base : base + units, :] = down_ref[pl.ds(half * units, units), :]
        base += units
        target[base : base + 3 * LANES, :] = proj_ref[...]
        base += 3 * LANES
        target[base : base + 4 * LANES, :] = cot_ref[...]
        base += 4 * LANES
        store_three(target, base, (v1, v2, v3, v4))


def join_decoder_kernel(place_ref, keep_ref, got_ref, mix_ref, feed_ref):
    core = place_ref[0]
    rows = LANES
    for source, side in ((keep_ref, core), (got_ref, 1 - core)):
        base = 0
        for i in range(3):
            mix_ref[pl.ds(2 * i * rows + side * rows, rows), :] = source[base : base + rows, :]
            base += rows
        mix_ref[pl.ds(DA_END + side * rows, rows), :] = source[base : base + rows, :]
        base += rows
        for i in range(4):
            feed_ref[pl.ds(2 * i * rows + side * rows, rows), :] = source[base : base + rows, :]
            base += rows
        feed_ref[pl.ds(F_END + side * 4 * rows, 4 * rows), :] = source[base : base + 4 * rows, :]
        base += 4 * rows
        mix_ref[pl.ds(DA_END + DB_PROJ + side * 3 * rows, 3 * rows), :] = source[
            base : base + 3 * rows, :
        ]
        base += 3 * rows
        for start in (F_COT, F_END + F_COT):
            feed_ref[pl.ds(start + side * 2 * rows, 2 * rows), :] = source[base : base + 2 * rows, :]
            base += 2 * rows
        mix_ref[pl.ds(DA_VEC + side * 16, 16), :] = source[base : base + 16, :]


def join_input_kernel(place_ref, own, by_row, by_y, first, second, out_ref):
    y = place_ref[3]
    width = own.shape[1]
    split = second.shape[0]
    for right, by_y_side, sources in (
        (0, 0, (own, own)),
        (1, 0, (by_row, by_row)),
        (0, 1, (by_y, by_y)),
        (1, 1, (first, second)),
    ):
        base = (y if by_y_side == 0 else 1 - y) * 2 * split
        for number, source in enumerate(sources):
            start = 0 if source is second else number * first.shape[0]
            at = pl.ds(base + number * split, split)
            out_ref[at, right * width : (right + 1) * width] = source[start : start + split, :]


def norm_rows(values):
    width = values.shape[1]
    average = jnp.sum(values, 1, keepdims=True) / width
    variance = jnp.sum(values * values, 1, keepdims=True) / width - average * average
    inverse = lax.rsqrt(variance + EPSILON)
    return ((values - average) * inverse, inverse)


def first_norm_kernel(core_ref, own, other, vec_own, vec_other, x_ref, normed_ref, vec_ref):
    core = core_ref[0]
    for side, source in ((0, vec_own), (3, vec_other)):
        for tile in range(3):
            vec_ref[:, (side + tile) * LANES : (side + tile + 1) * LANES] = join_three(
                source[A_VEC + 16 * tile : A_VEC + 16 * (tile + 1), :]
            )
    rows = own.shape[0] // 2
    gain, bias = vec_ref[0:1, :], vec_ref[1:2, :]
    for source, place in ((own, core), (other, 1 - core)):
        for y in range(2):
            values = source[y * rows : (y + 1) * rows, :]
            target = pl.ds((2 * y + place) * rows, rows)
            x_ref[target, :] = values
            centred, _ = norm_rows(values.astype(F32))
            normed_ref[target, :] = (centred * gain + bias).astype(BF16)


def encoder_mixing_kernel(normed_ref, *refs):
    pair = Pair(refs[:5], A_END)
    first, second = pair.first, pair.second
    mixed_ref, weight_ref, out_ref = refs[5:8]
    out_ref[...] = encoder_out_rows(second)
    rows = E_ROWS
    low = lax.broadcasted_iota(jnp.int32, (rows, LANES), 1) < HALF
    for half in range(2):
        at = slice(half * rows, (half + 1) * rows)
        for kind, parts, base in ((0, first, 0), (1, first, rows), (2, second, 0)):
            for group, side in ((0, 0), (2, 1)):
                tile = (3 * kind + group) * LANES
                weight_ref[at, tile : tile + LANES] = parts.rows(half, side, base, rows)
        mine = first.rows(half, 0, A_LAST, rows).astype(F32)
        theirs = first.rows(half, 1, A_LAST, rows).astype(F32)
        weight_ref[at, LANES : 2 * LANES] = jnp.where(low, mine, lane_roll(theirs)).astype(BF16)
        weight_ref[at, 4 * LANES : 5 * LANES] = jnp.where(low, lane_roll(mine), theirs).astype(BF16)
        mine = second.rows(half, 0, B_REST, rows // 2).astype(F32)
        theirs = second.rows(half, 1, B_REST, rows // 2).astype(F32)
        mine = jnp.concatenate([mine, lane_roll(mine)], 0)
        theirs = jnp.concatenate([lane_roll(theirs), theirs], 0)
        weight_ref[at, 7 * LANES : 8 * LANES] = jnp.where(low, mine, theirs).astype(BF16)

    @pl.loop(0, normed_ref.shape[0] // FEED)
    def _(tile):
        at = pl.ds(tile * FEED, FEED)
        mixed_ref[at, :] = mm(normed_ref[at, :], weight_ref[...]).astype(BF16)


def encoder_out_rows(parts):
    heads = 3 * LANES // 2
    sides = [
        jnp.concatenate(
            [parts.rows(i, j, B_OUT + t * heads, heads) for i in range(2) for t in range(3)], 1
        )
        for j in range(2)
    ]
    return jnp.concatenate([sides[0], sides[1][LANES:], sides[1][:LANES]], 0)


def decoder_out_rows(parts):
    return jnp.concatenate(
        [
            jnp.concatenate(
                [parts.rows(i, j, t * LANES, LANES) for j in range(2) for t in range(2)], 1
            )
            for i in range(2)
        ],
        0,
    )


def attend_kernel(
    head_size, mixed_ref, limit_ref, weight_ref, attended_ref, inverse_ref, partial_ref, aug_ref
):
    length, width = attended_ref.shape
    groups, heads = width // LANES, LANES // head_size
    scale = head_size ** (-0.5) * LOG2E
    for group in range(groups):
        at = (2 * groups + group) * LANES
        aug_ref[group, :, :LANES] = mixed_ref[:, at : at + LANES]
        aug_ref[group, :, LANES:] = jnp.ones((length, LANES), BF16)

    for block in range(length // BLOCK):

        @pl.loop(0, BLOCK // FEED)
        def _(step):
            at = pl.ds(block * BLOCK + step * FEED, FEED)
            limits = limit_ref[at, :]
            places = block * BLOCK + lax.broadcasted_iota(jnp.int32, (FEED, BLOCK), 1)
            visible = places <= limits

            @pl.loop(0, groups * heads // 2)
            def _(step):
                group, pair = step // (heads // 2), step % (heads // 2)
                lanes = pl.ds(pl.multiple_of(group * LANES, LANES), LANES)
                queries = mixed_ref[at, lanes]
                result = attended_ref[at, lanes]
                inverses = inverse_ref[at, lanes]
                lane = lax.broadcasted_iota(jnp.int32, (FEED, LANES), 1)
                for number in range(2):
                    start = (2 * pair + number) * head_size
                    own = (lane >= start) & (lane < start + head_size)
                    masked = jnp.where(own, queries, jnp.zeros_like(queries))
                    total = jnp.zeros((FEED, 2 * LANES), F32)
                    for part in range(block + 1):
                        span = slice(part * BLOCK, (part + 1) * BLOCK)
                        keys = mixed_ref[span, pl.ds((groups + group) * LANES, LANES)]
                        weights = jnp.exp2(mm_nt(masked, keys) * scale)
                        if part == block:
                            weights = jnp.where(visible, weights, 0.0)
                        total = total + mm(weights.astype(BF16), aug_ref[group, span, :])
                    inverse = 1.0 / total[:, LANES:]
                    result = jnp.where(own, (total[:, :LANES] * inverse).astype(BF16), result)
                    inverses = jnp.where(own, inverse, inverses)
                attended_ref[at, lanes] = result
                inverse_ref[at, lanes] = inverses

            partial_ref[at, :] = mm(attended_ref[at, :], weight_ref[...]).astype(BF16)


def gelu_pair(values):
    area = 0.5 * (1.0 + lax.erf(values * (0.5**0.5)))
    slope = area + values * jnp.exp2(values * values * (-0.5 * LOG2E)) * (0.5 / math.pi) ** 0.5
    return (values * area, slope)


class Feed:
    def __init__(self, up_parts, down_parts, decoder):
        self.up_parts = up_parts
        self.down_parts = down_parts
        self.decoder = decoder
        self.features = 2 * LANES if decoder else 3 * LANES
        self.units = 4 * LANES if decoder else 6 * LANES
        self.down = 0
        self.chunks = self.units // (2 * LANES)

    def rows(self, parts, feature, unit, base, count, offset):
        if self.decoder:
            return parts.rows(unit, feature, base, count, offset)
        return parts.rows(feature, unit, base, count, offset)

    def up_chunk(self, unit, chunk):
        f = self.features
        return jnp.concatenate(
            [
                jnp.concatenate(
                    [
                        self.rows(
                            self.up_parts, i, unit, 0, f, pl.multiple_of((2 * chunk + t) * f, f)
                        )
                        for t in range(2)
                    ],
                    1,
                )
                for i in range(2)
            ],
            0,
        )

    def up_both(self, chunk):
        return jnp.concatenate([self.up_chunk(unit, chunk) for unit in range(2)], 1)

    def down_both(self, chunk):
        return jnp.concatenate([self.down_chunk(unit, chunk) for unit in range(2)], 0)

    def down_chunk(self, unit, chunk):
        return jnp.concatenate(
            [
                self.rows(
                    self.down_parts,
                    i,
                    unit,
                    self.down + t * self.units,
                    2 * LANES,
                    pl.multiple_of(chunk * 2 * LANES, 2 * LANES),
                )
                for i in range(2)
                for t in range(self.features // LANES)
            ],
            1,
        )


def feed_forward_kernel(stream_ref, mine_ref, got_ref, vec_ref, *refs):
    middle_ref, normed_ref, active_ref, slope_ref, partial_ref, total_ref = refs[5:11]
    pair = Pair(refs[:5], E_FEED)
    feed = Feed(pair.first, pair.second, False)
    gain, bias = vec_ref[2:3, :], vec_ref[3:4, :]

    @pl.loop(0, stream_ref.shape[0] // FEED)
    def _(tile):
        at = pl.ds(tile * FEED, FEED)
        middle = stream_ref[at, :].astype(F32) + (
            mine_ref[at, :].astype(F32) + got_ref[at, :].astype(F32)
        )
        middle_ref[at, :] = middle
        centred, _ = norm_rows(middle)
        normed_ref[at, :] = (centred * gain + bias).astype(BF16)
        total_ref[...] = jnp.zeros_like(total_ref)

        @pl.loop(0, feed.chunks)
        def _(chunk):
            hidden = mm(normed_ref[at, :], feed.up_both(chunk))
            active, slope = gelu_pair(hidden)
            low = active.astype(BF16)
            slope = slope.astype(BF16)
            for unit in range(2):
                lanes = pl.ds(unit * feed.units + chunk * 2 * LANES, 2 * LANES)
                part = slice(unit * 2 * LANES, (unit + 1) * 2 * LANES)
                active_ref[at, lanes] = low[:, part]
                slope_ref[at, lanes] = slope[:, part]
            total_ref[...] += mm(low, feed.down_both(chunk))

        partial_ref[at, :] = total_ref[...].astype(BF16)


def decoder_feed_kernel(
    place_ref, stream_ref, mine_ref, got_ref, vec_ref, *refs
):
    middle_ref, normed_ref, active_ref, hidden_ref, partial_ref, cot_ref, total_ref = refs[4:11]
    first, second = Parts(refs[:4]), Parts(refs[:4], F_END)
    row = place_ref[2]
    for i in range(2):
        for number, parts in enumerate((first, second)):
            at = pl.ds((row if i == 0 else 1 - row) * 4 * LANES + number * 2 * LANES, 2 * LANES)
            for tile in range(4):
                cot_ref[at, tile * LANES : (tile + 1) * LANES] = parts.rows(
                    i, tile // 2, F_COT + (tile % 2) * 2 * LANES, 2 * LANES
                )
    feed = Feed(first, second, True)
    gain, bias = vec_ref[2:3, :], vec_ref[3:4, :]

    @pl.loop(0, stream_ref.shape[0] // FEED)
    def _(tile):
        at = pl.ds(tile * FEED, FEED)
        middle = stream_ref[at, :] + (mine_ref[at, :].astype(F32) + got_ref[at, :].astype(F32))
        middle_ref[at, :] = middle
        centred, _ = norm_rows(middle)
        normed_ref[at, :] = (centred * gain + bias).astype(BF16)
        total_ref[...] = jnp.zeros_like(total_ref)

        @pl.loop(0, feed.chunks)
        def _(chunk):
            upward = feed.up_both(chunk)
            hidden = mm(normed_ref[at, :], upward)
            active, slope = gelu_pair(hidden)
            active = active.astype(BF16)
            grad = mm_nt(cot_ref[at, :], feed.down_both(chunk))
            low = (grad * slope).astype(BF16)
            for unit in range(2):
                lanes = pl.ds(unit * feed.units + chunk * 2 * LANES, 2 * LANES)
                part = slice(unit * 2 * LANES, (unit + 1) * 2 * LANES)
                active_ref[at, lanes] = active[:, part]
                hidden_ref[at, lanes] = low[:, part]
            total_ref[...] += mm_nt(low, upward)

        partial_ref[at, :] = total_ref[...].astype(BF16)


def bridge_kernel(place_ref, middle_ref, mine_ref, got_ref, *refs):
    (
        out_ref, low_ref, stream_ref, normed_ref, mixed_ref, weight_ref, vec_ref, mixing_ref,
        back_ref,
    ) = refs[5:14]
    block = place_ref[1]
    pair = Pair(refs[:5], DA_END)
    first, second = pair.first, pair.second
    back_ref[...] = decoder_out_rows(second)
    rows = E_ROWS
    for j in range(2):
        for c in range(2):
            tile = (2 * j + c) * LANES
            for i in range(2):
                weight_ref[i * rows : (i + 1) * rows, tile : tile + LANES] = second.rows(
                    i, j, DB_PROJ + c * rows, rows
                )
            vec_ref[:, tile : tile + LANES] = join_three(first.rows(0, j, DA_VEC + 16 * c, 16))
    for kind in range(3):
        for i in range(2):
            tile = (2 * kind + i) * LANES
            for j in range(2):
                mixing_ref[2 * j * LANES : 2 * (j + 1) * LANES, tile : tile + LANES] = first.rows(
                    i, j, 2 * kind * LANES, 2 * LANES
                )
    gain, bias = vec_ref[0:1, :], vec_ref[1:2, :]
    width = low_ref.shape[1]

    @pl.loop(0, middle_ref.shape[0] // FEED)
    def _(tile):
        at = pl.ds(tile * FEED, FEED)
        total = middle_ref[at, :] + (mine_ref[at, :].astype(F32) + got_ref[at, :].astype(F32))
        low = total.astype(BF16)

        for part in range(FEED // TILE):

            @pl.when(tile * (FEED // TILE) + part == block)
            def _():
                out_ref[...] = total[part * TILE : (part + 1) * TILE, :width]

        low_ref[at, :] = low[:, :width]
        stream = mm(low, weight_ref[...])
        stream_ref[at, :] = stream
        centred, _ = norm_rows(stream)
        normed = (centred * gain + bias).astype(BF16)
        normed_ref[at, :] = normed
        mixed_ref[at, :] = mm(normed, mixing_ref[...]).astype(BF16)


def norm_back(incoming, centred, inverse, gain):
    width = incoming.shape[1]
    scaled = incoming * gain
    first = jnp.sum(scaled, 1, keepdims=True) / width
    second = jnp.sum(scaled * centred, 1, keepdims=True) / width
    return inverse * (scaled - first - centred * second)


def store_sums(sums_ref, incoming, centred):
    sums_ref[0:1, :] = jnp.sum(incoming * centred, 0, keepdims=True)
    sums_ref[1:2, :] = jnp.sum(incoming, 0, keepdims=True)


def own_sums(place_ref, tile, sums_ref, incoming, centred):
    half = TILE // 2

    @pl.when((tile == place_ref[1]) & (place_ref[2] == 0))
    def _():
        store_sums(sums_ref, incoming[:half], centred[:half])

    @pl.when((tile == place_ref[1]) & (place_ref[2] == 1))
    def _():
        store_sums(sums_ref, incoming[half:], centred[half:])


def middle_back_kernel(
    place_ref, mine_ref, got_ref, middle_ref, grad_ref, vec_ref, weight_ref,
    total_ref, low_ref, attended_ref, sums_ref,
):
    gain = vec_ref[2:3, :]
    width = low_ref.shape[1]

    @pl.loop(0, middle_ref.shape[0] // TILE)
    def _(tile):
        at = pl.ds(tile * TILE, TILE)
        incoming = mine_ref[at, :].astype(F32) + got_ref[at, :].astype(F32)
        centred, inverse = norm_rows(middle_ref[at, :])
        total = grad_ref[at, :].astype(F32) + norm_back(incoming, centred, inverse, gain)
        if total_ref.shape[0] == TILE:

            @pl.when(tile == place_ref[1])
            def _():
                total_ref[...] = total
        else:
            total_ref[at, :] = total
        low = total.astype(BF16)
        low_ref[at, :] = low[:, :width]
        attended_ref[at, :] = mm_nt(low, weight_ref[...])
        own_sums(place_ref, tile, sums_ref, incoming, centred)


def mixed_low(refs, at):
    kinds = len(refs) // 3
    return jnp.concatenate([refs[3 * g + i][at, :] for i in range(3) for g in range(kinds)], 1)


def mixed_back_kernel(*refs):
    lows, weight_ref, partial_ref = refs[:-2], refs[-2], refs[-1]

    @pl.loop(0, partial_ref.shape[0] // FEED)
    def _(tile):
        at = pl.ds(tile * FEED, FEED)
        partial_ref[at, :] = mm_nt(mixed_low(lows, at), weight_ref[...]).astype(BF16)


def mixed_last_kernel(place_ref, *refs):
    core, y = place_ref[0], place_ref[3]
    lows, weight_ref, keep_ref, send_ref = refs[:-3], refs[-3], refs[-2], refs[-1]
    for target, side in ((keep_ref, core), (send_ref, 1 - core)):
        at = pl.ds((2 * y + side) * TILE, TILE)
        target[...] = mm_nt(mixed_low(lows, at), weight_ref[...]).astype(BF16)


def bridge_back_kernel(
    place_ref, mine_ref, got_ref, stream_ref, grad_ref, vec_ref, proj_ref,
    low_ref, encoder_ref, down_ref, sums_ref,
):
    gain = vec_ref[0:1, :]

    @pl.loop(0, stream_ref.shape[0] // TILE)
    def _(tile):
        at = pl.ds(tile * TILE, TILE)
        incoming = mine_ref[at, :].astype(F32) + got_ref[at, :].astype(F32)
        centred, inverse = norm_rows(stream_ref[at, :])
        grad = grad_ref[at, :] + norm_back(incoming, centred, inverse, gain)
        own_sums(place_ref, tile, sums_ref, incoming, centred)
        low = grad.astype(BF16)
        low_ref[at, :] = low
        encoder = mm_nt(low, proj_ref[...])
        encoder_ref[at, :] = encoder
        down_ref[at, :] = encoder.astype(BF16)


def feed_back_kernel(down_ref, slope_ref, *refs):
    hidden_ref, partial_ref, total_ref = refs[5:8]
    pair = Pair(refs[:5], E_FEED)
    feed = Feed(pair.first, pair.second, False)

    @pl.loop(0, down_ref.shape[0] // FEED)
    def _(tile):
        at = pl.ds(tile * FEED, FEED)
        total_ref[...] = jnp.zeros_like(total_ref)

        @pl.loop(0, feed.chunks)
        def _(chunk):
            back = mm_nt(down_ref[at, :], feed.down_both(chunk))
            parts = []
            for unit in range(2):
                lanes = pl.ds(unit * feed.units + chunk * 2 * LANES, 2 * LANES)
                part = slice(unit * 2 * LANES, (unit + 1) * 2 * LANES)
                hidden = (back[:, part] * slope_ref[at, lanes].astype(F32)).astype(BF16)
                hidden_ref[at, lanes] = hidden
                parts.append(hidden)
            total_ref[...] += mm_nt(jnp.concatenate(parts, 1), feed.up_both(chunk))

        partial_ref[at, :] = total_ref[...].astype(BF16)


def input_back_kernel(place_ref, mine_ref, got_ref, x_ref, grad_ref, vec_ref, out_ref, sums_ref):
    at = pl.ds(place_ref[1] * TILE, TILE)
    incoming = mine_ref[...].astype(F32) + got_ref[...].astype(F32)
    centred, inverse = norm_rows(x_ref[at, :].astype(F32))
    total = grad_ref[...] + norm_back(incoming, centred, inverse, vec_ref[0:1, :])
    out_ref[...] = total[:, : out_ref.shape[1]]
    own_sums(place_ref, place_ref[1], sums_ref, incoming, centred)


def store_tiles(ref, base, value):
    rows = value.shape[0]
    for tile in range(value.shape[1] // LANES):
        ref[base + tile * rows : base + (tile + 1) * rows, :] = value[
            :, tile * LANES : (tile + 1) * LANES
        ].astype(BF16)


G_LAST = 3 * E_ROWS
G_REST = 4 * E_ROWS
G_OUT = G_REST + E_ROWS // 2
G_END = 6 * E_ROWS
GA_UP = 8 * LANES
GA_END = 16 * LANES
GB_OUT = 6 * LANES
GB_PROJ = 8 * LANES
GB_END = 11 * LANES


def feed_grads_kernel(active_ref, cot_ref, normed_ref, hidden_ref, pack_ref):
    units, features = 4 * LANES, 2 * LANES
    store_tiles(pack_ref, 0, mm_tn(active_ref[:, :units], cot_ref[:, :features]))
    store_tiles(pack_ref, GA_UP, mm_tn(normed_ref[:, :features], hidden_ref[:, :units]))


def mixing_grads_kernel(
    place_ref, normed_ref, q_ref, k_ref, v_ref, attended_ref, middle_ref, encoder_ref, proj_ref, pack_ref
):
    lows = jnp.concatenate([q_ref[:, :LANES], k_ref[:, :LANES], v_ref[:, :LANES]], 1)
    store_tiles(pack_ref, 0, mm_tn(normed_ref[:, : 2 * LANES], lows))
    store_tiles(pack_ref, GB_OUT, mm_tn(attended_ref[:, :LANES], middle_ref[...]))
    own = proj_ref[:, pl.ds(place_ref[0] * LANES, LANES)]
    store_tiles(pack_ref, GB_PROJ, mm_tn(encoder_ref[...], own))


def product_kernel(left_ref, right_ref, out_ref):
    rows, columns = out_ref.shape
    out_ref[...] = mm_tn(left_ref[:, :rows], right_ref[:, :columns]).astype(BF16)


def encoder_grads_kernel(
    normed_ref, q_ref, k_ref, v_ref, q2_ref, k2_ref, v2_ref, attended_ref, middle_ref, pack_ref
):
    low = lax.broadcasted_iota(jnp.int32, q2_ref.shape, 1) < HALF
    last = jnp.where(low, q2_ref[...].astype(F32), lane_roll(k2_ref[...])).astype(BF16)
    lows = jnp.concatenate([q_ref[...], k_ref[...], v_ref[...], last, v2_ref[...]], 1)
    grads = mm_tn(normed_ref[:, :E_ROWS], lows)
    store_tiles(pack_ref, 0, grads[:, : 4 * LANES])
    rest = grads[:, 4 * LANES :]
    half = E_ROWS // 2
    low = lax.broadcasted_iota(jnp.int32, (half, LANES), 1) < HALF
    pack_ref[G_REST:G_OUT, :] = jnp.where(low, rest[:half], lane_roll(rest[half:])).astype(BF16)
    grads = mm_tn(attended_ref[:, : 2 * LANES], middle_ref[...])
    store_tiles(pack_ref, G_OUT, grads[:half])


def encoder_unpack_kernel(pack_ref, mixing_ref, out_ref):
    rows, half = E_ROWS, E_ROWS // 2
    for kind in range(3):
        mixing_ref[kind, :LANES, :] = pack_ref[kind * rows : (kind + 1) * rows, :].astype(F32).T
    last = pack_ref[G_LAST:G_REST, :].astype(F32).T
    mixing_ref[0, LANES:, :] = last[:HALF]
    mixing_ref[1, LANES:, :] = last[HALF:]
    rest = pack_ref[G_REST:G_OUT, :].astype(F32).T
    mixing_ref[2, LANES:, :] = jnp.concatenate([rest[:HALF], rest[HALF:]], 1)
    for tile in range(3):
        at = slice(G_OUT + tile * half, G_OUT + (tile + 1) * half)
        out_ref[:, tile * LANES : (tile + 1) * LANES] = pack_ref[at, :].astype(F32)


def decoder_send_kernel(place_ref, feed_ref, mix_ref, send_ref):
    other = 1 - place_ref[0]
    rows = LANES
    send_ref[: 4 * rows, :] = feed_ref[pl.ds(other * 4 * rows, 4 * rows), :]
    for tile in range(4):
        send_ref[(4 + tile) * rows : (5 + tile) * rows, :] = feed_ref[
            pl.ds(GA_UP + 2 * tile * rows + other * rows, rows), :
        ]
    for tile in range(3):
        send_ref[(8 + tile) * rows : (9 + tile) * rows, :] = mix_ref[
            pl.ds(2 * tile * rows + other * rows, rows), :
        ]
    send_ref[11 * rows : 12 * rows, :] = mix_ref[pl.ds(GB_OUT + other * rows, rows), :]


def decoder_unpack_kernel(
    place_ref, feed_ref, mix_ref, got_ref, mixing_ref, out_ref, up_ref, down_ref, proj_ref
):
    core = place_ref[0]
    rows = LANES
    units = 4 * rows
    down_ref[pl.ds(core * units, units), :] = feed_ref[pl.ds(core * units, units), :].astype(F32)
    down_ref[pl.ds((1 - core) * units, units), :] = got_ref[:units, :].astype(F32)
    for tile in range(4):
        up_ref[:, pl.ds(core * units + tile * rows, rows)] = feed_ref[
            pl.ds(GA_UP + 2 * tile * rows + core * rows, rows), :
        ].astype(F32)
        up_ref[:, pl.ds((1 - core) * units + tile * rows, rows)] = got_ref[
            (4 + tile) * rows : (5 + tile) * rows, :
        ].astype(F32)
    for tile in range(3):
        mixing_ref[tile, :, pl.ds(core * rows, rows)] = mix_ref[
            pl.ds(2 * tile * rows + core * rows, rows), :
        ].astype(F32)
        mixing_ref[tile, :, pl.ds((1 - core) * rows, rows)] = got_ref[
            (8 + tile) * rows : (9 + tile) * rows, :
        ].astype(F32)
    out_ref[pl.ds(core * rows, rows), :] = mix_ref[pl.ds(GB_OUT + core * rows, rows), :].astype(F32)
    out_ref[pl.ds((1 - core) * rows, rows), :] = got_ref[11 * rows : 12 * rows, :].astype(F32)
    proj_ref[...] = mix_ref[GB_PROJ:GB_END, :].astype(F32)


def line_first(value, size):
    if size == 4:
        return (value, lax.ppermute(value, "dp", [(0, 1), (3, 2)]))
    if size & (size - 1):
        return lax.psum(value, "dp")
    distance = 1
    while distance < size:
        got = lax.ppermute(value, "dp", [(i, i ^ distance) for i in range(size)])
        value = (value.astype(F32) + got.astype(F32)).astype(BF16)
        distance *= 2
    return value


def line_next(state, size, pairs, *others):
    if size != 4:
        return state
    mine, got = after(state, *others)
    total = (mine.astype(F32) + got.astype(F32)).astype(BF16)
    return (total, lax.ppermute(total, "dp", pairs))


def line_across(state, size, *others):
    return line_next(state, size, [(1, 2), (2, 1)], *others)


def line_back(state, size, *others):
    return line_next(state, size, [(1, 0), (2, 3)], *others)


def line_last(state, size, *others):
    if size != 4:
        return state
    mine, got = after(state, *others)
    place = lax.axis_index("dp")
    return jnp.where((place == 0) | (place == 3), got, mine)


def dp_sum(value, size):
    place = lax.axis_index("dp")
    terms = [value] + [
        lax.ppermute(value, "dp", [(i, (i + step) % size) for i in range(size)])
        for step in range(1, size)
    ]
    terms = terms[::-1]
    return jnp.sum(lax.dynamic_slice_in_dim(jnp.stack(terms + terms), size - 1 - place, size, 0), 0)


def per_device(
    data_size,
    block_input,
    span_end,
    encoder_attention_gain,
    encoder_attention_bias,
    encoder_query_key_value,
    encoder_output_weight,
    encoder_feedforward_gain,
    encoder_feedforward_bias,
    encoder_up_weight,
    encoder_down_weight,
    projection,
    decoder_attention_gain,
    decoder_attention_bias,
    decoder_query_key_value,
    decoder_output_weight,
    decoder_feedforward_gain,
    decoder_feedforward_bias,
    decoder_up_weight,
    decoder_down_weight,
    output_cotangent,
):
    row = lax.axis_index("row").astype(jnp.int32)
    y = lax.axis_index("y").astype(jnp.int32)
    core = lax.axis_index("core").astype(jnp.int32)
    length = span_end.shape[0]
    own_rows, width = block_input.shape
    block = 2 * y + core
    place = jnp.stack([core, block, row, y])
    limits = span_end.reshape(length, 1)
    limits_row = span_end.reshape(1, length)
    full = 2 * width
    low_full = 4 * LANES
    units = 2 * encoder_up_weight.shape[1]
    d_units = decoder_up_weight.shape[1]
    features = 2 * LANES

    half = own_rows // 2
    x_near = near(block_input)
    tick = jnp.zeros((8, LANES), F32)
    row_of = lambda vector: vector.reshape(-1, LANES)
    keep, send = call(
        pack_decoder_kernel,
        "pack_decoder",
        (shaped(D_SEND, LANES, BF16),) * 2,
        (
            place,
            jnp.transpose(decoder_query_key_value, (1, 0, 2)),
            decoder_output_weight,
            decoder_up_weight,
            decoder_down_weight,
            row_of(decoder_attention_gain),
            row_of(decoder_attention_bias),
            row_of(decoder_feedforward_gain),
            row_of(decoder_feedforward_bias),
            projection,
            output_cotangent,
        ),
        scalars=1,
        limit=56,
        fetch=True,
    )
    m_pack = call(
        pack_mixing_kernel,
        "pack_mixing",
        shaped(A_END + B_END, LANES, BF16),
        (
            jnp.transpose(encoder_query_key_value, (1, 2, 0)),
            encoder_output_weight,
            row_of(encoder_attention_gain),
            row_of(encoder_attention_bias),
            row_of(encoder_feedforward_gain),
            row_of(encoder_feedforward_bias),
        ),
        limit=56,
        fetch=True,
        needs=(x_near, keep),
    )
    m_near = near(m_pack)
    d_got = swap(send, "core")
    dm_pack, f_pack = call(
        join_decoder_kernel,
        "join_decoder",
        (shaped(DA_END + DB_END, LANES, BF16), shaped(2 * F_END, LANES, BF16)),
        (place, keep, d_got),
        scalars=1,
        limit=8,
    )
    e_pack = call(
        pack_encoder_kernel,
        "pack_encoder",
        shaped(2 * E_FEED, LANES, BF16),
        (encoder_up_weight, encoder_down_weight),
        limit=56,
        fetch=True,
    )
    x_far = across_both(x_near, half, e_pack, dm_pack)
    m_far = across_both(m_near, A_END, x_far)
    sides = call(
        join_input_kernel,
        "join_input",
        shaped(2 * own_rows, full, BF16),
        (place, block_input, *x_near, *x_far),
        scalars=1,
        limit=56,
        fetch=True,
        needs=(m_near,),
    )
    m_parts = (m_pack, *m_near, *m_far)
    e_near = near(after(e_pack, sides))
    dm_near = near(after(dm_pack, sides))
    mark = marker(tick, 5000, m_far)
    stream, normed_first, e_vec = call(
        first_norm_kernel,
        "first_norm",
        (shaped(length, full, BF16), shaped(length, full, BF16), shaped(4, full, F32)),
        (place, sides, swap(sides, "core"), m_pack, m_near[0]),
        scalars=1,
        limit=8,
        marks=(mark,),
    )
    mixed, e_mixing, e_out = call(
        encoder_mixing_kernel,
        "encoder_mixing",
        (
            shaped(length, 9 * LANES, BF16),
            shaped(full, 9 * LANES, BF16),
            shaped(E_ROWS, full, BF16),
        ),
        (normed_first, *m_parts),
        limit=12,
        cost=3,
    )
    attended, inverse, partial = call(
        functools.partial(attend_kernel, HD1),
        "encoder_attend",
        (
            shaped(length, E_ROWS, BF16),
            shaped(length, E_ROWS, F32),
            shaped(length, full, BF16),
        ),
        (mixed, limits, e_out),
        (pltpu.VMEM((3, length, 2 * LANES), BF16),),
        limit=16,
        cost=12,
    )
    got = swap(partial, "core")
    e_far = across_both(e_near, E_FEED, attended, dm_near)
    e_parts = (e_pack, *e_near, *e_far)
    dm_far = across_both(dm_near, DA_END, attended)
    f_go = after(f_pack, e_far)
    f_parts = (f_pack, *near(f_go), across_direct(f_go))
    mark = marker(tick, 10000, e_far)
    middle, normed_second, active, slope, partial = call(
        feed_forward_kernel,
        "feed_forward",
        (
            shaped(length, full, F32),
            shaped(length, full, BF16),
            shaped(length, units, BF16),
            shaped(length, units, BF16),
            shaped(length, full, BF16),
        ),
        (stream, partial, got, e_vec, *e_parts),
        (pltpu.VMEM((FEED, full), F32),),
        limit=16,
        cost=12,
        marks=(mark,),
    )
    mark = marker(tick, 10000, middle)
    (
        own_encoder_out, encoder_low, d_stream, d_normed_first, d_mixed, proj_weight, d_vec, d_mixing,
        d_out,
    ) = call(
        bridge_kernel,
        "bridge",
        (
            shaped(own_rows, width, F32),
            shaped(length, width, BF16),
            shaped(length, low_full, F32),
            shaped(length, low_full, BF16),
            shaped(length, 6 * LANES, BF16),
            shaped(full, low_full, BF16),
            shaped(4, low_full, F32),
            shaped(low_full, 6 * LANES, BF16),
            shaped(2 * LANES, low_full, BF16),
        ),
        (place, middle, partial, swap(partial, "core"), dm_pack, *dm_near, *dm_far),
        scalars=1,
        limit=12,
        marks=(mark,),
        cost=5.7,
    )

    d_attended, d_inverse, partial = call(
        functools.partial(attend_kernel, HD2),
        "decoder_attend",
        (
            shaped(length, 2 * LANES, BF16),
            shaped(length, 2 * LANES, F32),
            shaped(length, low_full, BF16),
        ),
        (d_mixed, limits, d_out),
        (pltpu.VMEM((2, length, 2 * LANES), BF16),),
        limit=16,
        cost=11,
    )
    mark = marker(tick, 10000, partial)
    d_middle, d_normed_second, d_active, d_hidden, partial, cotangent = call(
        decoder_feed_kernel,
        "decoder_feed",
        (
            shaped(length, low_full, F32),
            shaped(length, low_full, BF16),
            shaped(length, d_units, BF16),
            shaped(length, d_units, BF16),
            shaped(length, low_full, BF16),
            shaped(length, low_full, BF16),
        ),
        (place, d_stream, partial, swap(partial, "core"), d_vec, *f_parts),
        (pltpu.VMEM((FEED, low_full), F32),),
        scalars=1,
        limit=16,
        marks=(mark,),
        cost=8,
    )

    got = swap(partial, "core")
    grads_a = call(
        feed_grads_kernel,
        "decoder_feed_grads",
        shaped(GA_END, LANES, BF16),
        (after(d_active, partial), cotangent, d_normed_second, d_hidden),
        limit=8,
        cost=0.8,
    )
    sum_a = line_first(grads_a, data_size)
    d_middle_grad, d_middle_low, attended_grad, d_second_sums = call(
        middle_back_kernel,
        "decoder_middle_back",
        (
            shaped(length, low_full, F32),
            shaped(length, features, BF16),
            shaped(length, 2 * LANES, F32),
            shaped(2, low_full, F32),
        ),
        (place, after(partial, grads_a), got, d_middle, cotangent, d_vec, d_out),
        scalars=1,
        limit=12,
        cost=2.6,
    )
    d_lows = attention_backward(
        d_mixed, d_attended, d_inverse, attended_grad, limits_row, HD2, 0, 1
    )
    sum_a = line_across(sum_a, data_size, d_lows)
    d_lows = d_lows + attention_backward(
        d_mixed, d_attended, d_inverse, after(attended_grad, sum_a[0]), limits_row, HD2, 1, 1
    )
    sum_a = line_back(sum_a, data_size, d_lows)
    partial = call(
        mixed_back_kernel,
        "decoder_mixed_back",
        shaped(length, low_full, BF16),
        (after(d_lows[0], sum_a[0]), *d_lows[1:], d_mixing),
        limit=12,
        cost=1.6,
    )
    got = swap(partial, "core")

    proj_low, encoder_grad, down_low, d_first_sums = call(
        bridge_back_kernel,
        "bridge_back",
        (
            shaped(length, low_full, BF16),
            shaped(length, full, F32),
            shaped(length, full, BF16),
            shaped(2, low_full, F32),
        ),
        (place, partial, got, d_stream, d_middle_grad, d_vec, proj_weight),
        scalars=1,
        limit=12,
        cost=3.9,
    )
    grads_b = call(
        mixing_grads_kernel,
        "decoder_mixing_grads",
        shaped(GB_END, LANES, BF16),
        (
            place, d_normed_first, *d_lows[:3], d_attended, d_middle_low, encoder_low,
            proj_low,
        ),
        scalars=1,
        limit=8,
        cost=1.3,
    )
    sum_b = line_first(grads_b, data_size)
    grads_c = call(
        product_kernel,
        "encoder_down_grads",
        shaped(units // 2, width, BF16),
        (after(active, grads_b), down_low),
        limit=8,
        cost=1,
    )
    sum_c = line_first(grads_c, data_size)
    hidden_low, partial = call(
        feed_back_kernel,
        "feed_back",
        (shaped(length, units, BF16), shaped(length, full, BF16)),
        (after(down_low, grads_c), slope, *e_parts),
        (pltpu.VMEM((FEED, full), F32),),
        limit=16,
        cost=12,
    )
    got = swap(partial, "core")
    sum_b = line_across(sum_b, data_size, partial)
    grads_e = call(
        product_kernel,
        "encoder_up_grads",
        shaped(width, units // 2, BF16),
        (normed_second, after(hidden_low, sum_b[0])),
        limit=8,
        cost=1000,
    )
    sum_e = line_first(grads_e, data_size)
    middle_grad, middle_low, attended_grad, second_sums = call(
        middle_back_kernel,
        "encoder_middle_back",
        (
            shaped(own_rows, full, F32),
            shaped(length, width, BF16),
            shaped(length, 3 * LANES, F32),
            shaped(2, full, F32),
        ),
        (place, after(partial, grads_e), got, middle, encoder_grad, e_vec, e_out),
        scalars=1,
        limit=12,
        cost=5.5,
    )
    sum_c = line_across(sum_c, data_size, middle_low)
    first = attention_backward(
        mixed, attended, inverse, after(attended_grad, sum_c[0]), limits_row, HD1, 0, 1
    )
    sum_b = line_back(sum_b, data_size, first)
    sum_e = line_across(sum_e, data_size, first)
    second = attention_backward(
        mixed,
        attended,
        inverse,
        after(attended_grad, sum_b[0], sum_e[0], sum_a),
        limits_row,
        HD1,
        1,
        1,
    )
    grads_d = call(
        encoder_grads_kernel,
        "encoder_mixing_grads",
        shaped(G_END, LANES, BF16),
        (normed_first, *first, *second, attended, middle_low),
        limit=12,
        cost=1.1,
    )
    sum_d = line_first(grads_d, data_size)
    sum_c = line_back(sum_c, data_size, grads_d)
    sum_e = line_back(sum_e, data_size, grads_d)
    third = attention_backward(
        mixed, attended, inverse, after(attended_grad, grads_d, sum_b, sum_c[0], sum_e[0]), limits_row, HD1, 2, 1
    )
    sum_d = line_across(sum_d, data_size, third)
    lows = (*first, *second, after(third[0], sum_d[0]), *third[1:])
    keep, send = call(
        mixed_last_kernel,
        "encoder_mixed_back",
        (shaped(own_rows, full, BF16),) * 2,
        (place, *lows, e_mixing),
        scalars=1,
        limit=12,
        cost=1.8,
    )
    got = swap(send, "core")
    own_input_grad, first_sums = call(
        input_back_kernel,
        "input_back",
        (shaped(own_rows, width, F32), shaped(2, full, F32)),
        (place, after(keep, sum_c), got, stream, middle_grad, e_vec),
        scalars=1,
        limit=8,
        cost=1.8,
    )

    def in_order(value, index):
        half = value.shape[1] // 2
        return jnp.where(index == 0, value, jnp.concatenate([value[:, half:], value[:, :half]], 1))

    e_sums = in_order(jnp.concatenate([first_sums, second_sums], 0), row)
    d_sums = in_order(jnp.concatenate([d_first_sums, d_second_sums], 0), y)
    sums = jnp.concatenate([e_sums, jnp.pad(d_sums, ((0, 0), (0, full - low_full)))], 0)
    sums = jnp.sum(lax.all_gather(sums, ("row", "y", "core")), 0)
    sum_d = line_back(sum_d, data_size, sums)

    own, by_row = after(f_parts[:2], sum_d[0])
    out_rows, out_columns = output_cotangent.shape
    active_rows = lax.dynamic_slice_in_dim(d_active, row * out_rows, out_rows, 0)
    half = d_units // 2
    span = F_END + half
    down = jnp.concatenate(
        [jnp.concatenate([p[F_END:span], p[span : span + half]], 1) for p in (own, by_row)], 0
    )
    last = mm(active_rows, down)
    mine = lax.dynamic_slice_in_dim(last, core * out_columns, out_columns, 1)
    others = lax.dynamic_slice_in_dim(last, (1 - core) * out_columns, out_columns, 1)
    own_decoder_out = (
        lax.dynamic_slice(d_middle, (row * out_rows, core * out_columns), (out_rows, out_columns))
        + mine
        + swap(others.astype(BF16), "core").astype(F32)
    )

    grads_a = line_last(sum_a, data_size, own_input_grad)
    grads_b = line_last(sum_b, data_size, sum_d[0])
    send = call(
        decoder_send_kernel,
        "decoder_send",
        shaped(12 * LANES, LANES, BF16),
        (place, grads_a, grads_b),
        scalars=1,
        limit=8,
    )
    d_mixing_grad, d_out_grad, d_up_grad, d_down_grad, proj_grad = call(
        decoder_unpack_kernel,
        "decoder_unpack",
        (
            jax.ShapeDtypeStruct((3, LANES, 2 * LANES), F32),
            shaped(2 * LANES, LANES, F32),
            shaped(LANES, d_units, F32),
            shaped(d_units, LANES, F32),
            shaped(width, LANES, F32),
        ),
        (place, grads_a, grads_b, swap(send, "core")),
        scalars=1,
        limit=8,
        cost=1.9,
    )
    grads_c = line_last(sum_c, data_size, sum_d[0]).astype(F32)
    grads_e = line_last(sum_e, data_size, sum_d[0]).astype(F32)
    sums = dp_sum(after(sums, sum_d[0], d_down_grad, own_decoder_out), data_size)
    e_sums = lax.dynamic_slice_in_dim(sums[:4], row * width, width, 1)
    share = decoder_attention_gain.shape[0]
    d_sums = lax.dynamic_slice_in_dim(sums[4:], block * share, share, 1)
    grads_d = line_last(sum_d, data_size, d_down_grad, grads_c, grads_e)
    mixing_grad, out_grad = call(
        encoder_unpack_kernel,
        "encoder_unpack",
        (
            jax.ShapeDtypeStruct((3, width // 2, width), F32),
            shaped(width // 2, width, F32),
        ),
        (grads_d,),
        limit=8,
    )
    return (
        own_encoder_out,
        own_decoder_out,
        own_input_grad,
        e_sums[0],
        e_sums[1],
        jnp.transpose(mixing_grad, (2, 0, 1)),
        out_grad,
        e_sums[2],
        e_sums[3],
        grads_e,
        grads_c,
        proj_grad,
        d_sums[0],
        d_sums[1],
        jnp.transpose(d_mixing_grad, (1, 0, 2)),
        d_out_grad,
        d_sums[2],
        d_sums[3],
        d_up_grad,
        d_down_grad,
    )


def solution(mesh):
    data, row, col = (mesh.shape[name] for name in ("dp", "row", "col"))
    split = Mesh(mesh.devices.reshape(data, row, col // 2, 2), ("dp", "row", "y", "core"))
    c = ("y", "core")
    in_specs = (
        P(("dp", *c), "row"),
        P("dp"),
        P("row"),
        P("row"),
        P("row", None, c),
        P(c, "row"),
        P("row"),
        P("row"),
        P("row", c),
        P(c, "row"),
        P("row", c),
        P(c),
        P(c),
        P(c, None, "row"),
        P("row", c),
        P(c),
        P(c),
        P(c, "row"),
        P("row", c),
        P(("dp", "row"), c),
    )
    out_specs = (
        P(("dp", *c), "row"),
        P(("dp", "row"), c),
        P(("dp", *c), "row"),
        P("row"),
        P("row"),
        P("row", None, c),
        P(c, "row"),
        P("row"),
        P("row"),
        P("row", c),
        P(c, "row"),
        P("row", c),
        P(c),
        P(c),
        P(c, None, "row"),
        P("row", c),
        P(c),
        P(c),
        P(c, "row"),
        P("row", c),
    )
    return jax.shard_map(
        functools.partial(per_device, data),
        mesh=split,
        in_specs=in_specs,
        out_specs=out_specs,
        check_vma=False,
    )
```
